32 devices in a mesh: dp: 16 (over z, y, x), tensor: 2 (over core).
Axes of the slice: x: 2, y: 2, z: 4, core: 2. Of those that a mesh axis runs over, the one named last changes fastest.
Arguments:
- tokens: bfloat16 [16384, 768], P(('dp', 'tensor')), may hold values from -6 to 6
- cotangent: bfloat16 [16384, 768], P(('dp', 'tensor')), may hold values from -6 to 6
- prefix: int32 [16], P('dp'), may hold values from 0 to 1024
- query_weight: bfloat16 [768, 768], P('dp', 'tensor'), may hold values from -0.21875 to 0.21875
- key_weight: bfloat16 [768, 768], P('dp', 'tensor'), may hold values from -0.21875 to 0.21875
- value_weight: bfloat16 [768, 768], P('dp', 'tensor'), may hold values from -0.375 to 0.375
- out_weight: bfloat16 [768, 768], P('dp', 'tensor'), may hold values from -0.375 to 0.375
- up_weight: bfloat16 [768, 3072], P('dp', 'tensor'), may hold values from -0.375 to 0.375
- down_weight: bfloat16 [768, 3072], P('dp', 'tensor'), may hold values from -0.1875 to 0.1875
- model_vectors: float32 [6, 768], replicated, may hold values from -1.2 to 2, as said below
- head_vectors: float32 [4, 768], P(None, 'tensor'), may hold values from -1.2 to 2, as said below
- hidden_vectors: float32 [3, 3072], P(None, 'tensor'), may hold values from -1.2 to 2, as said below
Outputs:
- output: bfloat16 [16384, 768], P(('dp', 'tensor'))
- input_grad: float32 [16384, 768], P(('dp', 'tensor'))
- query_weight_grad: float32 [768, 768], P('dp', 'tensor')
- key_weight_grad: float32 [768, 768], P('dp', 'tensor')
- value_weight_grad: float32 [768, 768], P('dp', 'tensor')
- out_weight_grad: float32 [768, 768], P('dp', 'tensor')
- up_weight_grad: float32 [768, 3072], P('dp', 'tensor')
- down_weight_grad: float32 [768, 3072], P('dp', 'tensor')
- model_vectors_grad: float32 [6, 768], replicated
- head_vectors_grad: float32 [4, 768], P(None, 'tensor')
- hidden_vectors_grad: float32 [3, 3072], P(None, 'tensor')
The draws below stay inside these ranges and needn't reach their ends.
Inputs may be any that keep to these rules, and one draw needn't show every extreme that they name: `model_vectors`: gains and biases as in the rows named by the meaning. `head_vectors`: gains and biases as in the rows named by the meaning. `hidden_vectors`: gains and biases as in the rows named by the meaning.
All inputs are finite; a program needn't handle non-finite values.
Results may differ from the reference program's by a relative error of at most 0.014.
Values may be sent and summed in bfloat16 or wider, within the bound.
No kernel may reach another device: no remote copies, remote signals or barrier semaphores. Data moves between devices by JAX's collectives and lax.ppermute only.
A program may use at most 128 MiB of HBM per device.

```python
import jax
import jax.numpy as jnp
from jax import lax

D = 768
HEAD_DIM = 64
FF = 3072
SEQ = 1024
SEQS = 16
TOKENS = 16384


def vector_rows(key, row_count, row_width, gain_rows):
    base_draw = jnp.clip(jax.random.normal(key, (row_count, row_width), jnp.float32), -4.0, 4.0)
    gain_flags = jnp.array([1.0 if row_number in gain_rows else 0.0 for row_number in range(row_count)], jnp.float32)[:, None]
    return gain_flags * (1.0 + 0.25 * base_draw) + (1.0 - gain_flags) * (0.3 * base_draw)


def draw_model_vectors(key, part):
    return vector_rows(jax.random.fold_in(key, 11), 6, D, (0, 3))


def draw_head_vectors(key, part):
    return vector_rows(jax.random.fold_in(key, 23), 4, D, (2,))


def draw_hidden_vectors(key, part):
    return vector_rows(jax.random.fold_in(key, 37), 3, FF, (1,))


def touch_ends(drawn, stream_key, smallest, top_value):
    longest = drawn.shape.index(max(drawn.shape))
    spots = []
    for shift in (0, 1):
        where = [jax.random.randint(jax.random.fold_in(stream_key, axis), (), 0, length) for axis, length in enumerate(drawn.shape)]
        where[longest] = (where[longest] + shift) % drawn.shape[longest]
        spots.append(tuple(where))
    return drawn.at[spots[0]].set(smallest).at[spots[1]].set(top_value)


def steps_of(own_key, shape, shards, low, top_value):
    def one(axis_at, shards_of):
        steps = jax.random.uniform(jax.random.fold_in(jax.random.fold_in(own_key, 6), axis_at), (shards_of,), jnp.float32, low / len(shards), top_value / len(shards))
        return jnp.repeat(jnp.exp(steps), shape[axis_at] // shards_of).reshape((-1,) + (1,) * (len(shape) - axis_at - 1))

    factor_of = one(*shards[0])
    for cut in shards[1:]:
        factor_of = factor_of * one(*cut)
    return factor_of


def normal_values(stream_key, extent, width, most, shards=(), kind=jnp.bfloat16):
    entries = jax.random.normal(stream_key, extent, jnp.float32) * width
    if len(shards) > 0:
        entries = steps_of(stream_key, extent, shards, -0.22, 0.18) * entries
    return jnp.clip(entries, min=-most, max=most).astype(kind)


def setup_inputs(seed: int = 0) -> dict:
    streams_of = jax.random.split(jax.random.key(seed), 13)
    tokens = normal_values(streams_of[0], (TOKENS, D), 1.0, 6.0, ((0, 32),))
    cotangent = normal_values(streams_of[1], (TOKENS, D), 1.0, 6.0, ((0, 32),))
    prefix = touch_ends(jax.random.randint(streams_of[2], (SEQS,), 0, SEQ + 1), jax.random.fold_in(streams_of[2], 1), 0, SEQ).astype(jnp.int32)
    query_weight = normal_values(streams_of[3], (D, D), D ** -0.5, 0.21875, ((0, 16), (1, 2)))
    key_weight = normal_values(streams_of[4], (D, D), D ** -0.5, 0.21875, ((0, 16), (1, 2)))
    value_weight = normal_values(streams_of[5], (D, D), (D // 3) ** -0.5, 0.375, ((0, 16), (1, 2)))
    out_weight = normal_values(streams_of[6], (D, D), (D // 3) ** -0.5, 0.375, ((0, 16), (1, 2)))
    up_weight = normal_values(streams_of[7], (D, FF), (D // 3) ** -0.5, 0.375, ((0, 16), (1, 2)))
    down_weight = normal_values(streams_of[8], (D, FF), (FF // 3) ** -0.5, 0.1875, ((0, 16), (1, 2)))
    model_vectors = draw_model_vectors(jax.random.fold_in(streams_of[12], 71), 0)
    head_vectors = draw_head_vectors(jax.random.fold_in(streams_of[12], 71), 0)
    hidden_vectors = draw_hidden_vectors(jax.random.fold_in(streams_of[12], 71), 0)
    return dict(tokens=tokens, cotangent=cotangent, prefix=prefix, query_weight=query_weight, key_weight=key_weight, value_weight=value_weight, out_weight=out_weight, up_weight=up_weight, down_weight=down_weight, model_vectors=model_vectors, head_vectors=head_vectors, hidden_vectors=hidden_vectors)


epsilon = 1e-05
masked = -1e+30

@jax.custom_vjp
def low(v):
    return lax.optimization_barrier(v.astype(jnp.bfloat16)).astype(jnp.float32)

@jax.custom_vjp
def low_back(v):
    return v

def low_keep(v):
    return (low(v), None)

def low_pass(kept, grad):
    return (grad,)

def back_keep(v):
    return (v, None)

def back_low(kept, grad):
    return (low(grad),)
low.defvjp(low_keep, low_pass)
low_back.defvjp(back_keep, back_low)

def coarse(values):
    return low(low_back(values))

def highest(left_side, right_side):
    return jnp.dot(left_side, right_side, precision=lax.Precision.HIGHEST, preferred_element_type=jnp.float32)

def layer_norm(values, gain_row, offset):
    center = lax.optimization_barrier(jnp.mean(values, axis=-1, keepdims=True))
    spread = lax.optimization_barrier(jnp.mean(values * values, axis=-1, keepdims=True)) - center * center
    return (values - center) * lax.rsqrt(spread + epsilon) * gain_row + offset

def attend(queries, key_states, value_states, prefix_len):
    length = queries.shape[0]
    head_count = queries.shape[1] // HEAD_DIM
    query_split = queries.reshape(length, head_count, HEAD_DIM)
    key_split = key_states.reshape(length, head_count, HEAD_DIM)
    value_split = value_states.reshape(length, head_count, HEAD_DIM)
    block_rows = min(512, length)
    columns = jnp.arange(length, dtype=jnp.int32)

    def one_block(block_index):
        first_row = block_index * block_rows
        query_rows = lax.dynamic_slice_in_dim(query_split, first_row, block_rows, 0)
        scores = jnp.einsum('qhd,khd->hqk', query_rows, key_split, precision=lax.Precision.HIGHEST) * 0.125
        scores = low_back(scores)
        places = first_row + jnp.arange(block_rows, dtype=jnp.int32)
        allowed = (columns[None, :] <= places[:, None]) | (columns[None, :] < prefix_len)
        scores = jnp.where(allowed[None], scores, masked)
        row_max = lax.optimization_barrier(jnp.max(scores, axis=-1, keepdims=True))
        raised = jnp.exp(scores - row_max)
        softmax_out = raised / lax.optimization_barrier(jnp.sum(raised, axis=-1, keepdims=True))
        return jnp.einsum('hqk,khd->qhd', low(softmax_out), value_split, precision=lax.Precision.HIGHEST)
    blocks = lax.map(jax.checkpoint(one_block), jnp.arange(length // block_rows, dtype=jnp.int32))
    return blocks.reshape(length, head_count * HEAD_DIM)

def layer(inputs, prefix_len, query_weight, key_weight, value_weight, out_weight, up_weight, down_weight, model_vectors, head_vectors, hidden_vectors):
    attend_in = low(layer_norm(inputs, model_vectors[0], model_vectors[1]))
    queries = coarse(highest(attend_in, query_weight) + head_vectors[0])
    key_states = coarse(highest(attend_in, key_weight))
    value_states = coarse(highest(attend_in, value_weight) + head_vectors[1])
    attended = low_back(attend(queries, key_states, value_states, prefix_len))
    mixed_in = low(layer_norm(attended, head_vectors[2], head_vectors[3]))
    middle = inputs + low_back(highest(mixed_in, out_weight.T) + model_vectors[2])
    feed_in = low(layer_norm(middle, model_vectors[3], model_vectors[4]))
    before = low_back(highest(feed_in, up_weight) + hidden_vectors[0])
    hidden = jax.nn.gelu(before, approximate=False)
    feed_mid = low(layer_norm(hidden, hidden_vectors[1], hidden_vectors[2]))
    return middle + low_back(highest(feed_mid, down_weight.T) + model_vectors[5])

def reference(tokens, cotangent, prefix, query_weight, key_weight, value_weight, out_weight, up_weight, down_weight, model_vectors, head_vectors, hidden_vectors):
    float_params = tuple((matrix.astype(jnp.float32) for matrix in (query_weight, key_weight, value_weight, out_weight, up_weight, down_weight, model_vectors, head_vectors, hidden_vectors)))
    inputs = tokens.astype(jnp.float32).reshape(SEQS, SEQ, D)
    grads_in = cotangent.astype(jnp.float32).reshape(SEQS, SEQ, D)

    def per_sequence(running, sequence_item):
        sequence_in, sequence_grad, prefix_len = sequence_item

        def forward(layer_in, *weights):
            return layer(layer_in, prefix_len, *weights)
        sequence_out, pullback = jax.vjp(forward, sequence_in, *float_params)
        gradients = pullback(sequence_grad)
        running = tuple((earlier + latest for earlier, latest in zip(running, gradients[1:])))
        return (running, (sequence_out, gradients[0]))
    initial = tuple((jnp.zeros(matrix.shape, jnp.float32) for matrix in float_params))
    totals, (outputs, input_grads) = lax.scan(per_sequence, initial, (inputs, grads_in, prefix))
    return (outputs.reshape(TOKENS, D).astype(jnp.bfloat16), input_grads.reshape(TOKENS, D), totals[0], totals[1], totals[2], totals[3], totals[4], totals[5], totals[6], totals[7], totals[8])
```

```python
from functools import partial

import jax
import jax.numpy as jnp
from jax import lax
from jax.experimental import pallas as pl
from jax.experimental.pallas import tpu as pltpu
from jax.sharding import PartitionSpec as P

HEAD_DIM = 64


epsilon = 1e-05
masked = -1e30


def flip_partner(values):
    return lax.ppermute(values, "tensor", [(0, 1), (1, 0)])


def whole_sequence(values):
    other = flip_partner(values)
    first = lax.axis_index("tensor") == 0
    return jnp.where(
        first, jnp.concatenate([values, other], 0), jnp.concatenate([other, values], 0)
    )


def share_of_sum(values):
    halves = values.reshape(2, values.shape[0] // 2, values.shape[1])
    core = lax.axis_index("tensor")
    mine = lax.dynamic_index_in_dim(halves, core, 0, keepdims=False)
    theirs = lax.dynamic_index_in_dim(halves, 1 - core, 0, keepdims=False)
    return mine + flip_partner(theirs.astype(jnp.bfloat16)).astype(jnp.float32)


def feature_totals(left_terms, right_terms):
    totals = jnp.stack([jnp.sum(left_terms, axis=-1), jnp.sum(right_terms, axis=-1)])
    totals = totals + flip_partner(totals)
    return totals[0], totals[1]


class Ring:
    def __init__(self, size):
        self.size = size
        rest, stride = size // 4, 4
        self.lines = []
        while rest > 1:
            factor = 4 if rest % 4 == 0 else 2 if rest % 2 == 0 else rest
            self.lines.append((factor, stride))
            rest, stride = rest // factor, stride * factor
        self.line_count = size // 4

    def shift(self, values, factor, stride, step):
        pairs = []
        for place in range(self.size):
            digit = place // stride % factor
            pairs.append((place, place + ((digit + step) % factor - digit) * stride))
        return lax.ppermute(values, "dp", pairs)

    def flip(self, values, stride):
        return self.shift(values, 2, stride, 1)

    def line_places(self, sign):
        own = lax.axis_index("dp")
        places = [jnp.int32(0)]
        for factor, stride in self.lines:
            digit = own // stride % factor
            places = [
                base + (digit + sign * step) % factor * stride
                for base in places
                for step in range(factor)
            ]
        return places

    def gather_order(self):
        own = lax.axis_index("dp")
        places = self.line_places_gather()
        return jnp.stack([base + (own % 4 ^ bits) for bits in (0, 1, 2, 3) for base in places])

    def line_places_gather(self):
        own = lax.axis_index("dp")
        places = [jnp.int32(0)]
        for factor, stride in self.lines:
            digit = own // stride % factor
            places = [
                base + (digit + factor - step) % factor * stride
                for step in range(factor)
                for base in places
            ]
        return places

    def gather(self, values):
        block = values
        for factor, stride in self.lines:
            block = jnp.concatenate(
                [block] + [self.shift(block, factor, stride, step) for step in range(1, factor)], 0
            )
        from_x, from_y = self.flip(block, 1), self.flip(block, 2)
        half = block.shape[0] // 2
        corner = (self.flip(from_x[:half], 2), self.flip(from_y[half:], 1))
        return (block, from_x, from_y) + corner

    def scatter_order(self, first_bit):
        own = lax.axis_index("dp")
        other_bit = 3 - first_bit
        places = self.line_places(1)
        return jnp.stack(
            [
                base + (own % 4 ^ (cross + side))
                for cross in (0, first_bit)
                for side in (0, other_bit)
                for base in places
            ]
        )

    def square_sum(self, keep, send, first_bit):
        f32 = jnp.float32
        half = keep.shape[0] // 2
        got = self.flip(send, first_bit)
        away = (keep[half:].astype(f32) + got[half:].astype(f32)).astype(jnp.bfloat16)
        second = self.flip(away, 3 - first_bit)
        return keep[:half].astype(f32) + got[:half].astype(f32) + second.astype(f32)

    def scatter(self, pair_one, pair_two):
        total = jnp.concatenate(
            [self.square_sum(*pair_one, 1), self.square_sum(*pair_two, 2)], axis=1
        )
        for factor, stride in self.lines:
            rows = total.shape[0] // factor
            rounded = total.astype(jnp.bfloat16)
            running = total[:rows]
            for step in range(1, factor):
                got = self.shift(rounded[step * rows : (step + 1) * rows], factor, stride, step)
                running = running + got.astype(jnp.float32)
            total = running
        return total

    def all_sum(self, values):
        stride = 1
        while stride < self.size:
            values = values + self.flip(values, stride)
            stride *= 2
        return values


def assemble(order, pieces, widths):
    rows = pieces[0].shape[0]
    count = order.shape[0]
    shard = rows // (count // 4)

    def body(order_ref, own, from_x, from_y, corner_a, corner_b, *outs):
        blocks = [(own, 0), (from_x, 0), (from_y, 0)]
        for block in range(count):
            kind, inner = divmod(block, count // 4)
            start = inner * shard
            if kind < 3:
                ref = blocks[kind][0]
            elif start < rows // 2:
                ref = corner_a
            else:
                ref, start = corner_b, start - rows // 2
            place = pl.multiple_of(order_ref[block] * shard, 16)
            left = 0
            for out, width in zip(outs, widths):
                out[pl.ds(place, shard), :] = ref[start : start + shard, left : left + width]
                left += width

    return pl.pallas_call(
        body,
        out_shape=[jax.ShapeDtypeStruct((count * shard, width), jnp.bfloat16) for width in widths],
        in_specs=[pl.BlockSpec(memory_space=pltpu.SMEM)]
        + [pl.BlockSpec(memory_space=pltpu.VMEM)] * 5,
        out_specs=[pl.BlockSpec(memory_space=pltpu.VMEM)] * len(widths),
    )(order, *pieces)


def weight_grad(order, left_side, right_side):
    tokens, features = left_side.shape
    width = right_side.shape[1]
    count = order.shape[0]
    shard = features // count
    tile = 384

    def body(order_ref, left, right, keep, send, turned, total):
        @pl.when(pl.program_id(0) == 0)
        def _():
            turned[...] = left[...].T

        total[...] = jnp.dot(turned[...], right[...], preferred_element_type=jnp.float32)
        for block in range(count):
            place = pl.multiple_of(order_ref[block] * shard, 16)
            out, at = (keep, block) if block < count // 2 else (send, block - count // 2)
            out[at * shard : (at + 1) * shard, :] = total[pl.ds(place, shard), :].astype(
                jnp.bfloat16
            )

    return pl.pallas_call(
        body,
        grid=(width // tile,),
        out_shape=[jax.ShapeDtypeStruct((features // 2, width), jnp.bfloat16)] * 2,
        in_specs=[
            pl.BlockSpec(memory_space=pltpu.SMEM),
            pl.BlockSpec((tokens, features), lambda i: (0, 0)),
            pl.BlockSpec((tokens, tile), lambda i: (0, i)),
        ],
        out_specs=[pl.BlockSpec((features // 2, tile), lambda i: (0, i))] * 2,
        scratch_shapes=[
            pltpu.VMEM((features, tokens), jnp.bfloat16),
            pltpu.VMEM((features, tile), jnp.float32),
        ],
        cost_estimate=pl.CostEstimate(
            flops=2 * tokens * features * width,
            bytes_accessed=2 * (tokens * features + tokens * width + features * width),
            transcendentals=0,
        ),
    )(order, left_side, right_side)


def matmul(left_side, right_side):
    return jnp.dot(left_side, right_side, preferred_element_type=jnp.float32)


def matmul_transposed(left_side, right_side):
    return lax.dot_general(
        left_side, right_side, (((1,), (1,)), ((), ())), preferred_element_type=jnp.float32
    )


def local_stats(values):
    center = jnp.mean(values, axis=-1, keepdims=True)
    spread = jnp.mean(values * values, axis=-1, keepdims=True) - center * center
    inverse = lax.rsqrt(spread + epsilon)
    return ((values - center) * inverse, inverse)


def split_stats(values):
    full_width = values.shape[-1] * lax.axis_size("tensor")
    row_total, squares = feature_totals(values, values * values)
    center = (row_total / full_width)[:, None]
    inverse = lax.rsqrt((squares / full_width)[:, None] - center * center + epsilon)
    return ((values - center) * inverse, inverse)


def local_back(grad_out, normal, inverse, gain_row):
    scaled = grad_out * gain_row
    return inverse * (
        scaled
        - jnp.mean(scaled, axis=-1, keepdims=True)
        - normal * jnp.mean(scaled * normal, axis=-1, keepdims=True)
    )


def split_back(grad_out, normal, inverse, gain_row):
    full_width = grad_out.shape[-1] * lax.axis_size("tensor")
    scaled = grad_out * gain_row
    row_total, crossed = feature_totals(scaled, scaled * normal)
    return inverse * (
        scaled - (row_total / full_width)[:, None] - normal * (crossed / full_width)[:, None]
    )


def on_device(
    tokens,
    cotangent,
    prefix,
    query_weight,
    key_weight,
    value_weight,
    out_weight,
    up_weight,
    down_weight,
    model_vectors,
    head_vectors,
    hidden_vectors,
):
    ring = Ring(lax.axis_size("dp"))
    order = ring.gather_order()
    near, far = ring.scatter_order(1), ring.scatter_order(2)
    half, full = query_weight.shape[1], up_weight.shape[1]
    query_full, key_full, value_full = assemble(
        order,
        ring.gather(jnp.concatenate([query_weight, key_weight, value_weight], 1)),
        (half, half, half),
    )
    out_full, up_full = assemble(
        order, ring.gather(jnp.concatenate([out_weight, up_weight], 1)), (half, full)
    )
    (down_full,) = assemble(order, ring.gather(down_weight), (full,))
    inputs = tokens.astype(jnp.float32)
    prefix_len = prefix[0]
    normal_one, inverse_one = local_stats(inputs)
    attend_in = whole_sequence(
        (normal_one * model_vectors[0] + model_vectors[1]).astype(jnp.bfloat16)
    )
    query_states = (matmul(attend_in, query_full) + head_vectors[0]).astype(jnp.bfloat16)
    key_states = matmul(attend_in, key_full).astype(jnp.bfloat16)
    value_states = (matmul(attend_in, value_full) + head_vectors[1]).astype(jnp.bfloat16)
    length = attend_in.shape[0]
    head_count = query_states.shape[1] // HEAD_DIM
    block_rows = min(512, length)
    block_count = length // block_rows
    key_split = key_states.reshape(length, head_count, HEAD_DIM)
    value_split = value_states.reshape(length, head_count, HEAD_DIM)
    columns = jnp.arange(length, dtype=jnp.int32)

    def allowed(first_row):
        places = first_row + jnp.arange(block_rows, dtype=jnp.int32)
        return (columns[None, :] <= places[:, None]) | (columns[None, :] < prefix_len)

    def block_scores(first_row):
        query_rows = lax.dynamic_slice_in_dim(query_states, first_row, block_rows, 0).reshape(
            block_rows, head_count, HEAD_DIM
        )
        scores = (
            jnp.einsum("qhd,khd->hqk", query_rows, key_split, preferred_element_type=jnp.float32)
            * 0.125
        )
        return (query_rows, jnp.where(allowed(first_row)[None], scores, masked))

    def forward_block(block_index):
        query_rows, scores = block_scores(block_index * block_rows)
        row_max = jnp.max(scores, axis=-1, keepdims=True)
        raised = jnp.exp(scores - row_max)
        totals = jnp.sum(raised, axis=-1, keepdims=True)
        softmax_out = (raised / totals).astype(jnp.bfloat16)
        attended_rows = jnp.einsum(
            "hqk,khd->qhd", softmax_out, value_split, preferred_element_type=jnp.float32
        )
        return (
            attended_rows.reshape(block_rows, head_count * HEAD_DIM),
            (row_max + jnp.log(totals))[..., 0],
        )

    attended_blocks, log_totals = lax.map(forward_block, jnp.arange(block_count, dtype=jnp.int32))
    attended = attended_blocks.reshape(length, head_count * HEAD_DIM)
    normal_two, inverse_two = split_stats(attended)
    mixed_in = (normal_two * head_vectors[2] + head_vectors[3]).astype(jnp.bfloat16)
    middle = inputs + share_of_sum(matmul_transposed(mixed_in, out_full)) + model_vectors[2]
    normal_three, inverse_three = local_stats(middle)
    feed_in = whole_sequence(
        (normal_three * model_vectors[3] + model_vectors[4]).astype(jnp.bfloat16)
    )
    before = matmul(feed_in, up_full) + hidden_vectors[0]
    hidden, gelu_pull = jax.vjp(partial(jax.nn.gelu, approximate=False), before)
    normal_four, inverse_four = split_stats(hidden)
    feed_mid = (normal_four * hidden_vectors[1] + hidden_vectors[2]).astype(jnp.bfloat16)
    result = middle + share_of_sum(matmul_transposed(feed_mid, down_full)) + model_vectors[5]
    output = result.astype(jnp.bfloat16)
    grad_out = cotangent.astype(jnp.float32)
    grad_full = whole_sequence(cotangent)
    down_pair = weight_grad(far, grad_full, feed_mid)
    mid_grad = matmul(grad_full, down_full)
    feed_gain_grad = jnp.sum(mid_grad * normal_four, axis=0)
    feed_offset_grad = jnp.sum(mid_grad, axis=0)
    hidden_grad = split_back(mid_grad, normal_four, inverse_four, hidden_vectors[1])
    before_grad = gelu_pull(hidden_grad)[0].astype(jnp.bfloat16)
    up_bias_grad = jnp.sum(before_grad, axis=0, dtype=jnp.float32)
    up_pair = weight_grad(near, feed_in, before_grad)
    wide_grads = ring.scatter(up_pair, down_pair)
    up_grad, down_grad = wide_grads[:, :full], wide_grads[:, full:]
    feed_in_grad = share_of_sum(matmul_transposed(before_grad, up_full))
    second_gain_grad = jnp.sum(feed_in_grad * normal_three, axis=0)
    second_offset_grad = jnp.sum(feed_in_grad, axis=0)
    middle_grad = grad_out + local_back(feed_in_grad, normal_three, inverse_three, model_vectors[3])
    down_bias_grad = jnp.sum(grad_out, axis=0)
    branch_grad = middle_grad.astype(jnp.bfloat16)
    out_bias_grad = jnp.sum(branch_grad, axis=0, dtype=jnp.float32)
    branch_full = whole_sequence(branch_grad)
    out_pair = weight_grad(far, branch_full, mixed_in)
    mixed_grad = matmul(branch_full, out_full)
    attend_gain_grad = jnp.sum(mixed_grad * normal_two, axis=0)
    attend_offset_grad = jnp.sum(mixed_grad, axis=0)
    attended_grad = split_back(mixed_grad, normal_two, inverse_two, head_vectors[2]).astype(
        jnp.bfloat16
    )

    def backward_block(running, block_item):
        key_total, value_total = running
        block_index, log_rows = block_item
        first_row = block_index * block_rows
        query_rows, scores = block_scores(first_row)
        grad_rows = lax.dynamic_slice_in_dim(attended_grad, first_row, block_rows, 0).reshape(
            block_rows, head_count, HEAD_DIM
        )
        softmax_out = jnp.exp(scores - log_rows[..., None])
        prob_grad = jnp.einsum(
            "qhd,khd->hqk", grad_rows, value_split, preferred_element_type=jnp.float32
        )
        score_grad = (
            softmax_out * (prob_grad - jnp.sum(softmax_out * prob_grad, axis=-1, keepdims=True))
        ).astype(jnp.bfloat16)
        query_block = (
            jnp.einsum("hqk,khd->qhd", score_grad, key_split, preferred_element_type=jnp.float32)
            * 0.125
        ).astype(jnp.bfloat16)
        key_total = (
            key_total
            + jnp.einsum("hqk,qhd->khd", score_grad, query_rows, preferred_element_type=jnp.float32)
            * 0.125
        )
        value_total = value_total + jnp.einsum(
            "hqk,qhd->khd",
            softmax_out.astype(jnp.bfloat16),
            grad_rows,
            preferred_element_type=jnp.float32,
        )
        return ((key_total, value_total), query_block.reshape(block_rows, head_count * HEAD_DIM))

    empty_grad = jnp.zeros((length, head_count, HEAD_DIM), jnp.float32)
    (key_total, value_total), query_blocks = lax.scan(
        backward_block,
        (empty_grad, empty_grad),
        (jnp.arange(block_count, dtype=jnp.int32), log_totals),
    )
    query_grad = query_blocks.reshape(length, head_count * HEAD_DIM)
    key_grad = key_total.reshape(length, head_count * HEAD_DIM).astype(jnp.bfloat16)
    value_grad = value_total.reshape(length, head_count * HEAD_DIM).astype(jnp.bfloat16)
    query_bias_grad = jnp.sum(query_grad, axis=0, dtype=jnp.float32)
    value_bias_grad = jnp.sum(value_grad, axis=0, dtype=jnp.float32)
    query_pair = weight_grad(near, attend_in, jnp.concatenate([query_grad, value_grad], 1))
    key_pair = weight_grad(far, attend_in, key_grad)
    second_pair = [jnp.concatenate(both, 1) for both in zip(key_pair, out_pair)]
    narrow = ring.scatter(query_pair, second_pair)
    query_weight_grad, value_weight_grad, key_weight_grad, out_grad = (
        narrow[:, i * half : (i + 1) * half] for i in range(4)
    )
    attend_in_grad = share_of_sum(
        matmul_transposed(query_grad, query_full)
        + matmul_transposed(key_grad, key_full)
        + matmul_transposed(value_grad, value_full)
    )
    first_gain_grad = jnp.sum(attend_in_grad * normal_one, axis=0)
    first_offset_grad = jnp.sum(attend_in_grad, axis=0)
    input_grad = middle_grad + local_back(attend_in_grad, normal_one, inverse_one, model_vectors[0])
    model_grads = jnp.stack(
        [
            first_gain_grad,
            first_offset_grad,
            out_bias_grad,
            second_gain_grad,
            second_offset_grad,
            down_bias_grad,
        ]
    )
    head_grads = jnp.stack([query_bias_grad, value_bias_grad, attend_gain_grad, attend_offset_grad])
    hidden_grads = jnp.stack([up_bias_grad, feed_gain_grad, feed_offset_grad])
    model_grads = model_grads + flip_partner(model_grads)
    sums = ring.all_sum(
        jnp.concatenate([g.reshape(-1, 128) for g in (model_grads, head_grads, hidden_grads)], 0)
    )
    rows_one, rows_two = model_grads.size // 128, head_grads.size // 128
    model_sum = sums[:rows_one].reshape(model_grads.shape)
    head_sum = sums[rows_one : rows_one + rows_two].reshape(head_grads.shape)
    hidden_sum = sums[rows_one + rows_two :].reshape(hidden_grads.shape)
    return (
        output,
        input_grad,
        query_weight_grad,
        key_weight_grad,
        value_weight_grad,
        out_grad,
        up_grad,
        down_grad,
        model_sum,
        head_sum,
        hidden_sum,
    )


def solution(mesh):
    return jax.shard_map(
        on_device,
        mesh=mesh,
        in_specs=(
            P(("dp", "tensor"), None),
            P(("dp", "tensor"), None),
            P("dp"),
            P("dp", "tensor"),
            P("dp", "tensor"),
            P("dp", "tensor"),
            P("dp", "tensor"),
            P("dp", "tensor"),
            P("dp", "tensor"),
            P(),
            P(None, "tensor"),
            P(None, "tensor"),
        ),
        out_specs=(
            P(("dp", "tensor"), None),
            P(("dp", "tensor"), None),
            P("dp", "tensor"),
            P("dp", "tensor"),
            P("dp", "tensor"),
            P("dp", "tensor"),
            P("dp", "tensor"),
            P("dp", "tensor"),
            P(),
            P(None, "tensor"),
            P(None, "tensor"),
        ),
        check_vma=False,
    )
```

```python
import jax
import jax.numpy as jnp
from jax import lax
from jax.experimental import pallas as pl
from jax.experimental.pallas import tpu as pltpu
from jax.sharding import PartitionSpec as P

HEAD_DIM = 64
PAIR = 2 * HEAD_DIM
LANES = 128
TILES = 4
SCALE = 0.125
LOG2E = 1.4426950408889634
WEIGHT = 4

epsilon = 1e-05
masked = -1e30

f32 = jnp.float32
bf16 = jnp.bfloat16
TRANSPOSED = (((1,), (1,)), ((), ()))
SMEM = pl.BlockSpec(memory_space=pltpu.SMEM)


def flip_partner(values):
    return lax.ppermute(values, "tensor", [(0, 1), (1, 0)])


def normal_of(values):
    center = jnp.mean(values, axis=-1, keepdims=True)
    spread = jnp.mean(values * values, axis=-1, keepdims=True) - center * center
    inverse = lax.rsqrt(spread + epsilon)
    return (values - center) * inverse, inverse


def normal_back(scaled, normal, inverse):
    return inverse * (
        scaled
        - jnp.mean(scaled, axis=-1, keepdims=True)
        - normal * jnp.mean(scaled * normal, axis=-1, keepdims=True)
    )


def widen(values):
    return values.astype(f32)


def after(values, *earlier):
    return lax.optimization_barrier((values, earlier))[0]


class Ring:
    def __init__(self, size):
        self.size = size
        rest, stride = size // 4, 4
        self.lines = []
        while rest > 1:
            factor = 4 if rest % 4 == 0 else 2 if rest % 2 == 0 else rest
            self.lines.append((factor, stride))
            rest, stride = rest // factor, stride * factor
        self.line_count = size // 4

    def shift(self, values, factor, stride, step):
        pairs = []
        for place in range(self.size):
            digit = place // stride % factor
            pairs.append((place, place + ((digit + step) % factor - digit) * stride))
        return lax.ppermute(values, "dp", pairs)

    def flip(self, values, stride):
        return self.shift(values, 2, stride, 1)

    def line_places(self, sign):
        own = lax.axis_index("dp")
        places = [jnp.int32(0)]
        for factor, stride in self.lines:
            digit = own // stride % factor
            places = [
                base + (digit + sign * step) % factor * stride
                for base in places
                for step in range(factor)
            ]
        return places

    def gather_order(self):
        own = lax.axis_index("dp")
        places = self.line_places_gather()
        return jnp.stack([base + (own % 4 ^ bits) for bits in (0, 1, 2, 3) for base in places])

    def line_places_gather(self):
        own = lax.axis_index("dp")
        places = [jnp.int32(0)]
        for factor, stride in self.lines:
            digit = own // stride % factor
            places = [
                base + (digit + factor - step) % factor * stride
                for step in range(factor)
                for base in places
            ]
        return places

    def along_lines(self, values):
        block = values
        for factor, stride in self.lines:
            block = jnp.concatenate(
                [block] + [self.shift(block, factor, stride, step) for step in range(1, factor)], 0
            )
        return block

    def to_sides(self, block):
        return self.flip(block, 1), self.flip(block, 2)

    def to_corner(self, from_x, from_y):
        half = from_x.shape[0] // 2
        return self.flip(from_x[:half], 2), self.flip(from_y[half:], 1)

    def scatter_order(self, first_bit):
        own = lax.axis_index("dp")
        other_bit = 3 - first_bit
        places = self.line_places(1)
        return jnp.stack(
            [
                base + (own % 4 ^ (cross + side))
                for cross in (0, first_bit)
                for side in (0, other_bit)
                for base in places
            ]
        )

    def sum_first(self, keep, got):
        half = keep.shape[0] // 2
        own = widen(keep[:half]) + widen(got[:half])
        return own, (widen(keep[half:]) + widen(got[half:])).astype(bf16)

    def sum_lines(self, total):
        for factor, stride in self.lines:
            rows = total.shape[0] // factor
            rounded = total.astype(bf16)
            running = total[:rows]
            for step in range(1, factor):
                got = self.shift(rounded[step * rows : (step + 1) * rows], factor, stride, step)
                running = running + widen(got)
            total = running
        return total

    def all_sum(self, values):
        stride = 1
        while stride < self.size:
            values = values + self.flip(values, stride)
            stride *= 2
        return values


def whole(shape):
    return pl.BlockSpec(shape, lambda i: (0,) * len(shape))


def rows_of(array, tiles=TILES):
    return pl.BlockSpec((array.shape[0] // tiles, array.shape[1]), lambda i: (i, 0))


def shape_of(shape, dtype):
    return jax.ShapeDtypeStruct(shape, dtype)


def cost(flops, moved, exponentials=0):
    return pl.CostEstimate(flops=WEIGHT * flops, bytes_accessed=moved, transcendentals=exponentials)


PARAMS = pltpu.CompilerParams(vmem_limit_bytes=60 * 2**20)


def place_rows(order_ref, pieces, outs, count):
    own, from_x, from_y, corner_a, corner_b = pieces
    rows = own.shape[0]
    shard = rows // (count // 4)
    for block in range(count):
        kind, inner = divmod(block, count // 4)
        start = inner * shard
        ref = (own, from_x, from_y, corner_a)[kind]
        if kind == 3 and start >= rows // 2:
            ref, start = corner_b, start - rows // 2
        place = pl.multiple_of(order_ref[block] * shard, 16)
        left = 0
        for out in outs:
            width = out.shape[1]
            out[pl.ds(place, shard), :] = ref[start : start + shard, left : left + width]
            left += width


def split_three(value):
    high = value.astype(bf16)
    rest = value - widen(high)
    middle = rest.astype(bf16)
    return high, middle, (rest - widen(middle)).astype(bf16)


def two_parts(row):
    high = row.astype(bf16)
    return high, (row - widen(high)).astype(bf16)


def pack_stats(center, spread):
    lane = lax.broadcasted_iota(jnp.int32, (1, LANES), 1)
    packed = jnp.zeros((center.shape[0], LANES), f32)
    for at, part in enumerate(split_three(center) + split_three(spread)):
        packed = jnp.where(lane == at, widen(part), packed)
    return packed.astype(bf16)


def unpack_stats(packed):
    lane = lax.broadcasted_iota(jnp.int32, (1, LANES), 1)
    values = widen(packed)
    center = jnp.sum(jnp.where(lane < 3, values, 0.0), axis=-1, keepdims=True)
    spread = jnp.sum(jnp.where((lane >= 3) & (lane < 6), values, 0.0), axis=-1, keepdims=True)
    return center, spread


def joined_product(one, two, side_one, side_two, features):
    center_one, spread_one = unpack_stats(one[:, features:])
    center_two, spread_two = unpack_stats(two[:, features:])
    center = 0.5 * (center_one + center_two)
    apart = 0.5 * (center_one - center_two)
    inverse = lax.rsqrt(0.5 * (spread_one + spread_two) + apart * apart + epsilon)
    product = inverse * (
        widen(one[:, :features])
        + widen(two[:, :features])
        + apart * (side_one[0:1, :] - side_two[0:1, :])
    )
    return center, inverse, product


def centered_product(values, gain, weight):
    center = jnp.mean(values, axis=-1, keepdims=True)
    away = values - center
    spread = jnp.mean(away * away, axis=-1, keepdims=True)
    product = lax.dot_general(
        (away * gain).astype(bf16), weight, TRANSPOSED, preferred_element_type=f32
    )
    return product.astype(bf16), pack_stats(center, spread)


def side_rows(gain, offset, weight):
    gain_high, gain_low = two_parts(gain)
    offset_high, offset_low = two_parts(offset)
    filler = jnp.zeros((4, gain.shape[1]), bf16)
    stacked = jnp.concatenate([gain_high, gain_low, offset_high, offset_low, filler], 0)
    rows = lax.dot_general(stacked, weight, TRANSPOSED, preferred_element_type=f32)
    return jnp.concatenate(
        [rows[0:1] + rows[1:2], rows[2:3] + rows[3:4], jnp.zeros((6, rows.shape[1]), f32)], 0
    )


def accumulate(ref, row, values):
    total = jnp.sum(values, axis=0, keepdims=True)
    first = pl.program_id(0) == 0
    ref[row : row + 1, :] = jnp.where(first, total, ref[row : row + 1, :] + total)


def prepare(core, tokens, tokens_other, cotangent, cotangent_other, model_vectors):
    rows, features = tokens.shape
    share = TILES // 2
    tile = rows // share

    def body(
        core_ref, x_own, x_other, g_own, g_other, model, inputs, grads, normal, turned, g_turned, sums
    ):
        here = pl.program_id(0) // share == core_ref[0]
        x = jnp.where(here, x_own[...], x_other[...])
        g = jnp.where(here, g_own[...], g_other[...])
        inputs[...] = x
        grads[...] = g
        n, _ = normal_of(widen(x))
        a = (n * model[0:1, :] + model[1:2, :]).astype(bf16)
        normal[...] = a
        turned[...] = a.T
        g_turned[...] = g.T
        accumulate(sums, 0, widen(g))

    own = pl.BlockSpec(
        (tile, features), lambda i, core: (jnp.clip(i - core[0] * share, 0, share - 1), 0)
    )
    other = pl.BlockSpec(
        (tile, features), lambda i, core: (jnp.clip(i - (1 - core[0]) * share, 0, share - 1), 0)
    )
    straight = pl.BlockSpec((tile, features), lambda i, core: (i, 0))
    across = pl.BlockSpec((features, tile), lambda i, core: (0, i))
    return pl.pallas_call(
        body,
        grid_spec=pltpu.PrefetchScalarGridSpec(
            num_scalar_prefetch=1,
            grid=(TILES,),
            in_specs=[own, other, own, other]
            + [pl.BlockSpec(model_vectors.shape, lambda i, core: (0, 0))],
            out_specs=[straight] * 3
            + [across] * 2
            + [pl.BlockSpec((8, features), lambda i, core: (0, 0))],
        ),
        out_shape=[shape_of((2 * rows, features), bf16)] * 3
        + [shape_of((features, 2 * rows), bf16)] * 2
        + [shape_of((8, features), f32)],
        compiler_params=PARAMS,
        cost_estimate=cost(20 * rows * features, 28 * rows * features),
        name="prepare",
    )(core, tokens, tokens_other, cotangent, cotangent_other, model_vectors)


def join(*parts):
    rows, width = parts[0].shape[0], sum(part.shape[1] for part in parts)

    def body(*refs):
        left = 0
        for ref in refs[:-1]:
            refs[-1][:, left : left + ref.shape[1]] = ref[...]
            left += ref.shape[1]

    return pl.pallas_call(
        body,
        out_shape=shape_of((rows, width), parts[0].dtype),
        in_specs=[pl.BlockSpec(memory_space=pltpu.VMEM)] * len(parts),
        out_specs=pl.BlockSpec(memory_space=pltpu.VMEM),
        name="join",
    )(*parts)


def project(order, pieces, attend_in, bias):
    length, features = attend_in.shape
    width = bias.shape[1]
    third = width // 3
    count = order.shape[0]

    def body(order_ref, *refs):
        pieces_in, (rows, bias_row, weight, *outs) = refs[:5], refs[5:]

        @pl.when(pl.program_id(0) == 0)
        def _():
            place_rows(order_ref, pieces_in, (weight,), count)

        states = jnp.dot(rows[...], weight[...], preferred_element_type=f32) + bias_row[...]
        for at, out in enumerate(outs):
            out[...] = states[:, at * third : (at + 1) * third].astype(bf16)

    return pl.pallas_call(
        body,
        grid=(TILES,),
        out_shape=[shape_of((features, width), bf16)] + [shape_of((length, third), bf16)] * 3,
        in_specs=[SMEM]
        + [whole(piece.shape) for piece in pieces]
        + [rows_of(attend_in), whole(bias.shape)],
        out_specs=[whole((features, width))]
        + [pl.BlockSpec((length // TILES, third), lambda i: (i, 0))] * 3,
        compiler_params=PARAMS,
        cost_estimate=cost(
            2 * length * features * width, 4 * features * width + 2 * length * (features + width)
        ),
        name="project",
    )(order, *pieces, attend_in, bias)


def attend_forward(prefix, queries, keys, values):
    length, width = queries.shape
    pairs = width // PAIR
    tile = length // 2

    def body(prefix_ref, query_ref, key_ref, value_ref, out_ref, log_ref, turned):
        turned[...] = value_ref[...].T
        first_half = lax.broadcasted_iota(jnp.int32, (1, PAIR), 1) < HEAD_DIM
        key_rows = key_ref[...]
        row_at = lax.broadcasted_iota(jnp.int32, (length, 1), 0)
        for start in range(0, length, tile):
            columns = slice(start, start + tile)
            places = lax.broadcasted_iota(jnp.int32, (1, tile), 1) + (start + 1)
            limit = jnp.maximum(places, prefix_ref[0])
            query_rows = query_ref[columns, :]
            parts = []
            for head in (0, 1):
                mine = jnp.where(
                    first_half == (head == 0), query_rows, jnp.zeros_like(query_rows)
                )
                scores = lax.dot_general(key_rows, mine, TRANSPOSED, preferred_element_type=f32)
                scores = jnp.where(row_at < limit, scores, masked)
                top = jnp.max(scores, axis=0, keepdims=True)
                raised = jnp.exp2((scores - top) * (SCALE * LOG2E))
                total = jnp.sum(raised, axis=0, keepdims=True)
                mixed = jnp.dot(
                    turned[head * HEAD_DIM : (head + 1) * HEAD_DIM, :],
                    raised.astype(bf16),
                    preferred_element_type=f32,
                )
                parts.append(mixed / total)
                log_ref[0, head : head + 1, columns] = top * (SCALE * LOG2E) + jnp.log2(total)
            out_ref[columns, :] = jnp.concatenate(parts, 0).T

    block = pl.BlockSpec((length, PAIR), lambda i: (0, i))
    return pl.pallas_call(
        body,
        grid=(pairs,),
        out_shape=[shape_of((length, width), f32), shape_of((pairs, 8, length), f32)],
        in_specs=[SMEM, block, block, block],
        out_specs=[block, pl.BlockSpec((1, 8, length), lambda i: (i, 0, 0))],
        scratch_shapes=[pltpu.VMEM((PAIR, length), bf16)],
        compiler_params=PARAMS,
        cost_estimate=cost(
            16 * length * length * width, 10 * length * width, 2 * pairs * length * length
        ),
        name="attend_forward",
    )(prefix, queries, keys, values)


def attend_backward(prefix, queries, keys, values, attended, grads, logs):
    length, width = queries.shape
    pairs = width // PAIR
    tile = length // 4

    def body(
        prefix_ref,
        query_ref,
        key_ref,
        value_ref,
        attended_ref,
        grad_ref,
        log_ref,
        query_out,
        key_out,
        value_out,
        turned,
        key_total,
        value_total,
    ):
        turned[...] = key_ref[...].T
        first_half = lax.broadcasted_iota(jnp.int32, (1, PAIR), 1) < HEAD_DIM
        key_rows, value_rows = key_ref[...], value_ref[...]
        row_at = lax.broadcasted_iota(jnp.int32, (length, 1), 0)
        for start in range(0, length, tile):
            columns = slice(start, start + tile)
            places = lax.broadcasted_iota(jnp.int32, (1, tile), 1) + (start + 1)
            limit = jnp.maximum(places, prefix_ref[0])
            query_rows, grad_rows = query_ref[columns, :], grad_ref[columns, :]
            crossed = (attended_ref[columns, :] * widen(grad_rows)).T
            parts = []
            key_part = value_part = 0.0
            for head in (0, 1):
                side = first_half == (head == 0)
                span = slice(head * HEAD_DIM, (head + 1) * HEAD_DIM)
                mine = jnp.where(side, query_rows, jnp.zeros_like(query_rows))
                grad = jnp.where(side, grad_rows, jnp.zeros_like(grad_rows))
                level = jnp.sum(crossed[span, :], axis=0, keepdims=True)
                scores = lax.dot_general(key_rows, mine, TRANSPOSED, preferred_element_type=f32)
                raised = jnp.exp2(
                    scores * (SCALE * LOG2E) - log_ref[0, head : head + 1, columns]
                )
                probs = jnp.where(row_at < limit, raised, 0.0)
                prob_grad = lax.dot_general(
                    value_rows, grad, TRANSPOSED, preferred_element_type=f32
                )
                score_grad = (probs * (prob_grad - level)).astype(bf16)
                value_part += jnp.dot(probs.astype(bf16), grad, preferred_element_type=f32)
                key_part += jnp.dot(score_grad, mine, preferred_element_type=f32)
                parts.append(jnp.dot(turned[span, :], score_grad, preferred_element_type=f32))
            query_out[columns, :] = (jnp.concatenate(parts, 0).T * SCALE).astype(bf16)
            if start == 0:
                key_total[...] = key_part
                value_total[...] = value_part
            else:
                key_total[...] += key_part
                value_total[...] += value_part
        key_out[...] = (key_total[...] * SCALE).astype(bf16)
        value_out[...] = value_total[...].astype(bf16)

    block = pl.BlockSpec((length, PAIR), lambda i: (0, i))
    return pl.pallas_call(
        body,
        grid=(pairs,),
        out_shape=[shape_of((length, width), bf16)] * 3,
        in_specs=[SMEM] + [block] * 5 + [pl.BlockSpec((1, 8, length), lambda i: (i, 0, 0))],
        out_specs=[block] * 3,
        scratch_shapes=[
            pltpu.VMEM((PAIR, length), bf16),
            pltpu.VMEM((length, PAIR), f32),
            pltpu.VMEM((length, PAIR), f32),
        ],
        compiler_params=PARAMS,
        cost_estimate=cost(
            40 * length * length * width, 18 * length * width, 2 * pairs * length * length
        ),
        name="attend_backward",
    )(prefix, queries, keys, values, attended, grads, logs)


def mix(order, pieces, attended, head_vectors, widths):
    length, width = attended.shape
    count = order.shape[0]
    features = pieces[0].shape[0] // (count // 4) * count

    def body(order_ref, *refs):
        pieces_in, (rows, vectors, weight, second, product, side) = refs[:5], refs[5:]

        @pl.when(pl.program_id(0) == 0)
        def _():
            place_rows(order_ref, pieces_in, (weight, second), count)
            side[...] = side_rows(vectors[2:3, :], vectors[3:4, :], weight[...])

        out, stats = centered_product(rows[...], vectors[2:3, :], weight[...])
        product[:, :features] = out
        product[:, features:] = stats

    return pl.pallas_call(
        body,
        grid=(TILES,),
        out_shape=[shape_of((features, each), bf16) for each in widths]
        + [shape_of((length, features + LANES), bf16), shape_of((8, features), f32)],
        in_specs=[SMEM]
        + [whole(piece.shape) for piece in pieces]
        + [rows_of(attended), whole(head_vectors.shape)],
        out_specs=[whole((features, each)) for each in widths]
        + [
            pl.BlockSpec((length // TILES, features + LANES), lambda i: (i, 0)),
            whole((8, features)),
        ],
        compiler_params=PARAMS,
        cost_estimate=cost(
            2 * length * features * width, 4 * features * sum(widths) + 6 * length * features
        ),
        name="mix",
    )(order, *pieces, attended, head_vectors)


def feed_up(product, product_other, side, side_other, inputs, weight, model_vectors, hidden_vectors):
    length, features = inputs.shape
    width = weight.shape[1]

    def body(one, two, side_one, side_two, x, weight_ref, model, hidden, middle, turned, kept, slope):
        _, _, branch = joined_product(one[...], two[...], side_one, side_two, features)
        offset = side_one[1:2, :] + side_two[1:2, :] + model[2:3, :]
        total = widen(x[...]) + (branch + offset)
        middle[...] = total
        normal, _ = normal_of(total)
        feed = (normal * model[3:4, :] + model[4:5, :]).astype(bf16)
        turned[...] = feed.T
        before = jnp.dot(feed, weight_ref[...], preferred_element_type=f32) + hidden[0:1, :]
        share = 0.5 + 0.5 * lax.erf(before * 0.7071067811865476)
        kept[...] = (before * share).astype(bf16)
        slope[...] = (
            share + before * (0.3989422804014327 * jnp.exp(-0.5 * before * before))
        ).astype(bf16)

    return pl.pallas_call(
        body,
        grid=(TILES,),
        out_shape=[
            shape_of((length, features), f32),
            shape_of((features, length), bf16),
            shape_of((length, width), bf16),
            shape_of((length, width), bf16),
        ],
        in_specs=[
            rows_of(product),
            rows_of(product),
            whole(side.shape),
            whole(side.shape),
            rows_of(inputs),
            whole(weight.shape),
            whole(model_vectors.shape),
            whole(hidden_vectors.shape),
        ],
        out_specs=[
            rows_of(inputs),
            pl.BlockSpec((features, length // TILES), lambda i: (0, i)),
            pl.BlockSpec((length // TILES, width), lambda i: (i, 0)),
            pl.BlockSpec((length // TILES, width), lambda i: (i, 0)),
        ],
        compiler_params=PARAMS,
        cost_estimate=cost(
            2 * length * features * width,
            2 * features * width + 12 * length * features + 4 * length * width,
            2 * length * width,
        ),
        name="feed_up",
    )(product, product_other, side, side_other, inputs, weight, model_vectors, hidden_vectors)


def feed_down(order, pieces, kept, hidden_vectors):
    length, width = kept.shape
    count = order.shape[0]
    features = pieces[0].shape[0] // (count // 4) * count

    def body(order_ref, *refs):
        pieces_in, (rows, vectors, weight, product, side) = refs[:5], refs[5:]

        @pl.when(pl.program_id(0) == 0)
        def _():
            place_rows(order_ref, pieces_in, (weight,), count)
            side[...] = side_rows(vectors[1:2, :], vectors[2:3, :], weight[...])

        out, stats = centered_product(widen(rows[...]), vectors[1:2, :], weight[...])
        product[:, :features] = out
        product[:, features:] = stats

    return pl.pallas_call(
        body,
        grid=(TILES,),
        out_shape=[
            shape_of((features, width), bf16),
            shape_of((length, features + LANES), bf16),
            shape_of((8, features), f32),
        ],
        in_specs=[SMEM]
        + [whole(piece.shape) for piece in pieces]
        + [rows_of(kept), whole(hidden_vectors.shape)],
        out_specs=[
            whole((features, width)),
            pl.BlockSpec((length // TILES, features + LANES), lambda i: (i, 0)),
            whole((8, features)),
        ],
        compiler_params=PARAMS,
        cost_estimate=cost(
            2 * length * features * width, 4 * features * width + 2 * length * (features + width)
        ),
        name="feed_down",
    )(order, *pieces, kept, hidden_vectors)


def feed_back(
    core,
    product,
    product_other,
    side,
    side_other,
    middle,
    cotangent,
    kept,
    slope,
    down,
    up,
    model_vectors,
    hidden_vectors,
):
    length, features = middle.shape
    width = kept.shape[1]
    joined = 2 * width
    share = TILES // 2

    def body(
        core_ref, one, two, side_one, side_two, mid, grad, kept_ref, slope_ref, down_ref, up_ref,
        model, hidden, output, norm_out, before_out, product_out, sums,
    ):
        center, inverse, branch = joined_product(one[...], two[...], side_one, side_two, features)
        offset = side_one[1:2, :] + side_two[1:2, :] + model[5:6, :]

        @pl.when(pl.program_id(0) // share == core_ref[0])
        def _():
            output[...] = (mid[...] + (branch + offset)).astype(bf16)

        rows = widen(grad[...])
        straight = side_one[0:1, :] + side_two[0:1, :]
        mean_scaled = jnp.sum(rows * straight, axis=-1, keepdims=True) / joined
        mean_crossed = jnp.sum(rows * branch, axis=-1, keepdims=True) / joined
        mid_grad = jnp.dot(grad[...], down_ref[...], preferred_element_type=f32)
        normal = (widen(kept_ref[...]) - center) * inverse
        norm_out[...] = (normal * hidden[1:2, :] + hidden[2:3, :]).astype(bf16)
        accumulate(sums, 1, mid_grad * normal)
        accumulate(sums, 2, mid_grad)
        hidden_grad = inverse * (
            mid_grad * hidden[1:2, :] - mean_scaled - normal * mean_crossed
        )
        before = (hidden_grad * widen(slope_ref[...])).astype(bf16)
        before_out[...] = before
        accumulate(sums, 0, widen(before))
        product_out[...] = lax.dot_general(
            before, up_ref[...], TRANSPOSED, preferred_element_type=f32
        ).astype(bf16)

    tile = length // TILES

    def at_rows(columns):
        return pl.BlockSpec((tile, columns), lambda i, core: (i, 0))

    def fixed(array):
        return pl.BlockSpec(array.shape, lambda i, core: (0, 0))

    return pl.pallas_call(
        body,
        grid_spec=pltpu.PrefetchScalarGridSpec(
            num_scalar_prefetch=1,
            grid=(TILES,),
            in_specs=[
                at_rows(features + LANES),
                at_rows(features + LANES),
                fixed(side),
                fixed(side),
                at_rows(features),
                at_rows(features),
                at_rows(width),
                at_rows(width),
                fixed(down),
                fixed(up),
                fixed(model_vectors),
                fixed(hidden_vectors),
            ],
            out_specs=[
                pl.BlockSpec(
                    (tile, features), lambda i, core: (jnp.clip(i - core[0] * share, 0, share - 1), 0)
                ),
                at_rows(width),
                at_rows(width),
                at_rows(features),
                pl.BlockSpec((8, width), lambda i, core: (0, 0)),
            ],
        ),
        out_shape=[
            shape_of((length // 2, features), bf16),
            shape_of((length, width), bf16),
            shape_of((length, width), bf16),
            shape_of((length, features), bf16),
            shape_of((8, width), f32),
        ],
        compiler_params=PARAMS,
        cost_estimate=cost(
            4 * length * features * width,
            4 * features * width + 12 * length * features + 8 * length * width,
        ),
        name="feed_back",
    )(
        core,
        product,
        product_other,
        side,
        side_other,
        middle,
        cotangent,
        kept,
        slope,
        down,
        up,
        model_vectors,
        hidden_vectors,
    )


def mix_back(
    passed,
    passed_other,
    product,
    product_other,
    side,
    side_other,
    middle,
    cotangent,
    attended,
    weight,
    model_vectors,
    head_vectors,
):
    length, features = middle.shape
    width = attended.shape[1]
    joined = 2 * width

    def body(
        back_one, back_two, one, two, side_one, side_two, mid, grad, attended_ref, weight_ref,
        model, head, middle_out, turned, mixed_out, attended_out, sums, head_sums,
    ):
        feed_grad = widen(back_one[...]) + widen(back_two[...])
        normal, inverse = normal_of(mid[...])
        accumulate(sums, 1, feed_grad * normal)
        accumulate(sums, 2, feed_grad)
        middle_grad = widen(grad[...]) + normal_back(feed_grad * model[3:4, :], normal, inverse)
        middle_out[...] = middle_grad
        branch_grad = middle_grad.astype(bf16)
        rows = widen(branch_grad)
        accumulate(sums, 0, rows)
        turned[...] = branch_grad.T
        center, inverse_two, branch = joined_product(
            one[...], two[...], side_one, side_two, features
        )
        straight = side_one[0:1, :] + side_two[0:1, :]
        mean_scaled = jnp.sum(rows * straight, axis=-1, keepdims=True) / joined
        mean_crossed = jnp.sum(rows * branch, axis=-1, keepdims=True) / joined
        mixed_grad = jnp.dot(branch_grad, weight_ref[...], preferred_element_type=f32)
        normal_two = (attended_ref[...] - center) * inverse_two
        mixed_out[...] = (normal_two * head[2:3, :] + head[3:4, :]).astype(bf16)
        accumulate(head_sums, 0, mixed_grad * normal_two)
        accumulate(head_sums, 1, mixed_grad)
        attended_out[...] = (
            inverse_two * (mixed_grad * head[2:3, :] - mean_scaled - normal_two * mean_crossed)
        ).astype(bf16)

    tile = length // TILES
    return pl.pallas_call(
        body,
        grid=(TILES,),
        out_shape=[
            shape_of((length, features), f32),
            shape_of((features, length), bf16),
            shape_of((length, width), bf16),
            shape_of((length, width), bf16),
            shape_of((8, features), f32),
            shape_of((8, width), f32),
        ],
        in_specs=[
            rows_of(passed),
            rows_of(passed),
            rows_of(product),
            rows_of(product),
            whole(side.shape),
            whole(side.shape),
            rows_of(middle),
            rows_of(cotangent),
            rows_of(attended),
            whole(weight.shape),
            whole(model_vectors.shape),
            whole(head_vectors.shape),
        ],
        out_specs=[
            rows_of(middle),
            pl.BlockSpec((features, tile), lambda i: (0, i)),
            rows_of(attended),
            rows_of(attended),
            whole((8, features)),
            whole((8, width)),
        ],
        compiler_params=PARAMS,
        cost_estimate=cost(
            2 * length * features * width, 2 * features * width + 24 * length * features
        ),
        name="mix_back",
    )(
        passed,
        passed_other,
        product,
        product_other,
        side,
        side_other,
        middle,
        cotangent,
        attended,
        weight,
        model_vectors,
        head_vectors,
    )


def project_back(core, parts, weight):
    length, third = parts[0].shape
    features = weight.shape[0]
    tile = length // TILES
    share = TILES // 2

    def body(core_ref, one, two, three, weight_ref, send, keep, sums):
        total = jnp.zeros((tile, features), f32)
        for at, part in enumerate((one, two, three)):
            total += lax.dot_general(
                part[...],
                weight_ref[:, at * third : (at + 1) * third],
                TRANSPOSED,
                preferred_element_type=f32,
            )
        accumulate(sums, 0, widen(one[...]))
        accumulate(sums, 1, widen(three[...]))

        @pl.when(pl.program_id(0) < share)
        def _():
            send[...] = total.astype(bf16)

        @pl.when(pl.program_id(0) >= share)
        def _():
            keep[...] = total

    moved = pl.BlockSpec((tile, third), lambda i, core: ((i + (1 - core[0]) * share) % TILES, 0))
    return pl.pallas_call(
        body,
        grid_spec=pltpu.PrefetchScalarGridSpec(
            num_scalar_prefetch=1,
            grid=(TILES,),
            in_specs=[moved, moved, moved, pl.BlockSpec(weight.shape, lambda i, core: (0, 0))],
            out_specs=[
                pl.BlockSpec((tile, features), lambda i, core: (jnp.minimum(i, share - 1), 0)),
                pl.BlockSpec((tile, features), lambda i, core: (jnp.maximum(i - share, 0), 0)),
                pl.BlockSpec((8, third), lambda i, core: (0, 0)),
            ],
        ),
        out_shape=[
            shape_of((length // 2, features), bf16),
            shape_of((length // 2, features), f32),
            shape_of((8, third), f32),
        ],
        compiler_params=PARAMS,
        cost_estimate=cost(
            6 * length * features * third, 6 * features * third + 6 * length * (features + third)
        ),
        name="project_back",
    )(core, *parts, weight)


def input_back(core, received, kept, middle_grad, tokens, model_vectors):
    rows, features = tokens.shape
    tiles = TILES // 2
    tile = rows // tiles

    def body(core_ref, got, own, mid, x, model, out, sums):
        grad = widen(got[...]) + own[...]
        normal, inverse = normal_of(widen(x[...]))
        accumulate(sums, 0, grad * normal)
        accumulate(sums, 1, grad)
        out[...] = mid[...] + normal_back(grad * model[0:1, :], normal, inverse)

    near = pl.BlockSpec((tile, features), lambda i, core: (i, 0))
    return pl.pallas_call(
        body,
        grid_spec=pltpu.PrefetchScalarGridSpec(
            num_scalar_prefetch=1,
            grid=(tiles,),
            in_specs=[
                near,
                near,
                pl.BlockSpec((tile, features), lambda i, core: (i + core[0] * tiles, 0)),
                near,
                pl.BlockSpec(model_vectors.shape, lambda i, core: (0, 0)),
            ],
            out_specs=[near, pl.BlockSpec((8, features), lambda i, core: (0, 0))],
        ),
        out_shape=[shape_of((rows, features), f32), shape_of((8, features), f32)],
        compiler_params=PARAMS,
        cost_estimate=cost(10 * rows * features, 16 * rows * features),
        name="input_back",
    )(core, received, kept, middle_grad, tokens, model_vectors)


def weight_grad(order, pairs, tile):
    features, tokens = pairs[0][0].shape
    width = sum(right.shape[1] for _, right in pairs)
    count = order.shape[0]
    shard = features // count
    lefts = []
    steps = []
    for left, right in pairs:
        if not any(left is known for known in lefts):
            lefts.append(left)
        at = [left is known for known in lefts].index(True)
        steps += [(at, len(steps), 0)] if right.shape[1] == tile else []
    rights = [right for _, right in pairs]
    single = len(pairs) == 1

    def body(order_ref, *refs):
        left_refs, right_refs = refs[: len(lefts)], refs[len(lefts) : -3]
        keep, send, total = refs[-3:]
        if single:
            total[...] = jnp.dot(left_refs[0][...], right_refs[0][...], preferred_element_type=f32)
        else:
            for at, step, _ in steps:

                @pl.when(pl.program_id(0) == step)
                def _(at=at, step=step):
                    total[...] = jnp.dot(
                        left_refs[at][...], right_refs[step][...], preferred_element_type=f32
                    )

        for block in range(count):
            place = pl.multiple_of(order_ref[block] * shard, 16)
            out, at = (keep, block) if block < count // 2 else (send, block - count // 2)
            out[at * shard : (at + 1) * shard, :] = total[pl.ds(place, shard), :].astype(bf16)

    return pl.pallas_call(
        body,
        grid=(width // tile,),
        out_shape=[shape_of((features // 2, width), bf16)] * 2,
        in_specs=[SMEM]
        + [whole(left.shape) for left in lefts]
        + (
            [pl.BlockSpec((tokens, tile), lambda i: (0, i))]
            if single
            else [whole(right.shape) for right in rights]
        ),
        out_specs=[pl.BlockSpec((features // 2, tile), lambda i: (0, i))] * 2,
        scratch_shapes=[pltpu.VMEM((features, tile), f32)],
        compiler_params=PARAMS,
        cost_estimate=cost(
            2 * tokens * features * width,
            2 * (tokens * (features + width) + features * width),
        ),
        name="weight_grad",
    )(order, *lefts, *rights)


def on_device(
    tokens,
    cotangent,
    prefix,
    query_weight,
    key_weight,
    value_weight,
    out_weight,
    up_weight,
    down_weight,
    model_vectors,
    head_vectors,
    hidden_vectors,
):
    ring = Ring(lax.axis_size("dp"))
    order = ring.gather_order()
    near, far = ring.scatter_order(1), ring.scatter_order(2)
    core = lax.axis_index("tensor").astype(jnp.int32)[None]
    half, full = query_weight.shape[1], up_weight.shape[1]
    features = tokens.shape[1]

    bias = jnp.concatenate([head_vectors[0], jnp.zeros_like(head_vectors[0]), head_vectors[1]])
    first_block = ring.along_lines(join(query_weight, key_weight, value_weight))
    second_block = ring.along_lines(after(join(out_weight, up_weight), first_block))
    third_block = ring.along_lines(after(down_weight, second_block))
    first_sides = ring.to_sides(first_block)
    first_pieces = (first_block, *first_sides, *ring.to_corner(*first_sides))

    inputs, grads, attend_in, attend_turned, grads_turned, grad_sums = prepare(
        core, tokens, flip_partner(tokens), cotangent, flip_partner(cotangent), model_vectors
    )

    second_block = after(second_block, first_pieces)
    second_sides = ring.to_sides(second_block)
    first_weight, queries, keys, values = project(order, first_pieces, attend_in, bias[None])
    attended, logs = attend_forward(prefix, queries, keys, values)
    second_pieces = (second_block, *second_sides, *ring.to_corner(*second_sides))
    third_block = after(third_block, second_sides)
    third_sides = ring.to_sides(third_block)
    out_full, up_full, mixed, mixed_side = mix(
        order, second_pieces, attended, head_vectors, (half, full)
    )
    mixed_other, mixed_side_other = flip_partner(mixed), flip_partner(mixed_side)
    middle, feed_turned, kept, slope = feed_up(
        after(mixed, third_sides),
        mixed_other,
        mixed_side,
        mixed_side_other,
        inputs,
        up_full,
        model_vectors,
        hidden_vectors,
    )
    third_pieces = (third_block, *third_sides, *ring.to_corner(*third_sides))
    down_full, fed, fed_side = feed_down(order, third_pieces, kept, hidden_vectors)
    fed_other, fed_side_other = flip_partner(fed), flip_partner(fed_side)
    output, feed_mid, before_grad, passed, hidden_sums = feed_back(
        core,
        fed,
        fed_other,
        fed_side,
        fed_side_other,
        middle,
        grads,
        kept,
        slope,
        down_full,
        up_full,
        model_vectors,
        hidden_vectors,
    )
    passed_other = flip_partner(passed)
    down_keep, down_send = weight_grad(far, [(grads_turned, feed_mid)], full // 2)
    up_keep, up_send = weight_grad(near, [(feed_turned, before_grad)], full // 2)
    down_got, up_got = ring.flip(down_send, 2), ring.flip(up_send, 1)

    middle_grad, branch_turned, mixed_in, attended_grad, model_sums, head_sums = mix_back(
        passed,
        passed_other,
        mixed,
        mixed_other,
        mixed_side,
        mixed_side_other,
        middle,
        grads,
        attended,
        out_full,
        model_vectors,
        head_vectors,
    )
    query_grad, key_grad, value_grad = attend_backward(
        prefix, queries, keys, values, attended, attended_grad, logs
    )
    down_own, down_away = ring.sum_first(down_keep, after(down_got, query_grad))
    up_own, up_away = ring.sum_first(up_keep, after(up_got, query_grad))
    down_second, up_second = ring.flip(down_away, 1), ring.flip(up_away, 2)
    parts = after((query_grad, key_grad, value_grad), down_away, up_away)
    send, keep, bias_sums = project_back(core, parts, first_weight)
    received = flip_partner(send)
    query_keep, query_send = weight_grad(
        near, [(attend_turned, query_grad), (attend_turned, after(value_grad, send))], half
    )
    wide = jnp.concatenate(
        [up_own + widen(up_second), down_own + widen(down_second)], axis=1
    )
    wide_grads = ring.sum_lines(after(wide, query_send))
    up_grad, down_grad = wide_grads[:, :full], wide_grads[:, full:]
    key_keep, key_send = weight_grad(
        far, [(attend_turned, after(key_grad, wide)), (branch_turned, mixed_in)], half
    )
    query_own, query_away = ring.sum_first(query_keep, ring.flip(query_send, 1))
    key_own, key_away = ring.sum_first(key_keep, ring.flip(key_send, 2))
    narrow = jnp.concatenate(
        [
            query_own + widen(ring.flip(query_away, 2)),
            key_own + widen(ring.flip(key_away, 1)),
        ],
        axis=1,
    )
    narrow = ring.sum_lines(narrow)
    query_weight_grad, value_weight_grad, key_weight_grad, out_grad = (
        narrow[:, at * half : (at + 1) * half] for at in range(4)
    )
    input_grad, first_sums = input_back(core, received, keep, middle_grad, tokens, model_vectors)
    first_sums = first_sums + flip_partner(first_sums)

    model_grads = jnp.concatenate([first_sums[:2], model_sums[:3], grad_sums[:1]], 0)
    head_grads = jnp.concatenate([bias_sums[:2], head_sums[:2]], 0)
    hidden_grads = hidden_sums[:3]
    sums = ring.all_sum(
        jnp.concatenate([g.reshape(-1, LANES) for g in (model_grads, head_grads, hidden_grads)], 0)
    )
    rows_one, rows_two = model_grads.size // LANES, head_grads.size // LANES
    model_sum = sums[:rows_one].reshape(model_grads.shape)
    head_sum = sums[rows_one : rows_one + rows_two].reshape(head_grads.shape)
    hidden_sum = sums[rows_one + rows_two :].reshape(hidden_grads.shape)
    return (
        output,
        input_grad,
        query_weight_grad,
        key_weight_grad,
        value_weight_grad,
        out_grad,
        up_grad,
        down_grad,
        model_sum,
        head_sum,
        hidden_sum,
    )


def solution(mesh):
    return jax.shard_map(
        on_device,
        mesh=mesh,
        in_specs=(
            P(("dp", "tensor"), None),
            P(("dp", "tensor"), None),
            P("dp"),
            P("dp", "tensor"),
            P("dp", "tensor"),
            P("dp", "tensor"),
            P("dp", "tensor"),
            P("dp", "tensor"),
            P("dp", "tensor"),
            P(),
            P(None, "tensor"),
            P(None, "tensor"),
        ),
        out_specs=(
            P(("dp", "tensor"), None),
            P(("dp", "tensor"), None),
            P("dp", "tensor"),
            P("dp", "tensor"),
            P("dp", "tensor"),
            P("dp", "tensor"),
            P("dp", "tensor"),
            P("dp", "tensor"),
            P(),
            P(None, "tensor"),
            P(None, "tensor"),
        ),
        check_vma=False,
    )
```

```python
import jax
import jax.numpy as jnp
from jax import lax
from jax.experimental import pallas as pl
from jax.experimental.pallas import tpu as pltpu
from jax.sharding import PartitionSpec as P

HEAD_DIM = 64
PAIR = 2 * HEAD_DIM
LANES = 128
TILES = 4
SCALE = 0.125
LOG2E = 1.4426950408889634
WEIGHT = 4

epsilon = 1e-05
masked = -1e30

f32 = jnp.float32
bf16 = jnp.bfloat16
TRANSPOSED = (((1,), (1,)), ((), ()))
SMEM = pl.BlockSpec(memory_space=pltpu.SMEM)


def flip_partner(values):
    return lax.ppermute(values, "tensor", [(0, 1), (1, 0)])


def normal_of(values):
    center = jnp.mean(values, axis=-1, keepdims=True)
    spread = jnp.mean(values * values, axis=-1, keepdims=True) - center * center
    inverse = lax.rsqrt(spread + epsilon)
    return (values - center) * inverse, inverse


def normal_back(scaled, normal, inverse):
    return inverse * (
        scaled
        - jnp.mean(scaled, axis=-1, keepdims=True)
        - normal * jnp.mean(scaled * normal, axis=-1, keepdims=True)
    )


def widen(values):
    return values.astype(f32)


def after(values, *earlier):
    return lax.optimization_barrier((values, earlier))[0]


class Ring:
    def __init__(self, size):
        self.size = size
        rest, stride = size // 4, 4
        self.lines = []
        while rest > 1:
            factor = 4 if rest % 4 == 0 else 2 if rest % 2 == 0 else rest
            self.lines.append((factor, stride))
            rest, stride = rest // factor, stride * factor
        self.line_count = size // 4

    def shift(self, values, factor, stride, step):
        pairs = []
        for place in range(self.size):
            digit = place // stride % factor
            pairs.append((place, place + ((digit + step) % factor - digit) * stride))
        return lax.ppermute(values, "dp", pairs)

    def flip(self, values, stride):
        return self.shift(values, 2, stride, 1)

    def line_places(self, sign):
        own = lax.axis_index("dp")
        places = [jnp.int32(0)]
        for factor, stride in self.lines:
            digit = own // stride % factor
            places = [
                base + (digit + sign * step) % factor * stride
                for base in places
                for step in range(factor)
            ]
        return places

    def gather_order(self):
        own = lax.axis_index("dp")
        places = self.line_places_gather()
        return jnp.stack([base + (own % 4 ^ bits) for bits in (0, 1, 2, 3) for base in places])

    def line_places_gather(self):
        own = lax.axis_index("dp")
        places = [jnp.int32(0)]
        for factor, stride in self.lines:
            digit = own // stride % factor
            places = [
                base + (digit + factor - step) % factor * stride
                for step in range(factor)
                for base in places
            ]
        return places

    def along_lines(self, values, meanwhile=lambda got: got):
        block = values
        for factor, stride in self.lines:
            got = [self.shift(block, factor, stride, step) for step in range(1, factor)]
            block = jnp.concatenate([block] + meanwhile(got), 0)
        return block

    def to_sides(self, block):
        return self.flip(block, 1), self.flip(block, 2)

    def to_corner(self, from_x, from_y):
        half = from_x.shape[0] // 2
        return self.flip(from_x[:half], 2), self.flip(from_y[half:], 1)

    def scatter_order(self, first_bit):
        own = lax.axis_index("dp")
        other_bit = 3 - first_bit
        places = self.line_places(1)
        return jnp.stack(
            [
                base + (own % 4 ^ (cross + side))
                for cross in (0, first_bit)
                for side in (0, other_bit)
                for base in places
            ]
        )

    def sum_first(self, keep, got):
        half = keep.shape[0] // 2
        own = widen(keep[:half]) + widen(got[:half])
        return own, (widen(keep[half:]) + widen(got[half:])).astype(bf16)

    def sum_lines(self, own, seconds, meanwhile):
        parts = square_end(own, seconds, self.lines[0][0])
        for at, (factor, stride) in enumerate(self.lines):
            got = [self.shift(parts[step], factor, stride, step) for step in range(1, factor)]
            total = parts[0]
            for piece in meanwhile(got, parts):
                total = total + widen(piece)
            if at + 1 < len(self.lines):
                pieces = jnp.split(total, self.lines[at + 1][0])
                parts = [pieces[0]] + [piece.astype(bf16) for piece in pieces[1:]]
        return total

    def sum_strides(self):
        stride, strides = 1, []
        while stride < self.size:
            strides.append(stride)
            stride *= 2
        return strides


def whole(shape):
    return pl.BlockSpec(shape, lambda i: (0,) * len(shape))


def rows_of(array, tiles=TILES):
    return pl.BlockSpec((array.shape[0] // tiles, array.shape[1]), lambda i: (i, 0))


def shape_of(shape, dtype):
    return jax.ShapeDtypeStruct(shape, dtype)


def cost(flops, moved, exponentials=0):
    return pl.CostEstimate(flops=WEIGHT * flops, bytes_accessed=moved, transcendentals=exponentials)


PARAMS = pltpu.CompilerParams(vmem_limit_bytes=60 * 2**20)


def place_rows(order_ref, pieces, outs, count):
    own, from_x, from_y, corner_a, corner_b = pieces
    rows = own.shape[0]
    shard = rows // (count // 4)
    for block in range(count):
        kind, inner = divmod(block, count // 4)
        start = inner * shard
        ref = (own, from_x, from_y, corner_a)[kind]
        if kind == 3 and start >= rows // 2:
            ref, start = corner_b, start - rows // 2
        place = pl.multiple_of(order_ref[block] * shard, 16)
        left = 0
        for out in outs:
            width = out.shape[1]
            out[pl.ds(place, shard), :] = ref[start : start + shard, left : left + width]
            left += width


def split_three(value):
    high = value.astype(bf16)
    rest = value - widen(high)
    middle = rest.astype(bf16)
    return high, middle, (rest - widen(middle)).astype(bf16)


def two_parts(row):
    high = row.astype(bf16)
    return high, (row - widen(high)).astype(bf16)


def pack_stats(center, spread):
    lane = lax.broadcasted_iota(jnp.int32, (1, LANES), 1)
    packed = jnp.zeros((center.shape[0], LANES), f32)
    for at, part in enumerate(split_three(center) + split_three(spread)):
        packed = jnp.where(lane == at, widen(part), packed)
    return packed.astype(bf16)


def unpack_stats(packed):
    lane = lax.broadcasted_iota(jnp.int32, (1, LANES), 1)
    values = widen(packed)
    center = jnp.sum(jnp.where(lane < 3, values, 0.0), axis=-1, keepdims=True)
    spread = jnp.sum(jnp.where((lane >= 3) & (lane < 6), values, 0.0), axis=-1, keepdims=True)
    return center, spread


def joined_product(one, two, side_one, side_two, features):
    center_one, spread_one = unpack_stats(one[:, features:])
    center_two, spread_two = unpack_stats(two[:, features:])
    center = 0.5 * (center_one + center_two)
    apart = 0.5 * (center_one - center_two)
    inverse = lax.rsqrt(0.5 * (spread_one + spread_two) + apart * apart + epsilon)
    product = inverse * (
        widen(one[:, :features])
        + widen(two[:, :features])
        + apart * (side_one[0:1, :] - side_two[0:1, :])
    )
    return center, inverse, product


def centered_product(values, gain, weight):
    center = jnp.mean(values, axis=-1, keepdims=True)
    away = values - center
    spread = jnp.mean(away * away, axis=-1, keepdims=True)
    product = lax.dot_general(
        (away * gain).astype(bf16), weight, TRANSPOSED, preferred_element_type=f32
    )
    return product.astype(bf16), pack_stats(center, spread)


def side_rows(gain, offset, weight):
    gain_high, gain_low = two_parts(gain)
    offset_high, offset_low = two_parts(offset)
    filler = jnp.zeros((4, gain.shape[1]), bf16)
    stacked = jnp.concatenate([gain_high, gain_low, offset_high, offset_low, filler], 0)
    rows = lax.dot_general(stacked, weight, TRANSPOSED, preferred_element_type=f32)
    return jnp.concatenate(
        [rows[0:1] + rows[1:2], rows[2:3] + rows[3:4], jnp.zeros((6, rows.shape[1]), f32)], 0
    )


def accumulate(ref, row, values):
    total = jnp.sum(values, axis=0, keepdims=True)
    first = pl.program_id(0) == 0
    ref[row : row + 1, :] = jnp.where(first, total, ref[row : row + 1, :] + total)


def square_end(own, seconds, factor):
    rows = own[0].shape[0] // factor
    width = sum(each.shape[1] for each in own)

    def body(*refs):
        ins, outs = refs[: 2 * len(own)], refs[2 * len(own) :]
        for at, out in enumerate(outs):
            left = 0
            for mine, theirs in zip(ins[: len(own)], ins[len(own) :]):
                span = slice(at * rows, (at + 1) * rows)
                total = mine[span, :] + widen(theirs[span, :])
                out[:, left : left + mine.shape[1]] = total.astype(out.dtype)
                left += mine.shape[1]

    return pl.pallas_call(
        body,
        out_shape=[shape_of((rows, width), f32)] + [shape_of((rows, width), bf16)] * (factor - 1),
        in_specs=[pl.BlockSpec(memory_space=pltpu.VMEM)] * (2 * len(own)),
        out_specs=[pl.BlockSpec(memory_space=pltpu.VMEM)] * factor,
        name="square_end",
    )(*own, *seconds)


def pack(first_sums, first_other, model_sums, grad_sums, bias_sums, head_sums, hidden_sums):
    def body(first, other, model, grad, bias, head, hidden, out):
        at = 0
        rows = [first[0:1, :] + other[0:1, :], first[1:2, :] + other[1:2, :]]
        rows += [model[0:1, :], model[1:2, :], model[2:3, :], grad[0:1, :]]
        rows += [bias[0:1, :], bias[1:2, :], head[0:1, :], head[1:2, :]]
        rows += [hidden[0:1, :], hidden[1:2, :], hidden[2:3, :]]
        for row in rows:
            for left in range(0, row.shape[1], LANES):
                out[at : at + 1, :] = row[:, left : left + LANES]
                at += 1

    parts = (first_sums, first_other, model_sums, grad_sums, bias_sums, head_sums, hidden_sums)
    count = 6 * model_sums.shape[1] + 4 * head_sums.shape[1] + 3 * hidden_sums.shape[1]
    return pl.pallas_call(
        body,
        out_shape=shape_of((count // LANES, LANES), f32),
        in_specs=[pl.BlockSpec(memory_space=pltpu.VMEM)] * len(parts),
        out_specs=pl.BlockSpec(memory_space=pltpu.VMEM),
        name="pack",
    )(*parts)


def unpack(one, two, shapes):
    def body(one_ref, two_ref, *outs):
        total = one_ref[...] + two_ref[...]
        at = 0
        for out in outs:
            for row in range(out.shape[0]):
                for left in range(0, out.shape[1], LANES):
                    out[row : row + 1, left : left + LANES] = total[at : at + 1, :]
                    at += 1

    return pl.pallas_call(
        body,
        out_shape=[shape_of(shape, f32) for shape in shapes],
        in_specs=[pl.BlockSpec(memory_space=pltpu.VMEM)] * 2,
        out_specs=[pl.BlockSpec(memory_space=pltpu.VMEM)] * len(shapes),
        name="unpack",
    )(one, two)


def prepare(core, tokens, tokens_other, cotangent, cotangent_other, model_vectors):
    rows, features = tokens.shape
    share = TILES // 2
    tile = rows // share

    def body(
        core_ref, x_own, x_other, g_own, g_other, model, inputs, grads, normal, turned, g_turned, sums
    ):
        here = pl.program_id(0) // share == core_ref[0]
        x = jnp.where(here, x_own[...], x_other[...])
        g = jnp.where(here, g_own[...], g_other[...])
        inputs[...] = x
        grads[...] = g
        n, _ = normal_of(widen(x))
        a = (n * model[0:1, :] + model[1:2, :]).astype(bf16)
        normal[...] = a
        turned[...] = a.T
        g_turned[...] = g.T
        accumulate(sums, 0, widen(g))

    own = pl.BlockSpec(
        (tile, features), lambda i, core: (jnp.clip(i - core[0] * share, 0, share - 1), 0)
    )
    other = pl.BlockSpec(
        (tile, features), lambda i, core: (jnp.clip(i - (1 - core[0]) * share, 0, share - 1), 0)
    )
    straight = pl.BlockSpec((tile, features), lambda i, core: (i, 0))
    across = pl.BlockSpec((features, tile), lambda i, core: (0, i))
    return pl.pallas_call(
        body,
        grid_spec=pltpu.PrefetchScalarGridSpec(
            num_scalar_prefetch=1,
            grid=(TILES,),
            in_specs=[own, other, own, other]
            + [pl.BlockSpec(model_vectors.shape, lambda i, core: (0, 0))],
            out_specs=[straight] * 3
            + [across] * 2
            + [pl.BlockSpec((8, features), lambda i, core: (0, 0))],
        ),
        out_shape=[shape_of((2 * rows, features), bf16)] * 3
        + [shape_of((features, 2 * rows), bf16)] * 2
        + [shape_of((8, features), f32)],
        compiler_params=PARAMS,
        cost_estimate=cost(20 * rows * features, 28 * rows * features),
        name="prepare",
    )(core, tokens, tokens_other, cotangent, cotangent_other, model_vectors)


def join(*parts):
    rows, width = parts[0].shape[0], sum(part.shape[1] for part in parts)

    def body(*refs):
        left = 0
        for ref in refs[:-1]:
            refs[-1][:, left : left + ref.shape[1]] = ref[...]
            left += ref.shape[1]

    return pl.pallas_call(
        body,
        out_shape=shape_of((rows, width), parts[0].dtype),
        in_specs=[pl.BlockSpec(memory_space=pltpu.VMEM)] * len(parts),
        out_specs=pl.BlockSpec(memory_space=pltpu.VMEM),
        name="join",
    )(*parts)


def project(order, pieces, attend_in, bias):
    length, features = attend_in.shape
    width = bias.shape[1]
    third = width // 3
    count = order.shape[0]

    def body(order_ref, *refs):
        pieces_in, (rows, bias_row, weight, *outs) = refs[:5], refs[5:]

        @pl.when(pl.program_id(0) == 0)
        def _():
            place_rows(order_ref, pieces_in, (weight,), count)

        states = jnp.dot(rows[...], weight[...], preferred_element_type=f32) + bias_row[...]
        for at, out in enumerate(outs):
            out[...] = states[:, at * third : (at + 1) * third].astype(bf16)

    return pl.pallas_call(
        body,
        grid=(TILES,),
        out_shape=[shape_of((features, width), bf16)] + [shape_of((length, third), bf16)] * 3,
        in_specs=[SMEM]
        + [whole(piece.shape) for piece in pieces]
        + [rows_of(attend_in), whole(bias.shape)],
        out_specs=[whole((features, width))]
        + [pl.BlockSpec((length // TILES, third), lambda i: (i, 0))] * 3,
        compiler_params=PARAMS,
        cost_estimate=cost(
            2 * length * features * width, 4 * features * width + 2 * length * (features + width)
        ),
        name="project",
    )(order, *pieces, attend_in, bias)


def attend_forward(pair, prefix, queries, keys, values):
    length = queries.shape[0]
    tile = length // 2

    def body(prefix_ref, query_ref, key_ref, value_ref, out_ref, log_ref, turned):
        turned[...] = value_ref[...].T
        first_half = lax.broadcasted_iota(jnp.int32, (1, PAIR), 1) < HEAD_DIM
        key_rows = key_ref[...]
        row_at = lax.broadcasted_iota(jnp.int32, (length, 1), 0)
        for start in range(0, length, tile):
            columns = slice(start, start + tile)
            places = lax.broadcasted_iota(jnp.int32, (1, tile), 1) + (start + 1)
            limit = jnp.maximum(places, prefix_ref[0])
            query_rows = query_ref[columns, :]
            parts = []
            for head in (0, 1):
                mine = jnp.where(
                    first_half == (head == 0), query_rows, jnp.zeros_like(query_rows)
                )
                scores = lax.dot_general(key_rows, mine, TRANSPOSED, preferred_element_type=f32)
                scores = jnp.where(row_at < limit, scores, masked)
                top = jnp.max(scores, axis=0, keepdims=True)
                raised = jnp.exp2((scores - top) * (SCALE * LOG2E))
                total = jnp.sum(raised, axis=0, keepdims=True)
                mixed = jnp.dot(
                    turned[head * HEAD_DIM : (head + 1) * HEAD_DIM, :],
                    raised.astype(bf16),
                    preferred_element_type=f32,
                )
                parts.append(mixed / total)
                log_ref[head : head + 1, columns] = top * (SCALE * LOG2E) + jnp.log2(total)
            out_ref[columns, :] = jnp.concatenate(parts, 0).T

    block = pl.BlockSpec((length, PAIR), lambda i: (0, pair))
    return pl.pallas_call(
        body,
        grid=(1,),
        out_shape=[shape_of((length, PAIR), f32), shape_of((8, length), f32)],
        in_specs=[SMEM, block, block, block],
        out_specs=[whole((length, PAIR)), whole((8, length))],
        scratch_shapes=[pltpu.VMEM((PAIR, length), bf16)],
        compiler_params=PARAMS,
        cost_estimate=cost(
            16 * length * length * PAIR, 10 * length * PAIR, 2 * length * length
        ),
        name="attend_forward",
    )(prefix, queries, keys, values)


def attend_backward(pair, prefix, queries, keys, values, attended, grads, logs):
    length = queries.shape[0]
    tile = length // 4

    def body(
        prefix_ref,
        query_ref,
        key_ref,
        value_ref,
        attended_ref,
        grad_ref,
        log_ref,
        query_out,
        key_out,
        value_out,
        turned,
        key_total,
        value_total,
    ):
        turned[...] = key_ref[...].T
        first_half = lax.broadcasted_iota(jnp.int32, (1, PAIR), 1) < HEAD_DIM
        key_rows, value_rows = key_ref[...], value_ref[...]
        row_at = lax.broadcasted_iota(jnp.int32, (length, 1), 0)
        for start in range(0, length, tile):
            columns = slice(start, start + tile)
            places = lax.broadcasted_iota(jnp.int32, (1, tile), 1) + (start + 1)
            limit = jnp.maximum(places, prefix_ref[0])
            query_rows, grad_rows = query_ref[columns, :], grad_ref[columns, :]
            crossed = (attended_ref[columns, :] * widen(grad_rows)).T
            parts = []
            key_part = value_part = 0.0
            for head in (0, 1):
                side = first_half == (head == 0)
                span = slice(head * HEAD_DIM, (head + 1) * HEAD_DIM)
                mine = jnp.where(side, query_rows, jnp.zeros_like(query_rows))
                grad = jnp.where(side, grad_rows, jnp.zeros_like(grad_rows))
                level = jnp.sum(crossed[span, :], axis=0, keepdims=True)
                scores = lax.dot_general(key_rows, mine, TRANSPOSED, preferred_element_type=f32)
                raised = jnp.exp2(
                    scores * (SCALE * LOG2E) - log_ref[head : head + 1, columns]
                )
                probs = jnp.where(row_at < limit, raised, 0.0)
                prob_grad = lax.dot_general(
                    value_rows, grad, TRANSPOSED, preferred_element_type=f32
                )
                score_grad = (probs * (prob_grad - level)).astype(bf16)
                value_part += jnp.dot(probs.astype(bf16), grad, preferred_element_type=f32)
                key_part += jnp.dot(score_grad, mine, preferred_element_type=f32)
                parts.append(jnp.dot(turned[span, :], score_grad, preferred_element_type=f32))
            query_out[columns, :] = (jnp.concatenate(parts, 0).T * SCALE).astype(bf16)
            if start == 0:
                key_total[...] = key_part
                value_total[...] = value_part
            else:
                key_total[...] += key_part
                value_total[...] += value_part
        key_out[...] = (key_total[...] * SCALE).astype(bf16)
        value_out[...] = value_total[...].astype(bf16)

    block = pl.BlockSpec((length, PAIR), lambda i: (0, pair))
    return pl.pallas_call(
        body,
        grid=(1,),
        out_shape=[shape_of((length, PAIR), bf16)] * 3,
        in_specs=[SMEM] + [block] * 3 + [whole((length, PAIR)), block, whole((8, length))],
        out_specs=[whole((length, PAIR))] * 3,
        scratch_shapes=[
            pltpu.VMEM((PAIR, length), bf16),
            pltpu.VMEM((length, PAIR), f32),
            pltpu.VMEM((length, PAIR), f32),
        ],
        compiler_params=PARAMS,
        cost_estimate=cost(
            40 * length * length * PAIR, 18 * length * PAIR, 2 * length * length
        ),
        name="attend_backward",
    )(prefix, queries, keys, values, attended, grads, logs)


def mix(order, pieces, attended, head_vectors, widths):
    length = attended[0].shape[0]
    width = PAIR * len(attended)
    count = order.shape[0]
    features = pieces[0].shape[0] // (count // 4) * count

    def body(order_ref, *refs):
        pieces_in, rows, (vectors, weight, second, product, side) = refs[:5], refs[5:-5], refs[-5:]

        @pl.when(pl.program_id(0) == 0)
        def _():
            place_rows(order_ref, pieces_in, (weight, second), count)
            side[...] = side_rows(vectors[2:3, :], vectors[3:4, :], weight[...])

        out, stats = centered_product(
            jnp.concatenate([part[...] for part in rows], 1), vectors[2:3, :], weight[...])
        product[:, :features] = out
        product[:, features:] = stats

    return pl.pallas_call(
        body,
        grid=(TILES,),
        out_shape=[shape_of((features, each), bf16) for each in widths]
        + [shape_of((length, features + LANES), bf16), shape_of((8, features), f32)],
        in_specs=[SMEM]
        + [whole(piece.shape) for piece in pieces]
        + [rows_of(part) for part in attended]
        + [whole(head_vectors.shape)],
        out_specs=[whole((features, each)) for each in widths]
        + [
            pl.BlockSpec((length // TILES, features + LANES), lambda i: (i, 0)),
            whole((8, features)),
        ],
        compiler_params=PARAMS,
        cost_estimate=cost(
            2 * length * features * width, 4 * features * sum(widths) + 6 * length * features
        ),
        name="mix",
    )(order, *pieces, *attended, head_vectors)


def feed_up(product, product_other, side, side_other, inputs, weight, model_vectors, hidden_vectors):
    length, features = inputs.shape
    width = weight.shape[1]

    def body(one, two, side_one, side_two, x, weight_ref, model, hidden, middle, turned, kept, slope):
        _, _, branch = joined_product(one[...], two[...], side_one, side_two, features)
        offset = side_one[1:2, :] + side_two[1:2, :] + model[2:3, :]
        total = widen(x[...]) + (branch + offset)
        middle[...] = total
        normal, _ = normal_of(total)
        feed = (normal * model[3:4, :] + model[4:5, :]).astype(bf16)
        turned[...] = feed.T
        before = jnp.dot(feed, weight_ref[...], preferred_element_type=f32) + hidden[0:1, :]
        share = 0.5 + 0.5 * lax.erf(before * 0.7071067811865476)
        kept[...] = (before * share).astype(bf16)
        slope[...] = (
            share + before * (0.3989422804014327 * jnp.exp(-0.5 * before * before))
        ).astype(bf16)

    return pl.pallas_call(
        body,
        grid=(TILES,),
        out_shape=[
            shape_of((length, features), f32),
            shape_of((features, length), bf16),
            shape_of((length, width), bf16),
            shape_of((length, width), bf16),
        ],
        in_specs=[
            rows_of(product),
            rows_of(product),
            whole(side.shape),
            whole(side.shape),
            rows_of(inputs),
            whole(weight.shape),
            whole(model_vectors.shape),
            whole(hidden_vectors.shape),
        ],
        out_specs=[
            rows_of(inputs),
            pl.BlockSpec((features, length // TILES), lambda i: (0, i)),
            pl.BlockSpec((length // TILES, width), lambda i: (i, 0)),
            pl.BlockSpec((length // TILES, width), lambda i: (i, 0)),
        ],
        compiler_params=PARAMS,
        cost_estimate=cost(
            2 * length * features * width,
            2 * features * width + 12 * length * features + 4 * length * width,
            2 * length * width,
        ),
        name="feed_up",
    )(product, product_other, side, side_other, inputs, weight, model_vectors, hidden_vectors)


def feed_down(order, pieces, kept, hidden_vectors):
    length, width = kept.shape
    count = order.shape[0]
    features = pieces[0].shape[0] // (count // 4) * count

    def body(order_ref, *refs):
        pieces_in, (rows, vectors, weight, product, side) = refs[:5], refs[5:]

        @pl.when(pl.program_id(0) == 0)
        def _():
            place_rows(order_ref, pieces_in, (weight,), count)
            side[...] = side_rows(vectors[1:2, :], vectors[2:3, :], weight[...])

        out, stats = centered_product(widen(rows[...]), vectors[1:2, :], weight[...])
        product[:, :features] = out
        product[:, features:] = stats

    return pl.pallas_call(
        body,
        grid=(TILES,),
        out_shape=[
            shape_of((features, width), bf16),
            shape_of((length, features + LANES), bf16),
            shape_of((8, features), f32),
        ],
        in_specs=[SMEM]
        + [whole(piece.shape) for piece in pieces]
        + [rows_of(kept), whole(hidden_vectors.shape)],
        out_specs=[
            whole((features, width)),
            pl.BlockSpec((length // TILES, features + LANES), lambda i: (i, 0)),
            whole((8, features)),
        ],
        compiler_params=PARAMS,
        cost_estimate=cost(
            2 * length * features * width, 4 * features * width + 2 * length * (features + width)
        ),
        name="feed_down",
    )(order, *pieces, kept, hidden_vectors)


def feed_back(
    core,
    product,
    product_other,
    side,
    side_other,
    middle,
    cotangent,
    kept,
    slope,
    down,
    up,
    model_vectors,
    hidden_vectors,
):
    length, features = middle.shape
    width = kept.shape[1]
    joined = 2 * width
    share = TILES // 2

    def body(
        core_ref, one, two, side_one, side_two, mid, grad, kept_ref, slope_ref, down_ref, up_ref,
        model, hidden, output, norm_out, before_out, product_out, sums,
    ):
        center, inverse, branch = joined_product(one[...], two[...], side_one, side_two, features)
        offset = side_one[1:2, :] + side_two[1:2, :] + model[5:6, :]

        @pl.when(pl.program_id(0) // share == core_ref[0])
        def _():
            output[...] = (mid[...] + (branch + offset)).astype(bf16)

        rows = widen(grad[...])
        straight = side_one[0:1, :] + side_two[0:1, :]
        mean_scaled = jnp.sum(rows * straight, axis=-1, keepdims=True) / joined
        mean_crossed = jnp.sum(rows * branch, axis=-1, keepdims=True) / joined
        mid_grad = jnp.dot(grad[...], down_ref[...], preferred_element_type=f32)
        normal = (widen(kept_ref[...]) - center) * inverse
        norm_out[...] = (normal * hidden[1:2, :] + hidden[2:3, :]).astype(bf16)
        accumulate(sums, 1, mid_grad * normal)
        accumulate(sums, 2, mid_grad)
        hidden_grad = inverse * (
            mid_grad * hidden[1:2, :] - mean_scaled - normal * mean_crossed
        )
        before = (hidden_grad * widen(slope_ref[...])).astype(bf16)
        before_out[...] = before
        accumulate(sums, 0, widen(before))
        product_out[...] = lax.dot_general(
            before, up_ref[...], TRANSPOSED, preferred_element_type=f32
        ).astype(bf16)

    tile = length // TILES

    def at_rows(columns):
        return pl.BlockSpec((tile, columns), lambda i, core: (i, 0))

    def fixed(array):
        return pl.BlockSpec(array.shape, lambda i, core: (0, 0))

    return pl.pallas_call(
        body,
        grid_spec=pltpu.PrefetchScalarGridSpec(
            num_scalar_prefetch=1,
            grid=(TILES,),
            in_specs=[
                at_rows(features + LANES),
                at_rows(features + LANES),
                fixed(side),
                fixed(side),
                at_rows(features),
                at_rows(features),
                at_rows(width),
                at_rows(width),
                fixed(down),
                fixed(up),
                fixed(model_vectors),
                fixed(hidden_vectors),
            ],
            out_specs=[
                pl.BlockSpec(
                    (tile, features), lambda i, core: (jnp.clip(i - core[0] * share, 0, share - 1), 0)
                ),
                at_rows(width),
                at_rows(width),
                at_rows(features),
                pl.BlockSpec((8, width), lambda i, core: (0, 0)),
            ],
        ),
        out_shape=[
            shape_of((length // 2, features), bf16),
            shape_of((length, width), bf16),
            shape_of((length, width), bf16),
            shape_of((length, features), bf16),
            shape_of((8, width), f32),
        ],
        compiler_params=PARAMS,
        cost_estimate=cost(
            4 * length * features * width,
            4 * features * width + 12 * length * features + 8 * length * width,
        ),
        name="feed_back",
    )(
        core,
        product,
        product_other,
        side,
        side_other,
        middle,
        cotangent,
        kept,
        slope,
        down,
        up,
        model_vectors,
        hidden_vectors,
    )


def mix_back(
    passed,
    passed_other,
    product,
    product_other,
    side,
    side_other,
    middle,
    cotangent,
    attended,
    weight,
    model_vectors,
    head_vectors,
):
    length, features = middle.shape
    width = PAIR * len(attended)
    joined = 2 * width

    def body(
        back_one, back_two, one, two, side_one, side_two, mid, grad, *refs
    ):
        attended_refs, (weight_ref, model, head, middle_out, turned, mixed_out, attended_out, sums, head_sums) = refs[:-9], refs[-9:]
        feed_grad = widen(back_one[...]) + widen(back_two[...])
        normal, inverse = normal_of(mid[...])
        accumulate(sums, 1, feed_grad * normal)
        accumulate(sums, 2, feed_grad)
        middle_grad = widen(grad[...]) + normal_back(feed_grad * model[3:4, :], normal, inverse)
        middle_out[...] = middle_grad
        branch_grad = middle_grad.astype(bf16)
        rows = widen(branch_grad)
        accumulate(sums, 0, rows)
        turned[...] = branch_grad.T
        center, inverse_two, branch = joined_product(
            one[...], two[...], side_one, side_two, features
        )
        straight = side_one[0:1, :] + side_two[0:1, :]
        mean_scaled = jnp.sum(rows * straight, axis=-1, keepdims=True) / joined
        mean_crossed = jnp.sum(rows * branch, axis=-1, keepdims=True) / joined
        mixed_grad = jnp.dot(branch_grad, weight_ref[...], preferred_element_type=f32)
        attended_rows = jnp.concatenate([part[...] for part in attended_refs], 1)
        normal_two = (attended_rows - center) * inverse_two
        mixed_out[...] = (normal_two * head[2:3, :] + head[3:4, :]).astype(bf16)
        accumulate(head_sums, 0, mixed_grad * normal_two)
        accumulate(head_sums, 1, mixed_grad)
        attended_out[...] = (
            inverse_two * (mixed_grad * head[2:3, :] - mean_scaled - normal_two * mean_crossed)
        ).astype(bf16)

    tile = length // TILES
    return pl.pallas_call(
        body,
        grid=(TILES,),
        out_shape=[
            shape_of((length, features), f32),
            shape_of((features, length), bf16),
            shape_of((length, width), bf16),
            shape_of((length, width), bf16),
            shape_of((8, features), f32),
            shape_of((8, width), f32),
        ],
        in_specs=[
            rows_of(passed),
            rows_of(passed),
            rows_of(product),
            rows_of(product),
            whole(side.shape),
            whole(side.shape),
            rows_of(middle),
            rows_of(cotangent),
            *[rows_of(part) for part in attended],
            whole(weight.shape),
            whole(model_vectors.shape),
            whole(head_vectors.shape),
        ],
        out_specs=[
            rows_of(middle),
            pl.BlockSpec((features, tile), lambda i: (0, i)),
            pl.BlockSpec((tile, width), lambda i: (i, 0)),
            pl.BlockSpec((tile, width), lambda i: (i, 0)),
            whole((8, features)),
            whole((8, width)),
        ],
        compiler_params=PARAMS,
        cost_estimate=cost(
            2 * length * features * width, 2 * features * width + 24 * length * features
        ),
        name="mix_back",
    )(
        passed,
        passed_other,
        product,
        product_other,
        side,
        side_other,
        middle,
        cotangent,
        *attended,
        weight,
        model_vectors,
        head_vectors,
    )


def project_back(core, groups, weight):
    length = groups[0][0].shape[0]
    parts = [part for group in groups for part in group]
    features, width = weight.shape
    third = width // 3
    tile = length // TILES
    share = TILES // 2
    each = len(groups[0])

    def body(core_ref, *refs):
        weight_ref, send, keep, sums = refs[-4:]
        grads = [
            jnp.concatenate([ref[...] for ref in refs[at * each : (at + 1) * each]], 1)
            for at in range(3)
        ]
        total = lax.dot_general(
            jnp.concatenate(grads, 1), weight_ref[...], TRANSPOSED, preferred_element_type=f32
        )
        accumulate(sums, 0, widen(grads[0]))
        accumulate(sums, 1, widen(grads[2]))

        @pl.when(pl.program_id(0) < share)
        def _():
            send[...] = total.astype(bf16)

        @pl.when(pl.program_id(0) >= share)
        def _():
            keep[...] = total

    moved = pl.BlockSpec((tile, PAIR), lambda i, core: ((i + (1 - core[0]) * share) % TILES, 0))
    return pl.pallas_call(
        body,
        grid_spec=pltpu.PrefetchScalarGridSpec(
            num_scalar_prefetch=1,
            grid=(TILES,),
            in_specs=[moved] * len(parts) + [pl.BlockSpec(weight.shape, lambda i, core: (0, 0))],
            out_specs=[
                pl.BlockSpec((tile, features), lambda i, core: (jnp.minimum(i, share - 1), 0)),
                pl.BlockSpec((tile, features), lambda i, core: (jnp.maximum(i - share, 0), 0)),
                pl.BlockSpec((8, third), lambda i, core: (0, 0)),
            ],
        ),
        out_shape=[
            shape_of((length // 2, features), bf16),
            shape_of((length // 2, features), f32),
            shape_of((8, third), f32),
        ],
        compiler_params=PARAMS,
        cost_estimate=cost(
            2 * length * features * width, 2 * features * width + 6 * length * (features + third)
        ),
        name="project_back",
    )(core, *parts, weight)


def input_back(core, received, kept, middle_grad, tokens, model_vectors):
    rows, features = tokens.shape
    tiles = TILES // 2
    tile = rows // tiles

    def body(core_ref, got, own, mid, x, model, out, sums):
        grad = widen(got[...]) + own[...]
        normal, inverse = normal_of(widen(x[...]))
        accumulate(sums, 0, grad * normal)
        accumulate(sums, 1, grad)
        out[...] = mid[...] + normal_back(grad * model[0:1, :], normal, inverse)

    near = pl.BlockSpec((tile, features), lambda i, core: (i, 0))
    return pl.pallas_call(
        body,
        grid_spec=pltpu.PrefetchScalarGridSpec(
            num_scalar_prefetch=1,
            grid=(tiles,),
            in_specs=[
                near,
                near,
                pl.BlockSpec((tile, features), lambda i, core: (i + core[0] * tiles, 0)),
                near,
                pl.BlockSpec(model_vectors.shape, lambda i, core: (0, 0)),
            ],
            out_specs=[near, pl.BlockSpec((8, features), lambda i, core: (0, 0))],
        ),
        out_shape=[shape_of((rows, features), f32), shape_of((8, features), f32)],
        compiler_params=PARAMS,
        cost_estimate=cost(10 * rows * features, 16 * rows * features),
        name="input_back",
    )(core, received, kept, middle_grad, tokens, model_vectors)


def weight_grad(order, pairs, tile):
    features, tokens = pairs[0][0].shape
    lefts, groups = [], []
    for left, group in pairs:
        if not any(left is known for known in lefts):
            lefts.append(left)
        groups.append(([left is known for known in lefts].index(True), len(group)))
    rights = [right for _, group in pairs for right in group]
    width = sum(right.shape[1] for right in rights)
    count = order.shape[0]
    shard = features // count
    single = len(rights) == 1

    def body(order_ref, *refs):
        left_refs, right_refs = refs[: len(lefts)], refs[len(lefts) : -3]
        keep, send, total = refs[-3:]
        if single:
            total[...] = jnp.dot(left_refs[0][...], right_refs[0][...], preferred_element_type=f32)
        else:
            first = 0
            for step, (at, size) in enumerate(groups):

                @pl.when(pl.program_id(0) == step)
                def _(at=at, first=first, size=size):
                    right = [ref[...] for ref in right_refs[first : first + size]]
                    total[...] = jnp.dot(
                        left_refs[at][...],
                        jnp.concatenate(right, 1) if size > 1 else right[0],
                        preferred_element_type=f32,
                    )

                first += size

        for block in range(count):
            place = pl.multiple_of(order_ref[block] * shard, 16)
            out, at = (keep, block) if block < count // 2 else (send, block - count // 2)
            out[at * shard : (at + 1) * shard, :] = total[pl.ds(place, shard), :].astype(bf16)

    return pl.pallas_call(
        body,
        grid=(width // tile,),
        out_shape=[shape_of((features // 2, width), bf16)] * 2,
        in_specs=[SMEM]
        + [whole(left.shape) for left in lefts]
        + (
            [pl.BlockSpec((tokens, tile), lambda i: (0, i))]
            if single
            else [whole(right.shape) for right in rights]
        ),
        out_specs=[pl.BlockSpec((features // 2, tile), lambda i: (0, i))] * 2,
        scratch_shapes=[pltpu.VMEM((features, tile), f32)],
        compiler_params=PARAMS,
        cost_estimate=cost(
            2 * tokens * features * width,
            2 * (tokens * (features + width) + features * width),
        ),
        name="weight_grad",
    )(order, *lefts, *rights)


def on_device(
    tokens,
    cotangent,
    prefix,
    query_weight,
    key_weight,
    value_weight,
    out_weight,
    up_weight,
    down_weight,
    model_vectors,
    head_vectors,
    hidden_vectors,
):
    ring = Ring(lax.axis_size("dp"))
    order = ring.gather_order()
    near, far = ring.scatter_order(1), ring.scatter_order(2)
    core = lax.axis_index("tensor").astype(jnp.int32)[None]
    half, full = query_weight.shape[1], up_weight.shape[1]
    features = tokens.shape[1]

    bias = jnp.concatenate([head_vectors[0], jnp.zeros_like(head_vectors[0]), head_vectors[1]])
    pair_count = half // PAIR
    tokens_other, cotangent_other = flip_partner(tokens), flip_partner(cotangent)
    first_block = ring.along_lines(join(query_weight, key_weight, value_weight))
    first_sides = ring.to_sides(first_block)
    second = after(join(out_weight, up_weight), first_block)
    whole_rows = after((tokens, tokens_other, cotangent, cotangent_other), first_block)
    inputs, grads, attend_in, attend_turned, grads_turned, grad_sums = prepare(
        core, *whole_rows, model_vectors
    )
    second_block = ring.along_lines(second, lambda got: after(got, attend_in))
    first_sides = after(first_sides, attend_in)
    first_pieces = (first_block, *first_sides, *ring.to_corner(*first_sides))

    second_sides = ring.to_sides(after(second_block, first_pieces))
    third = after(down_weight, second_block)
    first_weight, queries, keys, values = project(order, first_pieces, attend_in, bias[None])
    states = (prefix, queries, keys, values)
    attended, logs = zip(*[attend_forward(pair, *states) for pair in range(pair_count - 1)])
    third_block = ring.along_lines(third, lambda got: after(got, attended))
    second_sides = after(second_sides, attended)
    second_pieces = (second_block, *second_sides, *ring.to_corner(*second_sides))
    third_sides = ring.to_sides(after(third_block, second_sides))
    last, last_logs = attend_forward(pair_count - 1, *after(states, second_sides, third_block))
    attended, logs = (*attended, last), (*logs, last_logs)
    second_pieces = (second_block, *second_sides, *after(second_pieces[3:], last))
    out_full, up_full, mixed, mixed_side = mix(
        order, second_pieces, attended, head_vectors, (half, full)
    )
    mixed_other, mixed_side_other = flip_partner(mixed), flip_partner(mixed_side)
    third_sides = after(third_sides, mixed)
    third_corner = ring.to_corner(*third_sides)
    middle, feed_turned, kept, slope = feed_up(
        mixed,
        after(mixed_other, third_sides),
        mixed_side,
        mixed_side_other,
        inputs,
        up_full,
        model_vectors,
        hidden_vectors,
    )
    third_pieces = (third_block, *third_sides, *after(third_corner, kept))
    down_full, fed, fed_side = feed_down(order, third_pieces, kept, hidden_vectors)
    fed_other, fed_side_other = flip_partner(fed), flip_partner(fed_side)
    output, feed_mid, before_grad, passed, hidden_sums = feed_back(
        core,
        fed,
        fed_other,
        fed_side,
        fed_side_other,
        middle,
        grads,
        kept,
        slope,
        down_full,
        up_full,
        model_vectors,
        hidden_vectors,
    )
    passed_other = flip_partner(passed)
    down_keep, down_send = weight_grad(far, [(grads_turned, [feed_mid])], full // 2)
    up_keep, up_send = weight_grad(near, [(feed_turned, [before_grad])], full // 2)
    down_got, up_got = ring.flip(down_send, 2), ring.flip(up_send, 1)

    middle_grad, branch_turned, mixed_in, attended_grad, model_sums, head_sums = mix_back(
        passed,
        passed_other,
        mixed,
        mixed_other,
        mixed_side,
        mixed_side_other,
        middle,
        grads,
        attended,
        out_full,
        model_vectors,
        head_vectors,
    )
    def pair_back(pair, grad):
        return attend_backward(pair, *states, attended[pair], grad, logs[pair])

    pair_grads = [pair_back(pair, attended_grad) for pair in range(pair_count - 1)]
    down_own, down_away = ring.sum_first(down_keep, after(down_got, pair_grads))
    up_own, up_away = ring.sum_first(up_keep, after(up_got, pair_grads))
    up_second, down_second = ring.flip(up_away, 2), ring.flip(down_away, 1)
    pair_grads.append(pair_back(pair_count - 1, after(attended_grad, down_away, up_away)))
    query_grad, key_grad, value_grad = ([pair[at] for pair in pair_grads] for at in range(3))
    wide_seconds = after((up_second, down_second), pair_grads)

    progress = {}

    def during_wide(got, parts):
        tied_query, tied_value = after((query_grad, value_grad), parts)
        query_keep, query_send = weight_grad(
            near, [(attend_turned, tied_query), (attend_turned, tied_value)], half
        )
        query_got = ring.flip(query_send, 1)
        key_keep, key_send = weight_grad(
            far, [(attend_turned, after(key_grad, query_send)), (branch_turned, [mixed_in])], half
        )
        key_got = ring.flip(key_send, 2)
        sums = project_back(
            core, after((query_grad, key_grad, value_grad), key_send), first_weight
        )
        progress["narrow"] = (query_keep, query_got, key_keep, key_got)
        progress["project"] = sums
        return after(got, sums)

    if len(ring.lines) > 1:
        during_wide([], [])
        wide_grads = ring.sum_lines((up_own, down_own), wide_seconds, lambda got, parts: got)
    else:
        wide_grads = ring.sum_lines((up_own, down_own), wide_seconds, during_wide)
    up_grad, down_grad = wide_grads[:, :full], wide_grads[:, full:]
    query_keep, query_got, key_keep, key_got = progress["narrow"]
    send, keep, bias_sums = progress["project"]
    received = flip_partner(send)
    query_own, query_away = ring.sum_first(query_keep, after(query_got, send))
    key_own, key_away = ring.sum_first(key_keep, after(key_got, send))
    narrow_seconds = ring.flip(query_away, 2), ring.flip(key_away, 1)
    input_grad, first_sums = input_back(
        core, received, after(keep, query_away, key_away), middle_grad, tokens, model_vectors
    )
    narrow_seconds = after(narrow_seconds, input_grad)
    packed = pack(
        first_sums, flip_partner(first_sums), model_sums, grad_sums, bias_sums, head_sums, hidden_sums
    )
    strides = ring.sum_strides()
    for stride in strides[:-1]:
        packed = packed + ring.flip(packed, stride)
    model_sum, head_sum, hidden_sum = unpack(
        packed, ring.flip(packed, strides[-1]), ((6, features), (4, half), (3, full))
    )
    narrow = ring.sum_lines(
        (query_own, key_own), after(narrow_seconds, wide_grads), lambda got, parts: got
    )
    query_weight_grad, value_weight_grad, key_weight_grad, out_grad = (
        narrow[:, at * half : (at + 1) * half] for at in range(4)
    )
    return (
        output,
        input_grad,
        query_weight_grad,
        key_weight_grad,
        value_weight_grad,
        out_grad,
        up_grad,
        down_grad,
        model_sum,
        head_sum,
        hidden_sum,
    )


def solution(mesh):
    return jax.shard_map(
        on_device,
        mesh=mesh,
        in_specs=(
            P(("dp", "tensor"), None),
            P(("dp", "tensor"), None),
            P("dp"),
            P("dp", "tensor"),
            P("dp", "tensor"),
            P("dp", "tensor"),
            P("dp", "tensor"),
            P("dp", "tensor"),
            P("dp", "tensor"),
            P(),
            P(None, "tensor"),
            P(None, "tensor"),
        ),
        out_specs=(
            P(("dp", "tensor"), None),
            P(("dp", "tensor"), None),
            P("dp", "tensor"),
            P("dp", "tensor"),
            P("dp", "tensor"),
            P("dp", "tensor"),
            P("dp", "tensor"),
            P("dp", "tensor"),
            P(),
            P(None, "tensor"),
            P(None, "tensor"),
        ),
        check_vma=False,
    )
```

```python
import jax
import jax.numpy as jnp
from jax import lax
from jax.experimental import pallas as pl
from jax.experimental.pallas import tpu as pltpu
from jax.sharding import PartitionSpec as P

HEAD_DIM = 64
PAIR = 2 * HEAD_DIM
LANES = 128
TILES = 4
SCALE = 0.125
LOG2E = 1.4426950408889634
WEIGHT = 4

epsilon = 1e-05
masked = -1e30

f32 = jnp.float32
bf16 = jnp.bfloat16
TRANSPOSED = (((1,), (1,)), ((), ()))
SMEM = pl.BlockSpec(memory_space=pltpu.SMEM)


def flip_partner(values):
    return lax.ppermute(values, "tensor", [(0, 1), (1, 0)])


def normal_of(values):
    center = jnp.mean(values, axis=-1, keepdims=True)
    spread = jnp.mean(values * values, axis=-1, keepdims=True) - center * center
    inverse = lax.rsqrt(spread + epsilon)
    return (values - center) * inverse, inverse


def normal_back(scaled, normal, inverse):
    return inverse * (
        scaled
        - jnp.mean(scaled, axis=-1, keepdims=True)
        - normal * jnp.mean(scaled * normal, axis=-1, keepdims=True)
    )


def widen(values):
    return values.astype(f32)


def after(values, *earlier):
    return lax.optimization_barrier((values, earlier))[0]


class Ring:
    def __init__(self, size):
        self.size = size
        rest, stride = size // 4, 4
        self.lines = []
        while rest > 1:
            factor = 4 if rest % 4 == 0 else 2 if rest % 2 == 0 else rest
            self.lines.append((factor, stride))
            rest, stride = rest // factor, stride * factor
        self.line_count = size // 4

    def shift(self, values, factor, stride, step):
        pairs = []
        for place in range(self.size):
            digit = place // stride % factor
            pairs.append((place, place + ((digit + step) % factor - digit) * stride))
        return lax.ppermute(values, "dp", pairs)

    def flip(self, values, stride):
        return self.shift(values, 2, stride, 1)

    def line_places(self, sign):
        own = lax.axis_index("dp")
        places = [jnp.int32(0)]
        for factor, stride in self.lines:
            digit = own // stride % factor
            places = [
                base + (digit + sign * step) % factor * stride
                for base in places
                for step in range(factor)
            ]
        return places

    def gather_order(self):
        own = lax.axis_index("dp")
        places = self.line_places_gather()
        return jnp.stack([base + (own % 4 ^ bits) for bits in (0, 1, 2, 3) for base in places])

    def line_places_gather(self):
        own = lax.axis_index("dp")
        places = [jnp.int32(0)]
        for factor, stride in self.lines:
            digit = own // stride % factor
            places = [
                base + (digit + factor - step) % factor * stride
                for step in range(factor)
                for base in places
            ]
        return places

    def start_gather(self, values):
        factor, stride = self.lines[0]
        return [self.shift(values, factor, stride, step) for step in range(1, factor)]

    def end_gather(self, values, got):
        block = jnp.concatenate([values, *got], 0)
        for factor, stride in self.lines[1:]:
            block = jnp.concatenate(
                [block] + [self.shift(block, factor, stride, step) for step in range(1, factor)], 0
            )
        return block

    def to_sides(self, block):
        return self.flip(block, 1), self.flip(block, 2)

    def to_corner(self, from_x, from_y):
        half = from_x.shape[0] // 2
        return self.flip(from_x[:half], 2), self.flip(from_y[half:], 1)

    def scatter_order(self, first_bit):
        own = lax.axis_index("dp")
        other_bit = 3 - first_bit
        places = self.line_places(1)
        return jnp.stack(
            [
                base + (own % 4 ^ (cross + side))
                for cross in (0, first_bit)
                for side in (0, other_bit)
                for base in places
            ]
        )

    def sum_first(self, keep, got):
        half = keep.shape[0] // 2
        own = widen(keep[:half]) + widen(got[:half])
        return own, (widen(keep[half:]) + widen(got[half:])).astype(bf16)

    def start_lines(self, parts):
        factor, stride = self.lines[0]
        return [self.shift(parts[step], factor, stride, step) for step in range(1, factor)]

    def last_terms(self, parts, got):
        terms = [parts[0], *got]
        for factor, stride in self.lines[1:]:
            total = add_up(terms)
            pieces = jnp.split(total, factor)
            terms = [pieces[0]] + [
                self.shift(pieces[step].astype(bf16), factor, stride, step)
                for step in range(1, factor)
            ]
        return terms

    def around(self, values, factor, stride):
        return [self.shift(values, factor, stride, step) for step in range(1, factor)]

    def around_square(self, values):
        pairs = [(place, place ^ 3) for place in range(self.size)]
        return [self.flip(values, 1), self.flip(values, 2), lax.ppermute(values, "dp", pairs)]


def add_up(terms):
    total = widen(terms[0])
    for term in terms[1:]:
        total = total + widen(term)
    return total


def whole(shape):
    return pl.BlockSpec(shape, lambda i: (0,) * len(shape))


def rows_of(array, tiles=TILES):
    return pl.BlockSpec((array.shape[0] // tiles, array.shape[1]), lambda i: (i, 0))


def shape_of(shape, dtype):
    return jax.ShapeDtypeStruct(shape, dtype)


def cost(flops, moved, exponentials=0):
    return pl.CostEstimate(flops=WEIGHT * flops, bytes_accessed=moved, transcendentals=exponentials)


PARAMS = pltpu.CompilerParams(vmem_limit_bytes=60 * 2**20)


def place_rows(order_ref, pieces, outs, count):
    own, from_x, from_y, corner_a, corner_b = pieces
    rows = own.shape[0]
    shard = rows // (count // 4)
    for block in range(count):
        kind, inner = divmod(block, count // 4)
        start = inner * shard
        ref = (own, from_x, from_y, corner_a)[kind]
        if kind == 3 and start >= rows // 2:
            ref, start = corner_b, start - rows // 2
        place = pl.multiple_of(order_ref[block] * shard, 16)
        left = 0
        for out in outs:
            width = out.shape[1]
            out[pl.ds(place, shard), :] = ref[start : start + shard, left : left + width]
            left += width


def split_three(value):
    high = value.astype(bf16)
    rest = value - widen(high)
    middle = rest.astype(bf16)
    return high, middle, (rest - widen(middle)).astype(bf16)


def two_parts(row):
    high = row.astype(bf16)
    return high, (row - widen(high)).astype(bf16)


def pack_stats(center, spread):
    lane = lax.broadcasted_iota(jnp.int32, (1, LANES), 1)
    packed = jnp.zeros((center.shape[0], LANES), f32)
    for at, part in enumerate(split_three(center) + split_three(spread)):
        packed = jnp.where(lane == at, widen(part), packed)
    return packed.astype(bf16)


def unpack_stats(packed):
    lane = lax.broadcasted_iota(jnp.int32, (1, LANES), 1)
    values = widen(packed)
    center = jnp.sum(jnp.where(lane < 3, values, 0.0), axis=-1, keepdims=True)
    spread = jnp.sum(jnp.where((lane >= 3) & (lane < 6), values, 0.0), axis=-1, keepdims=True)
    return center, spread


def joined_product(one, two, side_one, side_two, features):
    center_one, spread_one = unpack_stats(one[:, features:])
    center_two, spread_two = unpack_stats(two[:, features:])
    center = 0.5 * (center_one + center_two)
    apart = 0.5 * (center_one - center_two)
    inverse = lax.rsqrt(0.5 * (spread_one + spread_two) + apart * apart + epsilon)
    product = inverse * (
        widen(one[:, :features])
        + widen(two[:, :features])
        + apart * (side_one[0:1, :] - side_two[0:1, :])
    )
    return center, inverse, product


def centered_product(values, gain, weight):
    center = jnp.mean(values, axis=-1, keepdims=True)
    away = values - center
    spread = jnp.mean(away * away, axis=-1, keepdims=True)
    product = lax.dot_general(
        (away * gain).astype(bf16), weight, TRANSPOSED, preferred_element_type=f32
    )
    return product.astype(bf16), pack_stats(center, spread)


def side_rows(gain, offset, weight):
    gain_high, gain_low = two_parts(gain)
    offset_high, offset_low = two_parts(offset)
    filler = jnp.zeros((4, gain.shape[1]), bf16)
    stacked = jnp.concatenate([gain_high, gain_low, offset_high, offset_low, filler], 0)
    rows = lax.dot_general(stacked, weight, TRANSPOSED, preferred_element_type=f32)
    return jnp.concatenate(
        [rows[0:1] + rows[1:2], rows[2:3] + rows[3:4], jnp.zeros((6, rows.shape[1]), f32)], 0
    )


def accumulate(ref, row, values):
    total = jnp.sum(values, axis=0, keepdims=True)
    first = pl.program_id(0) == 0
    ref[row : row + 1, :] = jnp.where(first, total, ref[row : row + 1, :] + total)


def square_end(own, seconds, factor):
    rows = own[0].shape[0] // factor
    width = sum(each.shape[1] for each in own)

    def body(*refs):
        ins, outs = refs[: 2 * len(own)], refs[2 * len(own) :]
        for at, out in enumerate(outs):
            left = 0
            for mine, theirs in zip(ins[: len(own)], ins[len(own) :]):
                span = slice(at * rows, (at + 1) * rows)
                total = mine[span, :] + widen(theirs[span, :])
                out[:, left : left + mine.shape[1]] = total.astype(out.dtype)
                left += mine.shape[1]

    return pl.pallas_call(
        body,
        out_shape=[shape_of((rows, width), f32)] + [shape_of((rows, width), bf16)] * (factor - 1),
        in_specs=[pl.BlockSpec(memory_space=pltpu.VMEM)] * (2 * len(own)),
        out_specs=[pl.BlockSpec(memory_space=pltpu.VMEM)] * factor,
        name="square_end",
    )(*own, *seconds)


def pack(first_sums, first_other, model_sums, grad_sums, bias_sums, head_sums, hidden_sums):
    def body(first, other, model, grad, bias, head, hidden, out):
        at = 0
        rows = [first[0:1, :] + other[0:1, :], first[1:2, :] + other[1:2, :]]
        rows += [model[0:1, :], model[1:2, :], model[2:3, :], grad[0:1, :]]
        rows += [bias[0:1, :], bias[1:2, :], head[0:1, :], head[1:2, :]]
        rows += [hidden[0:1, :], hidden[1:2, :], hidden[2:3, :]]
        for row in rows:
            for left in range(0, row.shape[1], LANES):
                out[at : at + 1, :] = row[:, left : left + LANES]
                at += 1

    parts = (first_sums, first_other, model_sums, grad_sums, bias_sums, head_sums, hidden_sums)
    count = 6 * model_sums.shape[1] + 4 * head_sums.shape[1] + 3 * hidden_sums.shape[1]
    return pl.pallas_call(
        body,
        out_shape=shape_of((count // LANES, LANES), f32),
        in_specs=[pl.BlockSpec(memory_space=pltpu.VMEM)] * len(parts),
        out_specs=pl.BlockSpec(memory_space=pltpu.VMEM),
        name="pack",
    )(*parts)


def unpack(terms, shapes):
    def body(*refs):
        total = add_up([ref[...] for ref in refs[: len(terms)]])
        at = 0
        for out in refs[len(terms) :]:
            for row in range(out.shape[0]):
                for left in range(0, out.shape[1], LANES):
                    out[row : row + 1, left : left + LANES] = total[at : at + 1, :]
                    at += 1

    return pl.pallas_call(
        body,
        out_shape=[shape_of(shape, f32) for shape in shapes],
        in_specs=[pl.BlockSpec(memory_space=pltpu.VMEM)] * len(terms),
        out_specs=[pl.BlockSpec(memory_space=pltpu.VMEM)] * len(shapes),
        name="unpack",
    )(*terms)


def finish(groups, layout):
    sizes = [len(terms) for terms in groups]
    terms = [term for group in groups for term in group]
    rows = groups[0][0].shape[0]

    def body(*refs):
        ins, outs = refs[: len(terms)], refs[len(terms) :]
        for out, columns in zip(outs, layout):
            left = 0
            for group, start, width in columns:
                first = sum(sizes[:group])
                span = slice(start, start + width)
                out[:, left : left + width] = add_up(
                    [ref[:, span] for ref in ins[first : first + sizes[group]]]
                )
                left += width

    return pl.pallas_call(
        body,
        out_shape=[
            shape_of((rows, sum(width for _, _, width in columns)), f32) for columns in layout
        ],
        in_specs=[pl.BlockSpec(memory_space=pltpu.VMEM)] * len(terms),
        out_specs=[pl.BlockSpec(memory_space=pltpu.VMEM)] * len(layout),
        name="finish",
    )(*terms)


def prepare(core, tokens, tokens_other, cotangent, cotangent_other, model_vectors):
    rows, features = tokens.shape
    share = TILES // 2
    tile = rows // share

    def body(
        core_ref, x_own, x_other, g_own, g_other, model, inputs, grads, normal, turned, g_turned, sums
    ):
        here = pl.program_id(0) // share == core_ref[0]
        x = jnp.where(here, x_own[...], x_other[...])
        g = jnp.where(here, g_own[...], g_other[...])
        inputs[...] = x
        grads[...] = g
        n, _ = normal_of(widen(x))
        a = (n * model[0:1, :] + model[1:2, :]).astype(bf16)
        normal[...] = a
        turned[...] = a.T
        g_turned[...] = g.T
        accumulate(sums, 0, widen(g))

    own = pl.BlockSpec(
        (tile, features), lambda i, core: (jnp.clip(i - core[0] * share, 0, share - 1), 0)
    )
    other = pl.BlockSpec(
        (tile, features), lambda i, core: (jnp.clip(i - (1 - core[0]) * share, 0, share - 1), 0)
    )
    straight = pl.BlockSpec((tile, features), lambda i, core: (i, 0))
    across = pl.BlockSpec((features, tile), lambda i, core: (0, i))
    return pl.pallas_call(
        body,
        grid_spec=pltpu.PrefetchScalarGridSpec(
            num_scalar_prefetch=1,
            grid=(TILES,),
            in_specs=[own, other, own, other]
            + [pl.BlockSpec(model_vectors.shape, lambda i, core: (0, 0))],
            out_specs=[straight] * 3
            + [across] * 2
            + [pl.BlockSpec((8, features), lambda i, core: (0, 0))],
        ),
        out_shape=[shape_of((2 * rows, features), bf16)] * 3
        + [shape_of((features, 2 * rows), bf16)] * 2
        + [shape_of((8, features), f32)],
        compiler_params=PARAMS,
        cost_estimate=cost(20 * rows * features, 28 * rows * features),
        name="prepare",
    )(core, tokens, tokens_other, cotangent, cotangent_other, model_vectors)


def join(*parts):
    rows, width = parts[0].shape[0], sum(part.shape[1] for part in parts)

    def body(*refs):
        left = 0
        for ref in refs[:-1]:
            refs[-1][:, left : left + ref.shape[1]] = ref[...]
            left += ref.shape[1]

    return pl.pallas_call(
        body,
        out_shape=shape_of((rows, width), parts[0].dtype),
        in_specs=[pl.BlockSpec(memory_space=pltpu.VMEM)] * len(parts),
        out_specs=pl.BlockSpec(memory_space=pltpu.VMEM),
        name="join",
    )(*parts)


def project(order, pieces, attend_in, bias):
    length, features = attend_in.shape
    width = bias.shape[1]
    third = width // 3
    count = order.shape[0]

    def body(order_ref, *refs):
        pieces_in, (rows, bias_row, weight, *outs) = refs[:5], refs[5:]

        @pl.when(pl.program_id(0) == 0)
        def _():
            place_rows(order_ref, pieces_in, (weight,), count)

        states = jnp.dot(rows[...], weight[...], preferred_element_type=f32) + bias_row[...]
        for at, out in enumerate(outs):
            out[...] = states[:, at * third : (at + 1) * third].astype(bf16)

    return pl.pallas_call(
        body,
        grid=(TILES,),
        out_shape=[shape_of((features, width), bf16)] + [shape_of((length, third), bf16)] * 3,
        in_specs=[SMEM]
        + [whole(piece.shape) for piece in pieces]
        + [rows_of(attend_in), whole(bias.shape)],
        out_specs=[whole((features, width))]
        + [pl.BlockSpec((length // TILES, third), lambda i: (i, 0))] * 3,
        compiler_params=PARAMS,
        cost_estimate=cost(
            2 * length * features * width, 4 * features * width + 2 * length * (features + width)
        ),
        name="project",
    )(order, *pieces, attend_in, bias)


def attend_forward(pair, prefix, queries, keys, values):
    length = queries.shape[0]
    tile = length // 2

    def body(prefix_ref, query_ref, key_ref, value_ref, out_ref, log_ref, turned):
        turned[...] = value_ref[...].T
        first_half = lax.broadcasted_iota(jnp.int32, (1, PAIR), 1) < HEAD_DIM
        key_rows = key_ref[...]
        row_at = lax.broadcasted_iota(jnp.int32, (length, 1), 0)
        for start in range(0, length, tile):
            columns = slice(start, start + tile)
            places = lax.broadcasted_iota(jnp.int32, (1, tile), 1) + (start + 1)
            limit = jnp.maximum(places, prefix_ref[0])
            query_rows = query_ref[columns, :]
            parts = []
            for head in (0, 1):
                mine = jnp.where(
                    first_half == (head == 0), query_rows, jnp.zeros_like(query_rows)
                )
                scores = lax.dot_general(key_rows, mine, TRANSPOSED, preferred_element_type=f32)
                scores = jnp.where(row_at < limit, scores, masked)
                top = jnp.max(scores, axis=0, keepdims=True)
                raised = jnp.exp2((scores - top) * (SCALE * LOG2E))
                total = jnp.sum(raised, axis=0, keepdims=True)
                mixed = jnp.dot(
                    turned[head * HEAD_DIM : (head + 1) * HEAD_DIM, :],
                    raised.astype(bf16),
                    preferred_element_type=f32,
                )
                parts.append(mixed / total)
                log_ref[head : head + 1, columns] = top * (SCALE * LOG2E) + jnp.log2(total)
            out_ref[columns, :] = jnp.concatenate(parts, 0).T

    block = pl.BlockSpec((length, PAIR), lambda i: (0, pair))
    return pl.pallas_call(
        body,
        grid=(1,),
        out_shape=[shape_of((length, PAIR), f32), shape_of((8, length), f32)],
        in_specs=[SMEM, block, block, block],
        out_specs=[whole((length, PAIR)), whole((8, length))],
        scratch_shapes=[pltpu.VMEM((PAIR, length), bf16)],
        compiler_params=PARAMS,
        cost_estimate=cost(
            16 * length * length * PAIR, 10 * length * PAIR, 2 * length * length
        ),
        name="attend_forward",
    )(prefix, queries, keys, values)


def attend_backward(pair, prefix, queries, keys, values, attended, grads, logs):
    length = queries.shape[0]
    tile = length // 4

    def body(
        prefix_ref,
        query_ref,
        key_ref,
        value_ref,
        attended_ref,
        grad_ref,
        log_ref,
        query_out,
        key_out,
        value_out,
        turned,
        key_total,
        value_total,
    ):
        turned[...] = key_ref[...].T
        first_half = lax.broadcasted_iota(jnp.int32, (1, PAIR), 1) < HEAD_DIM
        key_rows, value_rows = key_ref[...], value_ref[...]
        row_at = lax.broadcasted_iota(jnp.int32, (length, 1), 0)
        for start in range(0, length, tile):
            columns = slice(start, start + tile)
            places = lax.broadcasted_iota(jnp.int32, (1, tile), 1) + (start + 1)
            limit = jnp.maximum(places, prefix_ref[0])
            query_rows, grad_rows = query_ref[columns, :], grad_ref[columns, :]
            crossed = (attended_ref[columns, :] * widen(grad_rows)).T
            parts = []
            key_part = value_part = 0.0
            for head in (0, 1):
                side = first_half == (head == 0)
                span = slice(head * HEAD_DIM, (head + 1) * HEAD_DIM)
                mine = jnp.where(side, query_rows, jnp.zeros_like(query_rows))
                grad = jnp.where(side, grad_rows, jnp.zeros_like(grad_rows))
                level = jnp.sum(crossed[span, :], axis=0, keepdims=True)
                scores = lax.dot_general(key_rows, mine, TRANSPOSED, preferred_element_type=f32)
                raised = jnp.exp2(
                    scores * (SCALE * LOG2E) - log_ref[head : head + 1, columns]
                )
                probs = jnp.where(row_at < limit, raised, 0.0)
                prob_grad = lax.dot_general(
                    value_rows, grad, TRANSPOSED, preferred_element_type=f32
                )
                score_grad = (probs * (prob_grad - level)).astype(bf16)
                value_part += jnp.dot(probs.astype(bf16), grad, preferred_element_type=f32)
                key_part += jnp.dot(score_grad, mine, preferred_element_type=f32)
                parts.append(jnp.dot(turned[span, :], score_grad, preferred_element_type=f32))
            query_out[columns, :] = (jnp.concatenate(parts, 0).T * SCALE).astype(bf16)
            if start == 0:
                key_total[...] = key_part
                value_total[...] = value_part
            else:
                key_total[...] += key_part
                value_total[...] += value_part
        key_out[...] = (key_total[...] * SCALE).astype(bf16)
        value_out[...] = value_total[...].astype(bf16)

    block = pl.BlockSpec((length, PAIR), lambda i: (0, pair))
    return pl.pallas_call(
        body,
        grid=(1,),
        out_shape=[shape_of((length, PAIR), bf16)] * 3,
        in_specs=[SMEM] + [block] * 3 + [whole((length, PAIR)), block, whole((8, length))],
        out_specs=[whole((length, PAIR))] * 3,
        scratch_shapes=[
            pltpu.VMEM((PAIR, length), bf16),
            pltpu.VMEM((length, PAIR), f32),
            pltpu.VMEM((length, PAIR), f32),
        ],
        compiler_params=PARAMS,
        cost_estimate=cost(
            40 * length * length * PAIR, 18 * length * PAIR, 2 * length * length
        ),
        name="attend_backward",
    )(prefix, queries, keys, values, attended, grads, logs)


def mix(order, pieces, attended, head_vectors, widths):
    length = attended[0].shape[0]
    width = PAIR * len(attended)
    count = order.shape[0]
    features = pieces[0].shape[0] // (count // 4) * count

    def body(order_ref, *refs):
        pieces_in, rows, (vectors, weight, second, product, side) = refs[:5], refs[5:-5], refs[-5:]

        @pl.when(pl.program_id(0) == 0)
        def _():
            place_rows(order_ref, pieces_in, (weight, second), count)
            side[...] = side_rows(vectors[2:3, :], vectors[3:4, :], weight[...])

        out, stats = centered_product(
            jnp.concatenate([part[...] for part in rows], 1), vectors[2:3, :], weight[...])
        product[:, :features] = out
        product[:, features:] = stats

    return pl.pallas_call(
        body,
        grid=(TILES,),
        out_shape=[shape_of((features, each), bf16) for each in widths]
        + [shape_of((length, features + LANES), bf16), shape_of((8, features), f32)],
        in_specs=[SMEM]
        + [whole(piece.shape) for piece in pieces]
        + [rows_of(part) for part in attended]
        + [whole(head_vectors.shape)],
        out_specs=[whole((features, each)) for each in widths]
        + [
            pl.BlockSpec((length // TILES, features + LANES), lambda i: (i, 0)),
            whole((8, features)),
        ],
        compiler_params=PARAMS,
        cost_estimate=cost(
            2 * length * features * width, 4 * features * sum(widths) + 6 * length * features
        ),
        name="mix",
    )(order, *pieces, *attended, head_vectors)


def feed_up(product, product_other, side, side_other, inputs, weight, model_vectors, hidden_vectors):
    length, features = inputs.shape
    width = weight.shape[1]

    def body(one, two, side_one, side_two, x, weight_ref, model, hidden, middle, turned, kept, slope):
        _, _, branch = joined_product(one[...], two[...], side_one, side_two, features)
        offset = side_one[1:2, :] + side_two[1:2, :] + model[2:3, :]
        total = widen(x[...]) + (branch + offset)
        middle[...] = total
        normal, _ = normal_of(total)
        feed = (normal * model[3:4, :] + model[4:5, :]).astype(bf16)
        turned[...] = feed.T
        before = jnp.dot(feed, weight_ref[...], preferred_element_type=f32) + hidden[0:1, :]
        share = 0.5 + 0.5 * lax.erf(before * 0.7071067811865476)
        kept[...] = (before * share).astype(bf16)
        slope[...] = (
            share + before * (0.3989422804014327 * jnp.exp(-0.5 * before * before))
        ).astype(bf16)

    return pl.pallas_call(
        body,
        grid=(TILES,),
        out_shape=[
            shape_of((length, features), f32),
            shape_of((features, length), bf16),
            shape_of((length, width), bf16),
            shape_of((length, width), bf16),
        ],
        in_specs=[
            rows_of(product),
            rows_of(product),
            whole(side.shape),
            whole(side.shape),
            rows_of(inputs),
            whole(weight.shape),
            whole(model_vectors.shape),
            whole(hidden_vectors.shape),
        ],
        out_specs=[
            rows_of(inputs),
            pl.BlockSpec((features, length // TILES), lambda i: (0, i)),
            pl.BlockSpec((length // TILES, width), lambda i: (i, 0)),
            pl.BlockSpec((length // TILES, width), lambda i: (i, 0)),
        ],
        compiler_params=PARAMS,
        cost_estimate=cost(
            2 * length * features * width,
            2 * features * width + 12 * length * features + 4 * length * width,
            2 * length * width,
        ),
        name="feed_up",
    )(product, product_other, side, side_other, inputs, weight, model_vectors, hidden_vectors)


def feed_down(order, pieces, kept, hidden_vectors):
    length, width = kept.shape
    count = order.shape[0]
    features = pieces[0].shape[0] // (count // 4) * count

    def body(order_ref, *refs):
        pieces_in, (rows, vectors, weight, product, side) = refs[:5], refs[5:]

        @pl.when(pl.program_id(0) == 0)
        def _():
            place_rows(order_ref, pieces_in, (weight,), count)
            side[...] = side_rows(vectors[1:2, :], vectors[2:3, :], weight[...])

        out, stats = centered_product(widen(rows[...]), vectors[1:2, :], weight[...])
        product[:, :features] = out
        product[:, features:] = stats

    return pl.pallas_call(
        body,
        grid=(TILES,),
        out_shape=[
            shape_of((features, width), bf16),
            shape_of((length, features + LANES), bf16),
            shape_of((8, features), f32),
        ],
        in_specs=[SMEM]
        + [whole(piece.shape) for piece in pieces]
        + [rows_of(kept), whole(hidden_vectors.shape)],
        out_specs=[
            whole((features, width)),
            pl.BlockSpec((length // TILES, features + LANES), lambda i: (i, 0)),
            whole((8, features)),
        ],
        compiler_params=PARAMS,
        cost_estimate=cost(
            2 * length * features * width, 4 * features * width + 2 * length * (features + width)
        ),
        name="feed_down",
    )(order, *pieces, kept, hidden_vectors)


def feed_back(
    core,
    product,
    product_other,
    side,
    side_other,
    middle,
    cotangent,
    kept,
    slope,
    down,
    up,
    model_vectors,
    hidden_vectors,
):
    length, features = middle.shape
    width = kept.shape[1]
    joined = 2 * width
    share = TILES // 2

    def body(
        core_ref, one, two, side_one, side_two, mid, grad, kept_ref, slope_ref, down_ref, up_ref,
        model, hidden, output, norm_out, before_out, product_out, sums,
    ):
        center, inverse, branch = joined_product(one[...], two[...], side_one, side_two, features)
        offset = side_one[1:2, :] + side_two[1:2, :] + model[5:6, :]

        @pl.when(pl.program_id(0) // share == core_ref[0])
        def _():
            output[...] = (mid[...] + (branch + offset)).astype(bf16)

        rows = widen(grad[...])
        straight = side_one[0:1, :] + side_two[0:1, :]
        mean_scaled = jnp.sum(rows * straight, axis=-1, keepdims=True) / joined
        mean_crossed = jnp.sum(rows * branch, axis=-1, keepdims=True) / joined
        mid_grad = jnp.dot(grad[...], down_ref[...], preferred_element_type=f32)
        normal = (widen(kept_ref[...]) - center) * inverse
        norm_out[...] = (normal * hidden[1:2, :] + hidden[2:3, :]).astype(bf16)
        accumulate(sums, 1, mid_grad * normal)
        accumulate(sums, 2, mid_grad)
        hidden_grad = inverse * (
            mid_grad * hidden[1:2, :] - mean_scaled - normal * mean_crossed
        )
        before = (hidden_grad * widen(slope_ref[...])).astype(bf16)
        before_out[...] = before
        accumulate(sums, 0, widen(before))
        product_out[...] = lax.dot_general(
            before, up_ref[...], TRANSPOSED, preferred_element_type=f32
        ).astype(bf16)

    tile = length // TILES

    def at_rows(columns):
        return pl.BlockSpec((tile, columns), lambda i, core: (i, 0))

    def fixed(array):
        return pl.BlockSpec(array.shape, lambda i, core: (0, 0))

    return pl.pallas_call(
        body,
        grid_spec=pltpu.PrefetchScalarGridSpec(
            num_scalar_prefetch=1,
            grid=(TILES,),
            in_specs=[
                at_rows(features + LANES),
                at_rows(features + LANES),
                fixed(side),
                fixed(side),
                at_rows(features),
                at_rows(features),
                at_rows(width),
                at_rows(width),
                fixed(down),
                fixed(up),
                fixed(model_vectors),
                fixed(hidden_vectors),
            ],
            out_specs=[
                pl.BlockSpec(
                    (tile, features), lambda i, core: (jnp.clip(i - core[0] * share, 0, share - 1), 0)
                ),
                at_rows(width),
                at_rows(width),
                at_rows(features),
                pl.BlockSpec((8, width), lambda i, core: (0, 0)),
            ],
        ),
        out_shape=[
            shape_of((length // 2, features), bf16),
            shape_of((length, width), bf16),
            shape_of((length, width), bf16),
            shape_of((length, features), bf16),
            shape_of((8, width), f32),
        ],
        compiler_params=PARAMS,
        cost_estimate=cost(
            4 * length * features * width,
            4 * features * width + 12 * length * features + 8 * length * width,
        ),
        name="feed_back",
    )(
        core,
        product,
        product_other,
        side,
        side_other,
        middle,
        cotangent,
        kept,
        slope,
        down,
        up,
        model_vectors,
        hidden_vectors,
    )


def mix_back(
    passed,
    passed_other,
    product,
    product_other,
    side,
    side_other,
    middle,
    cotangent,
    attended,
    weight,
    model_vectors,
    head_vectors,
):
    length, features = middle.shape
    width = PAIR * len(attended)
    joined = 2 * width

    def body(
        back_one, back_two, one, two, side_one, side_two, mid, grad, *refs
    ):
        attended_refs, (weight_ref, model, head, middle_out, turned, mixed_out, attended_out, sums, head_sums) = refs[:-9], refs[-9:]
        feed_grad = widen(back_one[...]) + widen(back_two[...])
        normal, inverse = normal_of(mid[...])
        accumulate(sums, 1, feed_grad * normal)
        accumulate(sums, 2, feed_grad)
        middle_grad = widen(grad[...]) + normal_back(feed_grad * model[3:4, :], normal, inverse)
        middle_out[...] = middle_grad
        branch_grad = middle_grad.astype(bf16)
        rows = widen(branch_grad)
        accumulate(sums, 0, rows)
        turned[...] = branch_grad.T
        center, inverse_two, branch = joined_product(
            one[...], two[...], side_one, side_two, features
        )
        straight = side_one[0:1, :] + side_two[0:1, :]
        mean_scaled = jnp.sum(rows * straight, axis=-1, keepdims=True) / joined
        mean_crossed = jnp.sum(rows * branch, axis=-1, keepdims=True) / joined
        mixed_grad = jnp.dot(branch_grad, weight_ref[...], preferred_element_type=f32)
        attended_rows = jnp.concatenate([part[...] for part in attended_refs], 1)
        normal_two = (attended_rows - center) * inverse_two
        mixed_out[...] = (normal_two * head[2:3, :] + head[3:4, :]).astype(bf16)
        accumulate(head_sums, 0, mixed_grad * normal_two)
        accumulate(head_sums, 1, mixed_grad)
        attended_out[...] = (
            inverse_two * (mixed_grad * head[2:3, :] - mean_scaled - normal_two * mean_crossed)
        ).astype(bf16)

    tile = length // TILES
    return pl.pallas_call(
        body,
        grid=(TILES,),
        out_shape=[
            shape_of((length, features), f32),
            shape_of((features, length), bf16),
            shape_of((length, width), bf16),
            shape_of((length, width), bf16),
            shape_of((8, features), f32),
            shape_of((8, width), f32),
        ],
        in_specs=[
            rows_of(passed),
            rows_of(passed),
            rows_of(product),
            rows_of(product),
            whole(side.shape),
            whole(side.shape),
            rows_of(middle),
            rows_of(cotangent),
            *[rows_of(part) for part in attended],
            whole(weight.shape),
            whole(model_vectors.shape),
            whole(head_vectors.shape),
        ],
        out_specs=[
            rows_of(middle),
            pl.BlockSpec((features, tile), lambda i: (0, i)),
            pl.BlockSpec((tile, width), lambda i: (i, 0)),
            pl.BlockSpec((tile, width), lambda i: (i, 0)),
            whole((8, features)),
            whole((8, width)),
        ],
        compiler_params=PARAMS,
        cost_estimate=cost(
            2 * length * features * width, 2 * features * width + 24 * length * features
        ),
        name="mix_back",
    )(
        passed,
        passed_other,
        product,
        product_other,
        side,
        side_other,
        middle,
        cotangent,
        *attended,
        weight,
        model_vectors,
        head_vectors,
    )


def project_back(core, groups, weight):
    length = groups[0][0].shape[0]
    parts = [part for group in groups for part in group]
    features, width = weight.shape
    third = width // 3
    tile = length // TILES
    share = TILES // 2
    each = len(groups[0])

    def body(core_ref, *refs):
        weight_ref, send, keep, sums = refs[-4:]
        grads = [
            jnp.concatenate([ref[...] for ref in refs[at * each : (at + 1) * each]], 1)
            for at in range(3)
        ]
        total = lax.dot_general(
            jnp.concatenate(grads, 1), weight_ref[...], TRANSPOSED, preferred_element_type=f32
        )
        accumulate(sums, 0, widen(grads[0]))
        accumulate(sums, 1, widen(grads[2]))

        @pl.when(pl.program_id(0) < share)
        def _():
            send[...] = total.astype(bf16)

        @pl.when(pl.program_id(0) >= share)
        def _():
            keep[...] = total

    moved = pl.BlockSpec((tile, PAIR), lambda i, core: ((i + (1 - core[0]) * share) % TILES, 0))
    return pl.pallas_call(
        body,
        grid_spec=pltpu.PrefetchScalarGridSpec(
            num_scalar_prefetch=1,
            grid=(TILES,),
            in_specs=[moved] * len(parts) + [pl.BlockSpec(weight.shape, lambda i, core: (0, 0))],
            out_specs=[
                pl.BlockSpec((tile, features), lambda i, core: (jnp.minimum(i, share - 1), 0)),
                pl.BlockSpec((tile, features), lambda i, core: (jnp.maximum(i - share, 0), 0)),
                pl.BlockSpec((8, third), lambda i, core: (0, 0)),
            ],
        ),
        out_shape=[
            shape_of((length // 2, features), bf16),
            shape_of((length // 2, features), f32),
            shape_of((8, third), f32),
        ],
        compiler_params=PARAMS,
        cost_estimate=cost(
            2 * length * features * width, 2 * features * width + 6 * length * (features + third)
        ),
        name="project_back",
    )(core, *parts, weight)


def input_back(core, received, kept, middle_grad, tokens, model_vectors):
    rows, features = tokens.shape
    tiles = TILES // 2
    tile = rows // tiles

    def body(core_ref, got, own, mid, x, model, out, sums):
        grad = widen(got[...]) + own[...]
        normal, inverse = normal_of(widen(x[...]))
        accumulate(sums, 0, grad * normal)
        accumulate(sums, 1, grad)
        out[...] = mid[...] + normal_back(grad * model[0:1, :], normal, inverse)

    near = pl.BlockSpec((tile, features), lambda i, core: (i, 0))
    return pl.pallas_call(
        body,
        grid_spec=pltpu.PrefetchScalarGridSpec(
            num_scalar_prefetch=1,
            grid=(tiles,),
            in_specs=[
                near,
                near,
                pl.BlockSpec((tile, features), lambda i, core: (i + core[0] * tiles, 0)),
                near,
                pl.BlockSpec(model_vectors.shape, lambda i, core: (0, 0)),
            ],
            out_specs=[near, pl.BlockSpec((8, features), lambda i, core: (0, 0))],
        ),
        out_shape=[shape_of((rows, features), f32), shape_of((8, features), f32)],
        compiler_params=PARAMS,
        cost_estimate=cost(10 * rows * features, 16 * rows * features),
        name="input_back",
    )(core, received, kept, middle_grad, tokens, model_vectors)


def weight_grad(order, pairs, tile):
    features, tokens = pairs[0][0].shape
    lefts, groups = [], []
    for left, group in pairs:
        if not any(left is known for known in lefts):
            lefts.append(left)
        groups.append(([left is known for known in lefts].index(True), len(group)))
    rights = [right for _, group in pairs for right in group]
    width = sum(right.shape[1] for right in rights)
    count = order.shape[0]
    shard = features // count
    single = len(rights) == 1

    def body(order_ref, *refs):
        left_refs, right_refs = refs[: len(lefts)], refs[len(lefts) : -3]
        keep, send, total = refs[-3:]
        if single:
            total[...] = jnp.dot(left_refs[0][...], right_refs[0][...], preferred_element_type=f32)
        else:
            first = 0
            for step, (at, size) in enumerate(groups):

                @pl.when(pl.program_id(0) == step)
                def _(at=at, first=first, size=size):
                    right = [ref[...] for ref in right_refs[first : first + size]]
                    total[...] = jnp.dot(
                        left_refs[at][...],
                        jnp.concatenate(right, 1) if size > 1 else right[0],
                        preferred_element_type=f32,
                    )

                first += size

        for block in range(count):
            place = pl.multiple_of(order_ref[block] * shard, 16)
            out, at = (keep, block) if block < count // 2 else (send, block - count // 2)
            out[at * shard : (at + 1) * shard, :] = total[pl.ds(place, shard), :].astype(bf16)

    return pl.pallas_call(
        body,
        grid=(width // tile,),
        out_shape=[shape_of((features // 2, width), bf16)] * 2,
        in_specs=[SMEM]
        + [whole(left.shape) for left in lefts]
        + (
            [pl.BlockSpec((tokens, tile), lambda i: (0, i))]
            if single
            else [whole(right.shape) for right in rights]
        ),
        out_specs=[pl.BlockSpec((features // 2, tile), lambda i: (0, i))] * 2,
        scratch_shapes=[pltpu.VMEM((features, tile), f32)],
        compiler_params=PARAMS,
        cost_estimate=cost(
            2 * tokens * features * width,
            2 * (tokens * (features + width) + features * width),
        ),
        name="weight_grad",
    )(order, *lefts, *rights)


def on_device(
    tokens,
    cotangent,
    prefix,
    query_weight,
    key_weight,
    value_weight,
    out_weight,
    up_weight,
    down_weight,
    model_vectors,
    head_vectors,
    hidden_vectors,
):
    ring = Ring(lax.axis_size("dp"))
    order = ring.gather_order()
    near, far = ring.scatter_order(1), ring.scatter_order(2)
    core = lax.axis_index("tensor").astype(jnp.int32)[None]
    half, full = query_weight.shape[1], up_weight.shape[1]
    features = tokens.shape[1]

    bias = jnp.concatenate([head_vectors[0], jnp.zeros_like(head_vectors[0]), head_vectors[1]])
    pair_count = half // PAIR
    tokens_other, cotangent_other = flip_partner(tokens), flip_partner(cotangent)
    first = join(query_weight, key_weight, value_weight)
    first_got = ring.start_gather(first)
    inputs, grads, attend_in, attend_turned, grads_turned, grad_sums = prepare(
        core, tokens, tokens_other, cotangent, cotangent_other, model_vectors
    )
    first_block = ring.end_gather(first, after(first_got, attend_in))
    first_sides = ring.to_sides(first_block)
    second = after(join(out_weight, up_weight), first_block)
    second_got = ring.start_gather(second)
    first_pieces = (first_block, *first_sides, *ring.to_corner(*first_sides))
    first_weight, queries, keys, values = project(
        order, first_pieces, attend_in, bias[None]
    )
    states = (prefix, queries, keys, values)
    second_block = ring.end_gather(second, after(second_got, queries))
    second_sides = ring.to_sides(second_block)
    third = after(down_weight, second_block)
    third_got = ring.start_gather(third)
    attended, logs = [], []
    for pair in range(pair_count):
        out, log = attend_forward(pair, *states)
        attended.append(out)
        logs.append(log)
        states = after(states, out, third_got[0], third_got[-1])
        if pair == pair_count - 2:
            second_sides = after(second_sides, out)
            second_corner = ring.to_corner(*second_sides)
            states = after(states, second_sides, third_got)
    second_pieces = (second_block, *second_sides, *after(second_corner, attended[-1]))
    third_block = ring.end_gather(third, after(third_got, second_corner, attended[-1]))
    third_sides = ring.to_sides(third_block)
    out_full, up_full, mixed, mixed_side = mix(
        order, second_pieces, after(attended, third_block), head_vectors, (half, full)
    )
    mixed, mixed_side, third_sides = after((mixed, mixed_side, third_sides), mixed)
    mixed_other, mixed_side_other = flip_partner(mixed), flip_partner(mixed_side)
    third_corner = ring.to_corner(*third_sides)
    middle, feed_turned, kept, slope = feed_up(
        mixed,
        mixed_other,
        mixed_side,
        mixed_side_other,
        inputs,
        up_full,
        model_vectors,
        hidden_vectors,
    )
    third_pieces = (third_block, *third_sides, *after(third_corner, kept))
    down_full, fed, fed_side = feed_down(order, third_pieces, kept, hidden_vectors)
    fed_other, fed_side_other = flip_partner(fed), flip_partner(fed_side)
    output, feed_mid, before_grad, passed, hidden_sums = feed_back(
        core,
        fed,
        fed_other,
        fed_side,
        fed_side_other,
        middle,
        grads,
        kept,
        slope,
        down_full,
        up_full,
        model_vectors,
        hidden_vectors,
    )
    passed_other = flip_partner(passed)
    down_keep, down_send = weight_grad(far, [(grads_turned, [feed_mid])], full // 2)
    up_keep, up_send = weight_grad(near, [(feed_turned, [before_grad])], full // 2)
    down_got, up_got = ring.flip(down_send, 2), ring.flip(up_send, 1)

    middle_grad, branch_turned, mixed_in, attended_grad, model_sums, head_sums = mix_back(
        passed,
        passed_other,
        mixed,
        mixed_other,
        mixed_side,
        mixed_side_other,
        middle,
        grads,
        attended,
        out_full,
        model_vectors,
        head_vectors,
    )

    def pair_back(pair, grad):
        return attend_backward(pair, *states, attended[pair], grad, logs[pair])

    last_pair = pair_count - 1
    pair_grads = [pair_back(pair, attended_grad) for pair in range(last_pair)]
    down_own, down_away = ring.sum_first(down_keep, after(down_got, pair_grads))
    up_own, up_away = ring.sum_first(up_keep, after(up_got, pair_grads))
    up_second, down_second = ring.flip(up_away, 2), ring.flip(down_away, 1)
    early_grads = after(pair_grads, down_away, up_away)
    early_keep, early_send = weight_grad(
        near,
        [(attend_turned, [pair[at] for pair in early_grads]) for at in range(3)],
        last_pair * PAIR,
    )
    early_got = ring.flip(early_send, 1)
    out_keep, out_send = weight_grad(
        far, [(branch_turned, [after(mixed_in, early_send)])], half
    )
    out_got = ring.flip(out_send, 2)
    pair_grads.append(pair_back(last_pair, after(attended_grad, out_send)))
    query_grad, key_grad, value_grad = ([pair[at] for pair in pair_grads] for at in range(3))
    wide_parts = square_end(
        (up_own, down_own), after((up_second, down_second), pair_grads), ring.lines[0][0]
    )
    wide_got = ring.start_lines(wide_parts)
    send, keep, bias_sums = project_back(
        core, after((query_grad, key_grad, value_grad), wide_parts), first_weight
    )
    received = flip_partner(send)
    late_keep, late_send = weight_grad(
        near, [(attend_turned, after(list(pair_grads[last_pair]), send))], 3 * PAIR
    )
    late_got = ring.flip(late_send, 1)
    early_got, out_got = after((early_got, out_got), late_send, wide_got[0], wide_got[-1])
    early_own, early_away = ring.sum_first(early_keep, early_got)
    out_own, out_away = ring.sum_first(out_keep, out_got)
    early_second, out_second = ring.flip(early_away, 2), ring.flip(out_away, 1)
    input_grad, first_sums = input_back(
        core, received, after(keep, early_away, out_away), middle_grad, tokens, model_vectors
    )
    late_own, late_away = ring.sum_first(late_keep, after(late_got, input_grad))
    late_second = ring.flip(late_away, 2)
    packed = pack(
        first_sums, flip_partner(first_sums), model_sums, grad_sums, bias_sums, head_sums, hidden_sums
    )
    for factor, stride in [*ring.lines[1:][::-1], ring.lines[0]]:
        packed = add_up([packed, *ring.around(packed, factor, stride)])
    model_sum, head_sum, hidden_sum = unpack(
        [packed, *ring.around_square(packed)], ((6, features), (4, half), (3, full))
    )
    early_parts = square_end(
        (early_own, out_own),
        after((early_second, out_second), input_grad),
        ring.lines[0][0],
    )
    early_got = ring.start_lines(early_parts)
    late_parts = square_end((late_own,), (late_second,), ring.lines[0][0])
    late_got = ring.start_lines(late_parts)
    wide_terms = ring.last_terms(wide_parts, wide_got)
    early_terms = ring.last_terms(early_parts, early_got)
    late_terms = ring.last_terms(late_parts, late_got)
    up_grad, down_grad = finish([wide_terms], [[(0, 0, full)], [(0, full, full)]])
    early = last_pair * PAIR
    query_weight_grad, key_weight_grad, value_weight_grad, out_grad = finish(
        [early_terms, late_terms],
        [[(0, at * early, early), (1, at * PAIR, PAIR)] for at in range(3)]
        + [[(0, 3 * early, half)]],
    )
    return (
        output,
        input_grad,
        query_weight_grad,
        key_weight_grad,
        value_weight_grad,
        out_grad,
        up_grad,
        down_grad,
        model_sum,
        head_sum,
        hidden_sum,
    )


def solution(mesh):
    return jax.shard_map(
        on_device,
        mesh=mesh,
        in_specs=(
            P(("dp", "tensor"), None),
            P(("dp", "tensor"), None),
            P("dp"),
            P("dp", "tensor"),
            P("dp", "tensor"),
            P("dp", "tensor"),
            P("dp", "tensor"),
            P("dp", "tensor"),
            P("dp", "tensor"),
            P(),
            P(None, "tensor"),
            P(None, "tensor"),
        ),
        out_specs=(
            P(("dp", "tensor"), None),
            P(("dp", "tensor"), None),
            P("dp", "tensor"),
            P("dp", "tensor"),
            P("dp", "tensor"),
            P("dp", "tensor"),
            P("dp", "tensor"),
            P("dp", "tensor"),
            P(),
            P(None, "tensor"),
            P(None, "tensor"),
        ),
        check_vma=False,
    )
```

```python
import jax
import jax.numpy as jnp
from jax import lax
from jax.experimental import pallas as pl
from jax.experimental.pallas import tpu as pltpu
from jax.sharding import PartitionSpec as P

HEAD_DIM = 64
PAIR = 2 * HEAD_DIM
LANES = 128
TILES = 4
SCALE = 0.125
LOG2E = 1.4426950408889634
WEIGHT = 4

epsilon = 1e-05
masked = -1e30

f32 = jnp.float32
bf16 = jnp.bfloat16
TRANSPOSED = (((1,), (1,)), ((), ()))
SMEM = pl.BlockSpec(memory_space=pltpu.SMEM)


def flip_partner(values):
    return lax.ppermute(values, "tensor", [(0, 1), (1, 0)])


def normal_of(values):
    center = jnp.mean(values, axis=-1, keepdims=True)
    spread = jnp.mean(values * values, axis=-1, keepdims=True) - center * center
    inverse = lax.rsqrt(spread + epsilon)
    return (values - center) * inverse, inverse


def normal_back(scaled, normal, inverse):
    return inverse * (
        scaled
        - jnp.mean(scaled, axis=-1, keepdims=True)
        - normal * jnp.mean(scaled * normal, axis=-1, keepdims=True)
    )


def widen(values):
    return values.astype(f32)


def after(values, *earlier):
    return lax.optimization_barrier((values, earlier))[0]


class Ring:
    def __init__(self, size):
        self.size = size
        rest, stride = size // 4, 4
        self.lines = []
        while rest > 1:
            factor = 4 if rest % 4 == 0 else 2 if rest % 2 == 0 else rest
            self.lines.append((factor, stride))
            rest, stride = rest // factor, stride * factor
        self.line_count = size // 4

    def shift(self, values, factor, stride, step):
        pairs = []
        for place in range(self.size):
            digit = place // stride % factor
            pairs.append((place, place + ((digit + step) % factor - digit) * stride))
        return lax.ppermute(values, "dp", pairs)

    def flip(self, values, stride):
        return self.shift(values, 2, stride, 1)

    def line_places(self, sign):
        own = lax.axis_index("dp")
        places = [jnp.int32(0)]
        for factor, stride in self.lines:
            digit = own // stride % factor
            places = [
                base + (digit + sign * step) % factor * stride
                for base in places
                for step in range(factor)
            ]
        return places

    def gather_order(self):
        own = lax.axis_index("dp")
        places = self.line_places_gather()
        return jnp.stack([base + (own % 4 ^ bits) for bits in (0, 1, 2, 3) for base in places])

    def line_places_gather(self):
        own = lax.axis_index("dp")
        places = [jnp.int32(0)]
        for factor, stride in self.lines:
            digit = own // stride % factor
            places = [
                base + (digit + factor - step) % factor * stride
                for step in range(factor)
                for base in places
            ]
        return places

    def start_gather(self, values):
        factor, stride = self.lines[0]
        return [self.shift(values, factor, stride, step) for step in range(1, factor)]

    def end_gather(self, values, got):
        block = jnp.concatenate([values, *got], 0)
        for factor, stride in self.lines[1:]:
            block = jnp.concatenate(
                [block] + [self.shift(block, factor, stride, step) for step in range(1, factor)], 0
            )
        return block

    def to_sides(self, block):
        return self.flip(block, 1), self.flip(block, 2)

    def to_corner(self, from_x, from_y):
        half = from_x.shape[0] // 2
        return self.flip(from_x[:half], 2), self.flip(from_y[half:], 1)

    def scatter_order(self, first_bit):
        own = lax.axis_index("dp")
        other_bit = 3 - first_bit
        places = self.line_places(1)
        return jnp.stack(
            [
                base + (own % 4 ^ (cross + side))
                for cross in (0, first_bit)
                for side in (0, other_bit)
                for base in places
            ]
        )

    def sum_first(self, keep, got):
        half = keep.shape[0] // 2
        own = widen(keep[:half]) + widen(got[:half])
        return own, (widen(keep[half:]) + widen(got[half:])).astype(bf16)

    def start_lines(self, parts):
        factor, stride = self.lines[0]
        return [self.shift(parts[step], factor, stride, step) for step in range(1, factor)]

    def last_terms(self, parts, got):
        terms = [parts[0], *got]
        for factor, stride in self.lines[1:]:
            total = add_up(terms)
            pieces = jnp.split(total, factor)
            terms = [pieces[0]] + [
                self.shift(pieces[step].astype(bf16), factor, stride, step)
                for step in range(1, factor)
            ]
        return terms

    def around(self, values, factor, stride):
        return [self.shift(values, factor, stride, step) for step in range(1, factor)]

    def around_square(self, values):
        pairs = [(place, place ^ 3) for place in range(self.size)]
        return [self.flip(values, 1), self.flip(values, 2), lax.ppermute(values, "dp", pairs)]


def add_up(terms):
    total = widen(terms[0])
    for term in terms[1:]:
        total = total + widen(term)
    return total


def whole(shape):
    return pl.BlockSpec(shape, lambda i: (0,) * len(shape))


def rows_of(array, tiles=TILES):
    return pl.BlockSpec((array.shape[0] // tiles, array.shape[1]), lambda i: (i, 0))


def shape_of(shape, dtype):
    return jax.ShapeDtypeStruct(shape, dtype)


def cost(flops, moved, exponentials=0):
    return pl.CostEstimate(flops=WEIGHT * flops, bytes_accessed=moved, transcendentals=exponentials)


PARAMS = pltpu.CompilerParams(vmem_limit_bytes=60 * 2**20)


def place_rows(order_ref, pieces, outs, count):
    own, from_x, from_y, corner_a, corner_b = pieces
    rows = own.shape[0]
    shard = rows // (count // 4)
    for block in range(count):
        kind, inner = divmod(block, count // 4)
        start = inner * shard
        ref = (own, from_x, from_y, corner_a)[kind]
        if kind == 3 and start >= rows // 2:
            ref, start = corner_b, start - rows // 2
        place = pl.multiple_of(order_ref[block] * shard, 16)
        left = 0
        for out in outs:
            width = out.shape[1]
            out[pl.ds(place, shard), :] = ref[start : start + shard, left : left + width]
            left += width


def split_three(value):
    high = value.astype(bf16)
    rest = value - widen(high)
    middle = rest.astype(bf16)
    return high, middle, (rest - widen(middle)).astype(bf16)


def two_parts(row):
    high = row.astype(bf16)
    return high, (row - widen(high)).astype(bf16)


def pack_stats(center, spread):
    lane = lax.broadcasted_iota(jnp.int32, (1, LANES), 1)
    packed = jnp.zeros((center.shape[0], LANES), f32)
    for at, part in enumerate(split_three(center) + split_three(spread)):
        packed = jnp.where(lane == at, widen(part), packed)
    return packed.astype(bf16)


def unpack_stats(packed):
    lane = lax.broadcasted_iota(jnp.int32, (1, LANES), 1)
    values = widen(packed)
    center = jnp.sum(jnp.where(lane < 3, values, 0.0), axis=-1, keepdims=True)
    spread = jnp.sum(jnp.where((lane >= 3) & (lane < 6), values, 0.0), axis=-1, keepdims=True)
    return center, spread


def joined_product(one, two, side_one, side_two, features):
    center_one, spread_one = unpack_stats(one[:, features:])
    center_two, spread_two = unpack_stats(two[:, features:])
    center = 0.5 * (center_one + center_two)
    apart = 0.5 * (center_one - center_two)
    inverse = lax.rsqrt(0.5 * (spread_one + spread_two) + apart * apart + epsilon)
    product = inverse * (
        widen(one[:, :features])
        + widen(two[:, :features])
        + apart * (side_one[0:1, :] - side_two[0:1, :])
    )
    return center, inverse, product


def centered_product(values, gain, weight):
    center = jnp.mean(values, axis=-1, keepdims=True)
    away = values - center
    spread = jnp.mean(away * away, axis=-1, keepdims=True)
    product = lax.dot_general(
        (away * gain).astype(bf16), weight, TRANSPOSED, preferred_element_type=f32
    )
    return product.astype(bf16), pack_stats(center, spread)


def side_rows(gain, offset, weight):
    gain_high, gain_low = two_parts(gain)
    offset_high, offset_low = two_parts(offset)
    filler = jnp.zeros((4, gain.shape[1]), bf16)
    stacked = jnp.concatenate([gain_high, gain_low, offset_high, offset_low, filler], 0)
    rows = lax.dot_general(stacked, weight, TRANSPOSED, preferred_element_type=f32)
    return jnp.concatenate(
        [rows[0:1] + rows[1:2], rows[2:3] + rows[3:4], jnp.zeros((6, rows.shape[1]), f32)], 0
    )


def accumulate(ref, row, values):
    total = jnp.sum(values, axis=0, keepdims=True)
    first = pl.program_id(0) == 0
    ref[row : row + 1, :] = jnp.where(first, total, ref[row : row + 1, :] + total)


def square_end(own, seconds, factor):
    rows = own[0].shape[0] // factor
    width = sum(each.shape[1] for each in own)

    def body(*refs):
        ins, outs = refs[: 2 * len(own)], refs[2 * len(own) :]
        for at, out in enumerate(outs):
            left = 0
            for mine, theirs in zip(ins[: len(own)], ins[len(own) :]):
                span = slice(at * rows, (at + 1) * rows)
                total = mine[span, :] + widen(theirs[span, :])
                out[:, left : left + mine.shape[1]] = total.astype(out.dtype)
                left += mine.shape[1]

    return pl.pallas_call(
        body,
        out_shape=[shape_of((rows, width), f32)] + [shape_of((rows, width), bf16)] * (factor - 1),
        in_specs=[pl.BlockSpec(memory_space=pltpu.VMEM)] * (2 * len(own)),
        out_specs=[pl.BlockSpec(memory_space=pltpu.VMEM)] * factor,
        name="square_end",
    )(*own, *seconds)


def pack(first_sums, first_other, model_sums, grad_sums, bias_sums, head_sums, hidden_sums):
    def body(first, other, model, grad, bias, head, hidden, out):
        at = 0
        rows = [first[0:1, :] + other[0:1, :], first[1:2, :] + other[1:2, :]]
        rows += [model[0:1, :], model[1:2, :], model[2:3, :], grad[0:1, :]]
        rows += [bias[0:1, :], bias[1:2, :], head[0:1, :], head[1:2, :]]
        rows += [hidden[0:1, :], hidden[1:2, :], hidden[2:3, :]]
        for row in rows:
            for left in range(0, row.shape[1], LANES):
                out[at : at + 1, :] = row[:, left : left + LANES]
                at += 1

    parts = (first_sums, first_other, model_sums, grad_sums, bias_sums, head_sums, hidden_sums)
    count = 6 * model_sums.shape[1] + 4 * head_sums.shape[1] + 3 * hidden_sums.shape[1]
    return pl.pallas_call(
        body,
        out_shape=shape_of((count // LANES, LANES), f32),
        in_specs=[pl.BlockSpec(memory_space=pltpu.VMEM)] * len(parts),
        out_specs=pl.BlockSpec(memory_space=pltpu.VMEM),
        name="pack",
    )(*parts)


def unpack(terms, shapes):
    def body(*refs):
        total = add_up([ref[...] for ref in refs[: len(terms)]])
        at = 0
        for out in refs[len(terms) :]:
            for row in range(out.shape[0]):
                for left in range(0, out.shape[1], LANES):
                    out[row : row + 1, left : left + LANES] = total[at : at + 1, :]
                    at += 1

    return pl.pallas_call(
        body,
        out_shape=[shape_of(shape, f32) for shape in shapes],
        in_specs=[pl.BlockSpec(memory_space=pltpu.VMEM)] * len(terms),
        out_specs=[pl.BlockSpec(memory_space=pltpu.VMEM)] * len(shapes),
        name="unpack",
    )(*terms)


def finish(groups, layout):
    sizes = [len(terms) for terms in groups]
    terms = [term for group in groups for term in group]
    rows = groups[0][0].shape[0]

    def body(*refs):
        ins, outs = refs[: len(terms)], refs[len(terms) :]
        for out, columns in zip(outs, layout):
            left = 0
            for group, start, width in columns:
                first = sum(sizes[:group])
                span = slice(start, start + width)
                out[:, left : left + width] = add_up(
                    [ref[:, span] for ref in ins[first : first + sizes[group]]]
                )
                left += width

    return pl.pallas_call(
        body,
        out_shape=[
            shape_of((rows, sum(width for _, _, width in columns)), f32) for columns in layout
        ],
        in_specs=[pl.BlockSpec(memory_space=pltpu.VMEM)] * len(terms),
        out_specs=[pl.BlockSpec(memory_space=pltpu.VMEM)] * len(layout),
        name="finish",
    )(*terms)


def prepare(core, tokens, tokens_other, cotangent, cotangent_other, model_vectors):
    rows, features = tokens.shape
    share = TILES // 2
    tile = rows // share

    def body(
        core_ref, x_own, x_other, g_own, g_other, model, inputs, grads, normal, turned, g_turned, sums
    ):
        here = pl.program_id(0) // share == core_ref[0]
        x = jnp.where(here, x_own[...], x_other[...])
        g = jnp.where(here, g_own[...], g_other[...])
        inputs[...] = x
        grads[...] = g
        n, _ = normal_of(widen(x))
        a = (n * model[0:1, :] + model[1:2, :]).astype(bf16)
        normal[...] = a
        turned[...] = a.T
        g_turned[...] = g.T
        accumulate(sums, 0, widen(g))

    own = pl.BlockSpec(
        (tile, features), lambda i, core: (jnp.clip(i - core[0] * share, 0, share - 1), 0)
    )
    other = pl.BlockSpec(
        (tile, features), lambda i, core: (jnp.clip(i - (1 - core[0]) * share, 0, share - 1), 0)
    )
    straight = pl.BlockSpec((tile, features), lambda i, core: (i, 0))
    across = pl.BlockSpec((features, tile), lambda i, core: (0, i))
    return pl.pallas_call(
        body,
        grid_spec=pltpu.PrefetchScalarGridSpec(
            num_scalar_prefetch=1,
            grid=(TILES,),
            in_specs=[own, other, own, other]
            + [pl.BlockSpec(model_vectors.shape, lambda i, core: (0, 0))],
            out_specs=[straight] * 3
            + [across] * 2
            + [pl.BlockSpec((8, features), lambda i, core: (0, 0))],
        ),
        out_shape=[shape_of((2 * rows, features), bf16)] * 3
        + [shape_of((features, 2 * rows), bf16)] * 2
        + [shape_of((8, features), f32)],
        compiler_params=PARAMS,
        cost_estimate=cost(20 * rows * features, 28 * rows * features),
        name="prepare",
    )(core, tokens, tokens_other, cotangent, cotangent_other, model_vectors)


def join(*parts):
    rows, width = parts[0].shape[0], sum(part.shape[1] for part in parts)

    def body(*refs):
        left = 0
        for ref in refs[:-1]:
            refs[-1][:, left : left + ref.shape[1]] = ref[...]
            left += ref.shape[1]

    return pl.pallas_call(
        body,
        out_shape=shape_of((rows, width), parts[0].dtype),
        in_specs=[pl.BlockSpec(memory_space=pltpu.VMEM)] * len(parts),
        out_specs=pl.BlockSpec(memory_space=pltpu.VMEM),
        name="join",
    )(*parts)


def project(order, pieces, attend_in, bias):
    length, features = attend_in.shape
    width = bias.shape[1]
    third = width // 3
    count = order.shape[0]

    def body(order_ref, *refs):
        pieces_in, (rows, bias_row, weight, *outs) = refs[:5], refs[5:]

        @pl.when(pl.program_id(0) == 0)
        def _():
            place_rows(order_ref, pieces_in, (weight,), count)

        states = jnp.dot(rows[...], weight[...], preferred_element_type=f32) + bias_row[...]
        for at, out in enumerate(outs):
            out[...] = states[:, at * third : (at + 1) * third].astype(bf16)

    return pl.pallas_call(
        body,
        grid=(TILES,),
        out_shape=[shape_of((features, width), bf16)] + [shape_of((length, third), bf16)] * 3,
        in_specs=[SMEM]
        + [whole(piece.shape) for piece in pieces]
        + [rows_of(attend_in), whole(bias.shape)],
        out_specs=[whole((features, width))]
        + [pl.BlockSpec((length // TILES, third), lambda i: (i, 0))] * 3,
        compiler_params=PARAMS,
        cost_estimate=cost(
            2 * length * features * width, 4 * features * width + 2 * length * (features + width)
        ),
        name="project",
    )(order, *pieces, attend_in, bias)


def attend_forward(pair, prefix, queries, keys, values):
    length = queries.shape[0]
    tile = length // 2

    def body(prefix_ref, query_ref, key_ref, value_ref, out_ref, log_ref, turned):
        turned[...] = value_ref[...].T
        first_half = lax.broadcasted_iota(jnp.int32, (1, PAIR), 1) < HEAD_DIM
        key_rows = key_ref[...]
        row_at = lax.broadcasted_iota(jnp.int32, (length, 1), 0)
        for start in range(0, length, tile):
            columns = slice(start, start + tile)
            places = lax.broadcasted_iota(jnp.int32, (1, tile), 1) + (start + 1)
            limit = jnp.maximum(places, prefix_ref[0])
            query_rows = query_ref[columns, :]
            parts = []
            for head in (0, 1):
                mine = jnp.where(
                    first_half == (head == 0), query_rows, jnp.zeros_like(query_rows)
                )
                scores = lax.dot_general(key_rows, mine, TRANSPOSED, preferred_element_type=f32)
                scores = jnp.where(row_at < limit, scores, masked)
                top = jnp.max(scores, axis=0, keepdims=True)
                raised = jnp.exp2((scores - top) * (SCALE * LOG2E))
                total = jnp.sum(raised, axis=0, keepdims=True)
                mixed = jnp.dot(
                    turned[head * HEAD_DIM : (head + 1) * HEAD_DIM, :],
                    raised.astype(bf16),
                    preferred_element_type=f32,
                )
                parts.append(mixed / total)
                log_ref[head : head + 1, columns] = top * (SCALE * LOG2E) + jnp.log2(total)
            out_ref[columns, :] = jnp.concatenate(parts, 0).T

    block = pl.BlockSpec((length, PAIR), lambda i: (0, pair))
    return pl.pallas_call(
        body,
        grid=(1,),
        out_shape=[shape_of((length, PAIR), f32), shape_of((8, length), f32)],
        in_specs=[SMEM, block, block, block],
        out_specs=[whole((length, PAIR)), whole((8, length))],
        scratch_shapes=[pltpu.VMEM((PAIR, length), bf16)],
        compiler_params=PARAMS,
        cost_estimate=cost(
            16 * length * length * PAIR, 10 * length * PAIR, 2 * length * length
        ),
        name="attend_forward",
    )(prefix, queries, keys, values)


def attend_backward(pair, prefix, queries, keys, values, attended, grads, logs):
    length = queries.shape[0]
    tile = length // 4

    def body(
        prefix_ref,
        query_ref,
        key_ref,
        value_ref,
        attended_ref,
        grad_ref,
        log_ref,
        query_out,
        key_out,
        value_out,
        turned,
        key_total,
        value_total,
    ):
        turned[...] = key_ref[...].T
        first_half = lax.broadcasted_iota(jnp.int32, (1, PAIR), 1) < HEAD_DIM
        key_rows, value_rows = key_ref[...], value_ref[...]
        row_at = lax.broadcasted_iota(jnp.int32, (length, 1), 0)
        for start in range(0, length, tile):
            columns = slice(start, start + tile)
            places = lax.broadcasted_iota(jnp.int32, (1, tile), 1) + (start + 1)
            limit = jnp.maximum(places, prefix_ref[0])
            query_rows, grad_rows = query_ref[columns, :], grad_ref[columns, :]
            crossed = (attended_ref[columns, :] * widen(grad_rows)).T
            parts = []
            key_part = value_part = 0.0
            for head in (0, 1):
                side = first_half == (head == 0)
                span = slice(head * HEAD_DIM, (head + 1) * HEAD_DIM)
                mine = jnp.where(side, query_rows, jnp.zeros_like(query_rows))
                grad = jnp.where(side, grad_rows, jnp.zeros_like(grad_rows))
                level = jnp.sum(crossed[span, :], axis=0, keepdims=True)
                scores = lax.dot_general(key_rows, mine, TRANSPOSED, preferred_element_type=f32)
                raised = jnp.exp2(
                    scores * (SCALE * LOG2E) - log_ref[head : head + 1, columns]
                )
                probs = jnp.where(row_at < limit, raised, 0.0)
                prob_grad = lax.dot_general(
                    value_rows, grad, TRANSPOSED, preferred_element_type=f32
                )
                score_grad = (probs * (prob_grad - level)).astype(bf16)
                value_part += jnp.dot(probs.astype(bf16), grad, preferred_element_type=f32)
                key_part += jnp.dot(score_grad, mine, preferred_element_type=f32)
                parts.append(jnp.dot(turned[span, :], score_grad, preferred_element_type=f32))
            query_out[columns, :] = (jnp.concatenate(parts, 0).T * SCALE).astype(bf16)
            if start == 0:
                key_total[...] = key_part
                value_total[...] = value_part
            else:
                key_total[...] += key_part
                value_total[...] += value_part
        key_out[...] = (key_total[...] * SCALE).astype(bf16)
        value_out[...] = value_total[...].astype(bf16)

    block = pl.BlockSpec((length, PAIR), lambda i: (0, pair))
    return pl.pallas_call(
        body,
        grid=(1,),
        out_shape=[shape_of((length, PAIR), bf16)] * 3,
        in_specs=[SMEM] + [block] * 3 + [whole((length, PAIR)), block, whole((8, length))],
        out_specs=[whole((length, PAIR))] * 3,
        scratch_shapes=[
            pltpu.VMEM((PAIR, length), bf16),
            pltpu.VMEM((length, PAIR), f32),
            pltpu.VMEM((length, PAIR), f32),
        ],
        compiler_params=PARAMS,
        cost_estimate=cost(
            40 * length * length * PAIR, 18 * length * PAIR, 2 * length * length
        ),
        name="attend_backward",
    )(prefix, queries, keys, values, attended, grads, logs)


def mix(order, pieces, attended, head_vectors, widths):
    length = attended[0].shape[0]
    width = PAIR * len(attended)
    count = order.shape[0]
    features = pieces[0].shape[0] // (count // 4) * count

    def body(order_ref, *refs):
        pieces_in, rows, (vectors, weight, second, product, side) = refs[:5], refs[5:-5], refs[-5:]

        @pl.when(pl.program_id(0) == 0)
        def _():
            place_rows(order_ref, pieces_in, (weight, second), count)
            side[...] = side_rows(vectors[2:3, :], vectors[3:4, :], weight[...])

        out, stats = centered_product(
            jnp.concatenate([part[...] for part in rows], 1), vectors[2:3, :], weight[...])
        product[:, :features] = out
        product[:, features:] = stats

    return pl.pallas_call(
        body,
        grid=(TILES,),
        out_shape=[shape_of((features, each), bf16) for each in widths]
        + [shape_of((length, features + LANES), bf16), shape_of((8, features), f32)],
        in_specs=[SMEM]
        + [whole(piece.shape) for piece in pieces]
        + [rows_of(part) for part in attended]
        + [whole(head_vectors.shape)],
        out_specs=[whole((features, each)) for each in widths]
        + [
            pl.BlockSpec((length // TILES, features + LANES), lambda i: (i, 0)),
            whole((8, features)),
        ],
        compiler_params=PARAMS,
        cost_estimate=cost(
            2 * length * features * width, 4 * features * sum(widths) + 6 * length * features
        ),
        name="mix",
    )(order, *pieces, *attended, head_vectors)


def feed_up(product, product_other, side, side_other, inputs, weight, model_vectors, hidden_vectors):
    length, features = inputs.shape
    width = weight.shape[1]

    def body(one, two, side_one, side_two, x, weight_ref, model, hidden, middle, turned, kept, slope):
        _, _, branch = joined_product(one[...], two[...], side_one, side_two, features)
        offset = side_one[1:2, :] + side_two[1:2, :] + model[2:3, :]
        total = widen(x[...]) + (branch + offset)
        middle[...] = total
        normal, _ = normal_of(total)
        feed = (normal * model[3:4, :] + model[4:5, :]).astype(bf16)
        turned[...] = feed.T
        before = jnp.dot(feed, weight_ref[...], preferred_element_type=f32) + hidden[0:1, :]
        share = 0.5 + 0.5 * lax.erf(before * 0.7071067811865476)
        kept[...] = (before * share).astype(bf16)
        slope[...] = (
            share + before * (0.3989422804014327 * jnp.exp(-0.5 * before * before))
        ).astype(bf16)

    return pl.pallas_call(
        body,
        grid=(TILES,),
        out_shape=[
            shape_of((length, features), f32),
            shape_of((features, length), bf16),
            shape_of((length, width), bf16),
            shape_of((length, width), bf16),
        ],
        in_specs=[
            rows_of(product),
            rows_of(product),
            whole(side.shape),
            whole(side.shape),
            rows_of(inputs),
            whole(weight.shape),
            whole(model_vectors.shape),
            whole(hidden_vectors.shape),
        ],
        out_specs=[
            rows_of(inputs),
            pl.BlockSpec((features, length // TILES), lambda i: (0, i)),
            pl.BlockSpec((length // TILES, width), lambda i: (i, 0)),
            pl.BlockSpec((length // TILES, width), lambda i: (i, 0)),
        ],
        compiler_params=PARAMS,
        cost_estimate=cost(
            2 * length * features * width,
            2 * features * width + 12 * length * features + 4 * length * width,
            2 * length * width,
        ),
        name="feed_up",
    )(product, product_other, side, side_other, inputs, weight, model_vectors, hidden_vectors)


def feed_down(order, pieces, kept, hidden_vectors):
    length, width = kept.shape
    count = order.shape[0]
    features = pieces[0].shape[0] // (count // 4) * count

    def body(order_ref, *refs):
        pieces_in, (rows, vectors, weight, product, side) = refs[:5], refs[5:]

        @pl.when(pl.program_id(0) == 0)
        def _():
            place_rows(order_ref, pieces_in, (weight,), count)
            side[...] = side_rows(vectors[1:2, :], vectors[2:3, :], weight[...])

        out, stats = centered_product(widen(rows[...]), vectors[1:2, :], weight[...])
        product[:, :features] = out
        product[:, features:] = stats

    return pl.pallas_call(
        body,
        grid=(TILES,),
        out_shape=[
            shape_of((features, width), bf16),
            shape_of((length, features + LANES), bf16),
            shape_of((8, features), f32),
        ],
        in_specs=[SMEM]
        + [whole(piece.shape) for piece in pieces]
        + [rows_of(kept), whole(hidden_vectors.shape)],
        out_specs=[
            whole((features, width)),
            pl.BlockSpec((length // TILES, features + LANES), lambda i: (i, 0)),
            whole((8, features)),
        ],
        compiler_params=PARAMS,
        cost_estimate=cost(
            2 * length * features * width, 4 * features * width + 2 * length * (features + width)
        ),
        name="feed_down",
    )(order, *pieces, kept, hidden_vectors)


def feed_back(
    core,
    product,
    product_other,
    side,
    side_other,
    middle,
    cotangent,
    kept,
    slope,
    down,
    up,
    model_vectors,
    hidden_vectors,
):
    length, features = middle.shape
    width = kept.shape[1]
    joined = 2 * width
    share = TILES // 2

    def body(
        core_ref, one, two, side_one, side_two, mid, grad, kept_ref, slope_ref, down_ref, up_ref,
        model, hidden, output, norm_out, before_out, product_out, sums,
    ):
        center, inverse, branch = joined_product(one[...], two[...], side_one, side_two, features)
        offset = side_one[1:2, :] + side_two[1:2, :] + model[5:6, :]

        @pl.when(pl.program_id(0) // share == core_ref[0])
        def _():
            output[...] = (mid[...] + (branch + offset)).astype(bf16)

        rows = widen(grad[...])
        straight = side_one[0:1, :] + side_two[0:1, :]
        mean_scaled = jnp.sum(rows * straight, axis=-1, keepdims=True) / joined
        mean_crossed = jnp.sum(rows * branch, axis=-1, keepdims=True) / joined
        mid_grad = jnp.dot(grad[...], down_ref[...], preferred_element_type=f32)
        normal = (widen(kept_ref[...]) - center) * inverse
        norm_out[...] = (normal * hidden[1:2, :] + hidden[2:3, :]).astype(bf16)
        accumulate(sums, 1, mid_grad * normal)
        accumulate(sums, 2, mid_grad)
        hidden_grad = inverse * (
            mid_grad * hidden[1:2, :] - mean_scaled - normal * mean_crossed
        )
        before = (hidden_grad * widen(slope_ref[...])).astype(bf16)
        before_out[...] = before
        accumulate(sums, 0, widen(before))
        product_out[...] = lax.dot_general(
            before, up_ref[...], TRANSPOSED, preferred_element_type=f32
        ).astype(bf16)

    tile = length // TILES

    def at_rows(columns):
        return pl.BlockSpec((tile, columns), lambda i, core: (i, 0))

    def fixed(array):
        return pl.BlockSpec(array.shape, lambda i, core: (0, 0))

    return pl.pallas_call(
        body,
        grid_spec=pltpu.PrefetchScalarGridSpec(
            num_scalar_prefetch=1,
            grid=(TILES,),
            in_specs=[
                at_rows(features + LANES),
                at_rows(features + LANES),
                fixed(side),
                fixed(side),
                at_rows(features),
                at_rows(features),
                at_rows(width),
                at_rows(width),
                fixed(down),
                fixed(up),
                fixed(model_vectors),
                fixed(hidden_vectors),
            ],
            out_specs=[
                pl.BlockSpec(
                    (tile, features), lambda i, core: (jnp.clip(i - core[0] * share, 0, share - 1), 0)
                ),
                at_rows(width),
                at_rows(width),
                at_rows(features),
                pl.BlockSpec((8, width), lambda i, core: (0, 0)),
            ],
        ),
        out_shape=[
            shape_of((length // 2, features), bf16),
            shape_of((length, width), bf16),
            shape_of((length, width), bf16),
            shape_of((length, features), bf16),
            shape_of((8, width), f32),
        ],
        compiler_params=PARAMS,
        cost_estimate=cost(
            4 * length * features * width,
            4 * features * width + 12 * length * features + 8 * length * width,
        ),
        name="feed_back",
    )(
        core,
        product,
        product_other,
        side,
        side_other,
        middle,
        cotangent,
        kept,
        slope,
        down,
        up,
        model_vectors,
        hidden_vectors,
    )


def mix_back(
    passed,
    passed_other,
    product,
    product_other,
    side,
    side_other,
    middle,
    cotangent,
    attended,
    weight,
    model_vectors,
    head_vectors,
):
    length, features = middle.shape
    width = PAIR * len(attended)
    joined = 2 * width

    def body(
        back_one, back_two, one, two, side_one, side_two, mid, grad, *refs
    ):
        attended_refs, (weight_ref, model, head, middle_out, turned, mixed_out, attended_out, sums, head_sums) = refs[:-9], refs[-9:]
        feed_grad = widen(back_one[...]) + widen(back_two[...])
        normal, inverse = normal_of(mid[...])
        accumulate(sums, 1, feed_grad * normal)
        accumulate(sums, 2, feed_grad)
        middle_grad = widen(grad[...]) + normal_back(feed_grad * model[3:4, :], normal, inverse)
        middle_out[...] = middle_grad
        branch_grad = middle_grad.astype(bf16)
        rows = widen(branch_grad)
        accumulate(sums, 0, rows)
        turned[...] = branch_grad.T
        center, inverse_two, branch = joined_product(
            one[...], two[...], side_one, side_two, features
        )
        straight = side_one[0:1, :] + side_two[0:1, :]
        mean_scaled = jnp.sum(rows * straight, axis=-1, keepdims=True) / joined
        mean_crossed = jnp.sum(rows * branch, axis=-1, keepdims=True) / joined
        mixed_grad = jnp.dot(branch_grad, weight_ref[...], preferred_element_type=f32)
        attended_rows = jnp.concatenate([part[...] for part in attended_refs], 1)
        normal_two = (attended_rows - center) * inverse_two
        mixed_out[...] = (normal_two * head[2:3, :] + head[3:4, :]).astype(bf16)
        accumulate(head_sums, 0, mixed_grad * normal_two)
        accumulate(head_sums, 1, mixed_grad)
        attended_out[...] = (
            inverse_two * (mixed_grad * head[2:3, :] - mean_scaled - normal_two * mean_crossed)
        ).astype(bf16)

    tile = length // TILES
    return pl.pallas_call(
        body,
        grid=(TILES,),
        out_shape=[
            shape_of((length, features), f32),
            shape_of((features, length), bf16),
            shape_of((length, width), bf16),
            shape_of((length, width), bf16),
            shape_of((8, features), f32),
            shape_of((8, width), f32),
        ],
        in_specs=[
            rows_of(passed),
            rows_of(passed),
            rows_of(product),
            rows_of(product),
            whole(side.shape),
            whole(side.shape),
            rows_of(middle),
            rows_of(cotangent),
            *[rows_of(part) for part in attended],
            whole(weight.shape),
            whole(model_vectors.shape),
            whole(head_vectors.shape),
        ],
        out_specs=[
            rows_of(middle),
            pl.BlockSpec((features, tile), lambda i: (0, i)),
            pl.BlockSpec((tile, width), lambda i: (i, 0)),
            pl.BlockSpec((tile, width), lambda i: (i, 0)),
            whole((8, features)),
            whole((8, width)),
        ],
        compiler_params=PARAMS,
        cost_estimate=cost(
            2 * length * features * width, 2 * features * width + 24 * length * features
        ),
        name="mix_back",
    )(
        passed,
        passed_other,
        product,
        product_other,
        side,
        side_other,
        middle,
        cotangent,
        *attended,
        weight,
        model_vectors,
        head_vectors,
    )


def project_back(core, groups, weight):
    length = groups[0][0].shape[0]
    parts = [part for group in groups for part in group]
    features, width = weight.shape
    third = width // 3
    tile = length // TILES
    share = TILES // 2
    each = len(groups[0])

    def body(core_ref, *refs):
        weight_ref, send, keep, sums = refs[-4:]
        grads = [
            jnp.concatenate([ref[...] for ref in refs[at * each : (at + 1) * each]], 1)
            for at in range(3)
        ]
        total = lax.dot_general(
            jnp.concatenate(grads, 1), weight_ref[...], TRANSPOSED, preferred_element_type=f32
        )
        accumulate(sums, 0, widen(grads[0]))
        accumulate(sums, 1, widen(grads[2]))

        @pl.when(pl.program_id(0) < share)
        def _():
            send[...] = total.astype(bf16)

        @pl.when(pl.program_id(0) >= share)
        def _():
            keep[...] = total

    moved = pl.BlockSpec((tile, PAIR), lambda i, core: ((i + (1 - core[0]) * share) % TILES, 0))
    return pl.pallas_call(
        body,
        grid_spec=pltpu.PrefetchScalarGridSpec(
            num_scalar_prefetch=1,
            grid=(TILES,),
            in_specs=[moved] * len(parts) + [pl.BlockSpec(weight.shape, lambda i, core: (0, 0))],
            out_specs=[
                pl.BlockSpec((tile, features), lambda i, core: (jnp.minimum(i, share - 1), 0)),
                pl.BlockSpec((tile, features), lambda i, core: (jnp.maximum(i - share, 0), 0)),
                pl.BlockSpec((8, third), lambda i, core: (0, 0)),
            ],
        ),
        out_shape=[
            shape_of((length // 2, features), bf16),
            shape_of((length // 2, features), f32),
            shape_of((8, third), f32),
        ],
        compiler_params=PARAMS,
        cost_estimate=cost(
            2 * length * features * width, 2 * features * width + 6 * length * (features + third)
        ),
        name="project_back",
    )(core, *parts, weight)


def input_back(core, received, kept, middle_grad, tokens, model_vectors):
    rows, features = tokens.shape
    tiles = TILES // 2
    tile = rows // tiles

    def body(core_ref, got, own, mid, x, model, out, sums):
        grad = widen(got[...]) + own[...]
        normal, inverse = normal_of(widen(x[...]))
        accumulate(sums, 0, grad * normal)
        accumulate(sums, 1, grad)
        out[...] = mid[...] + normal_back(grad * model[0:1, :], normal, inverse)

    near = pl.BlockSpec((tile, features), lambda i, core: (i, 0))
    return pl.pallas_call(
        body,
        grid_spec=pltpu.PrefetchScalarGridSpec(
            num_scalar_prefetch=1,
            grid=(tiles,),
            in_specs=[
                near,
                near,
                pl.BlockSpec((tile, features), lambda i, core: (i + core[0] * tiles, 0)),
                near,
                pl.BlockSpec(model_vectors.shape, lambda i, core: (0, 0)),
            ],
            out_specs=[near, pl.BlockSpec((8, features), lambda i, core: (0, 0))],
        ),
        out_shape=[shape_of((rows, features), f32), shape_of((8, features), f32)],
        compiler_params=PARAMS,
        cost_estimate=cost(10 * rows * features, 16 * rows * features),
        name="input_back",
    )(core, received, kept, middle_grad, tokens, model_vectors)


def weight_grad(order, pairs, tile):
    features, tokens = pairs[0][0].shape
    lefts, groups = [], []
    for left, group in pairs:
        if not any(left is known for known in lefts):
            lefts.append(left)
        groups.append(([left is known for known in lefts].index(True), len(group)))
    rights = [right for _, group in pairs for right in group]
    width = sum(right.shape[1] for right in rights)
    count = order.shape[0]
    shard = features // count
    single = len(rights) == 1

    def body(order_ref, *refs):
        left_refs, right_refs = refs[: len(lefts)], refs[len(lefts) : -3]
        keep, send, total = refs[-3:]
        if single:
            total[...] = jnp.dot(left_refs[0][...], right_refs[0][...], preferred_element_type=f32)
        else:
            first = 0
            for step, (at, size) in enumerate(groups):

                @pl.when(pl.program_id(0) == step)
                def _(at=at, first=first, size=size):
                    right = [ref[...] for ref in right_refs[first : first + size]]
                    total[...] = jnp.dot(
                        left_refs[at][...],
                        jnp.concatenate(right, 1) if size > 1 else right[0],
                        preferred_element_type=f32,
                    )

                first += size

        for block in range(count):
            place = pl.multiple_of(order_ref[block] * shard, 16)
            out, at = (keep, block) if block < count // 2 else (send, block - count // 2)
            out[at * shard : (at + 1) * shard, :] = total[pl.ds(place, shard), :].astype(bf16)

    return pl.pallas_call(
        body,
        grid=(width // tile,),
        out_shape=[shape_of((features // 2, width), bf16)] * 2,
        in_specs=[SMEM]
        + [whole(left.shape) for left in lefts]
        + (
            [pl.BlockSpec((tokens, tile), lambda i: (0, i))]
            if single
            else [whole(right.shape) for right in rights]
        ),
        out_specs=[pl.BlockSpec((features // 2, tile), lambda i: (0, i))] * 2,
        scratch_shapes=[pltpu.VMEM((features, tile), f32)],
        compiler_params=PARAMS,
        cost_estimate=cost(
            2 * tokens * features * width,
            2 * (tokens * (features + width) + features * width),
        ),
        name="weight_grad",
    )(order, *lefts, *rights)


def on_device(
    tokens,
    cotangent,
    prefix,
    query_weight,
    key_weight,
    value_weight,
    out_weight,
    up_weight,
    down_weight,
    model_vectors,
    head_vectors,
    hidden_vectors,
):
    ring = Ring(lax.axis_size("dp"))
    order = ring.gather_order()
    near, far = ring.scatter_order(1), ring.scatter_order(2)
    core = lax.axis_index("tensor").astype(jnp.int32)[None]
    half, full = query_weight.shape[1], up_weight.shape[1]
    features = tokens.shape[1]

    bias = jnp.concatenate([head_vectors[0], jnp.zeros_like(head_vectors[0]), head_vectors[1]])
    pair_count = half // PAIR
    tokens_other, cotangent_other = flip_partner(tokens), flip_partner(cotangent)
    first = join(query_weight, key_weight, value_weight)
    first_got = ring.start_gather(first)
    inputs, grads, attend_in, attend_turned, grads_turned, grad_sums = prepare(
        core, tokens, tokens_other, cotangent, cotangent_other, model_vectors
    )
    first_block = ring.end_gather(first, after(first_got, attend_in))
    first_sides = ring.to_sides(first_block)
    second = after(join(out_weight, up_weight), first_block)
    second_got = ring.start_gather(second)
    first_pieces = (first_block, *first_sides, *ring.to_corner(*first_sides))
    first_weight, queries, keys, values = project(
        order, first_pieces, attend_in, bias[None]
    )
    states = (prefix, queries, keys, values)
    second_block = ring.end_gather(second, after(second_got, queries))
    second_sides = ring.to_sides(second_block)
    third = after(down_weight, second_block)
    third_got = ring.start_gather(third)
    attended, logs = [], []
    for pair in range(pair_count):
        out, log = attend_forward(pair, *states)
        attended.append(out)
        logs.append(log)
        states = after(states, out, third_got[0], third_got[-1])
        if pair == pair_count - 2:
            second_sides = after(second_sides, out)
            second_corner = ring.to_corner(*second_sides)
            states = after(states, second_sides, third_got)
    second_pieces = (second_block, *second_sides, *after(second_corner, attended[-1]))
    third_block = ring.end_gather(third, after(third_got, second_corner, attended[-1]))
    third_sides = ring.to_sides(third_block)
    out_full, up_full, mixed, mixed_side = mix(
        order, second_pieces, after(attended, third_block), head_vectors, (half, full)
    )
    mixed, mixed_side, third_sides = after((mixed, mixed_side, third_sides), mixed)
    mixed_other, mixed_side_other = flip_partner(mixed), flip_partner(mixed_side)
    third_corner = ring.to_corner(*third_sides)
    middle, feed_turned, kept, slope = feed_up(
        mixed,
        mixed_other,
        mixed_side,
        mixed_side_other,
        inputs,
        up_full,
        model_vectors,
        hidden_vectors,
    )
    third_pieces = (third_block, *third_sides, *after(third_corner, kept))
    down_full, fed, fed_side = feed_down(order, third_pieces, kept, hidden_vectors)
    fed_other, fed_side_other = flip_partner(fed), flip_partner(fed_side)
    output, feed_mid, before_grad, passed, hidden_sums = feed_back(
        core,
        fed,
        fed_other,
        fed_side,
        fed_side_other,
        middle,
        grads,
        kept,
        slope,
        down_full,
        up_full,
        model_vectors,
        hidden_vectors,
    )
    passed_other = flip_partner(passed)
    down_keep, down_send = weight_grad(far, [(grads_turned, [feed_mid])], full // 2)
    up_keep, up_send = weight_grad(near, [(feed_turned, [before_grad])], full // 2)
    down_got, up_got = ring.flip(down_send, 2), ring.flip(up_send, 1)

    middle_grad, branch_turned, mixed_in, attended_grad, model_sums, head_sums = mix_back(
        passed,
        passed_other,
        mixed,
        mixed_other,
        mixed_side,
        mixed_side_other,
        middle,
        grads,
        attended,
        out_full,
        model_vectors,
        head_vectors,
    )

    def pair_back(pair, grad):
        return attend_backward(pair, *states, attended[pair], grad, logs[pair])

    last_pair = pair_count - 1
    pair_grads = [pair_back(pair, attended_grad) for pair in range(last_pair)]
    down_own, down_away = ring.sum_first(down_keep, after(down_got, pair_grads))
    up_own, up_away = ring.sum_first(up_keep, after(up_got, pair_grads))
    up_second, down_second = ring.flip(up_away, 2), ring.flip(down_away, 1)
    early_grads = after(pair_grads, down_away, up_away)
    early_keep, early_send = weight_grad(
        near,
        [(attend_turned, [pair[at] for pair in early_grads]) for at in range(3)],
        last_pair * PAIR,
    )
    early_got = ring.flip(early_send, 1)
    out_keep, out_send = weight_grad(
        far, [(branch_turned, [after(mixed_in, early_send)])], half
    )
    out_got = ring.flip(out_send, 2)
    pair_grads.append(pair_back(last_pair, after(attended_grad, out_send)))
    query_grad, key_grad, value_grad = ([pair[at] for pair in pair_grads] for at in range(3))
    wide_parts = square_end(
        (up_own, down_own), after((up_second, down_second), pair_grads), ring.lines[0][0]
    )
    wide_got = ring.start_lines(wide_parts)
    send, keep, bias_sums = project_back(
        core, after((query_grad, key_grad, value_grad), wide_parts), first_weight
    )
    received = flip_partner(send)
    late_keep, late_send = weight_grad(
        near, [(attend_turned, after(list(pair_grads[last_pair]), send))], 3 * PAIR
    )
    late_got = ring.flip(late_send, 1)
    early_got, out_got = after((early_got, out_got), late_send, wide_got[0], wide_got[-1])
    early_own, early_away = ring.sum_first(early_keep, early_got)
    out_own, out_away = ring.sum_first(out_keep, out_got)
    early_second, out_second = ring.flip(early_away, 2), ring.flip(out_away, 1)
    input_grad, first_sums = input_back(
        core, received, after(keep, early_away, out_away), middle_grad, tokens, model_vectors
    )
    late_own, late_away = ring.sum_first(late_keep, after(late_got, input_grad))
    late_second = ring.flip(late_away, 2)
    packed = pack(
        first_sums, flip_partner(first_sums), model_sums, grad_sums, bias_sums, head_sums, hidden_sums
    )
    for factor, stride in [*ring.lines[1:][::-1], ring.lines[0]]:
        packed = add_up([packed, *ring.around(packed, factor, stride)])
    model_sum, head_sum, hidden_sum = unpack(
        [packed, *ring.around_square(packed)], ((6, features), (4, half), (3, full))
    )
    narrow_parts = square_end(
        (early_own, out_own, late_own),
        after((early_second, out_second, late_second), input_grad),
        ring.lines[0][0],
    )
    narrow_got = ring.start_lines(narrow_parts)
    wide_terms = ring.last_terms(wide_parts, wide_got)
    narrow_terms = ring.last_terms(narrow_parts, narrow_got)
    up_grad, down_grad = finish([wide_terms], [[(0, 0, full)], [(0, full, full)]])
    early = last_pair * PAIR
    query_weight_grad, key_weight_grad, value_weight_grad, out_grad = finish(
        [narrow_terms],
        [
            [(0, at * early, early), (0, 3 * early + half + at * PAIR, PAIR)]
            for at in range(3)
        ]
        + [[(0, 3 * early, half)]],
    )
    return (
        output,
        input_grad,
        query_weight_grad,
        key_weight_grad,
        value_weight_grad,
        out_grad,
        up_grad,
        down_grad,
        model_sum,
        head_sum,
        hidden_sum,
    )


def solution(mesh):
    return jax.shard_map(
        on_device,
        mesh=mesh,
        in_specs=(
            P(("dp", "tensor"), None),
            P(("dp", "tensor"), None),
            P("dp"),
            P("dp", "tensor"),
            P("dp", "tensor"),
            P("dp", "tensor"),
            P("dp", "tensor"),
            P("dp", "tensor"),
            P("dp", "tensor"),
            P(),
            P(None, "tensor"),
            P(None, "tensor"),
        ),
        out_specs=(
            P(("dp", "tensor"), None),
            P(("dp", "tensor"), None),
            P("dp", "tensor"),
            P("dp", "tensor"),
            P("dp", "tensor"),
            P("dp", "tensor"),
            P("dp", "tensor"),
            P("dp", "tensor"),
            P(),
            P(None, "tensor"),
            P(None, "tensor"),
        ),
        check_vma=False,
    )
```
